32 devices in a mesh: items: 16 (over z, x, core), heads: 2 (over y).
Axes of the slice: x: 2, y: 2, z: 4, core: 2. Of those that a mesh axis runs over, the one named last changes fastest.
Arguments:
- tokens: bfloat16 [32, 512, 768], P(('items', 'heads')), may hold values from -6 to 6
- earlier: bfloat16 [32, 512, 768], P(('items', 'heads')), may hold values from -6 to 6
- coeffs: float32 [32, 256, 768], P(('items', 'heads')), may hold values from -6 to 6
- present: int32 [32], P(('items', 'heads')), may hold values 0 or 1
- sample_at: int32 [32, 512], P(('items', 'heads')), may hold values from 0 to 1023
- w_qkv: float32 [3, 768, 768], P(None, 'items', 'heads'), may hold values from -0.21875 to 0.21875
- w_out: float32 [768, 768], P('heads', 'items'), may hold values from -1.25 to 1.25
- w_up: float32 [768, 3072], P('items', 'heads'), may hold values from -0.21875 to 0.21875
- w_down: float32 [3072, 768], P('heads', 'items'), may hold values from -0.109375 to 0.109375
- gain_attn: float32 [768], P('items'), may hold values from 0.25 to 1.75
- gain_mlp: float32 [768], P('items'), may hold values from 0.25 to 1.75
- w_mean: float32 [12, 256], P('heads', 'items'), may hold values from -0.375 to 0.375
- w_var: float32 [12, 256], P('heads', 'items'), may hold values from -0.375 to 0.375
- cotangent: bfloat16 [32, 512, 768], P(('items', 'heads')), may hold values from -6 to 6
Outputs:
- output: bfloat16 [32, 512, 768], P(('items', 'heads'))
- grad_tokens: float32 [32, 512, 768], P(('items', 'heads'))
- grad_coeffs: float32 [32, 256, 768], P(('items', 'heads'))
- grad_w_qkv: float32 [3, 768, 768], P(None, 'items', 'heads')
- grad_w_out: float32 [768, 768], P('heads', 'items')
- grad_w_up: float32 [768, 3072], P('items', 'heads')
- grad_w_down: float32 [3072, 768], P('heads', 'items')
- grad_gain_attn: float32 [768], P(('items', 'heads'))
- grad_gain_mlp: float32 [768], P(('items', 'heads'))
- grad_w_mean: float32 [12, 256], P('heads', 'items')
- grad_w_var: float32 [12, 256], P('heads', 'items')
The draws below stay inside these ranges and needn't reach their ends.
Inputs may be any that keep to these rules, and one draw needn't show every extreme that they name: `sample_at`: grid points, out of 1024, at which an item's old memory is sampled. `present`: 1 where the item carries old memory.
All inputs are finite; a program needn't handle non-finite values. No bound on the sum of `present` on one device may be relied on, other than what follows from the above.
Results may differ from the reference program's by a relative error of at most 0.017.
The reference program's roundings to bfloat16 on the way count: a program that leaves them out, or rounds other values in their place, can miss the bound.
Values may be sent and summed in bfloat16 or wider, within the bound.
No kernel may reach another device: no remote copies, remote signals or barrier semaphores. Data moves between devices by JAX's collectives and lax.ppermute only.
A program may use at most 128 MiB of HBM per device.

```python
import math
import jax
import jax.numpy as jnp
from jax import lax

D = 768
HEADS = 12
HD = 64
FF = 3072
NB = 256
SEG = 512
GRID = 1024
ITEMS = 32


def with_ends(array, stream_key, smallest, top_value):
    spot = [jax.random.randint(jax.random.fold_in(stream_key, axis), (), 0, length) for axis, length in enumerate(array.shape)]
    main_axis = array.shape.index(max(array.shape))
    beside = spot[:main_axis] + [(spot[main_axis] + 1) % array.shape[main_axis]] + spot[main_axis + 1:]
    return array.at[tuple(spot)].set(smallest).at[tuple(beside)].set(top_value)


def shard_levels(key, dims, split, low, largest):
    factor_of = 1.0
    for dim, shards_of in split:
        draws = jax.random.uniform(jax.random.fold_in(jax.random.fold_in(key, 6), dim), (shards_of,), jnp.float32, low / len(split), largest / len(split))
        factor_of = factor_of * jnp.repeat(jnp.exp(draws), dims[dim] // shards_of).reshape((-1,) + (1,) * (len(dims) - 1 - dim))
    return factor_of


def normal_values(key, extent, scale, bound, pieces=(), held_as=jnp.bfloat16):
    factor_of = shard_levels(key, extent, pieces, -0.22, 0.18) if pieces else 1.0
    values = jax.random.normal(key, extent, jnp.float32) * scale * factor_of
    return jnp.minimum(jnp.maximum(values, -bound), bound).astype(held_as)


def setup_inputs(seed: int = 0) -> dict:
    key_of = jax.random.split(jax.random.key(seed), 15)
    return {
        "tokens": normal_values(key_of[0], (ITEMS, SEG, D), 1.0, 6.0, ((0, 32),)),
        "earlier": normal_values(key_of[1], (ITEMS, SEG, D), 1.0, 6.0, ((0, 32),)),
        "coeffs": normal_values(key_of[2], (ITEMS, NB, D), 1.0, 6.0, ((0, 32),), jnp.float32),
        "present": with_ends((jax.random.randint(key_of[3], (ITEMS,), 0, 2) < 1).astype(jnp.int32), jax.random.fold_in(key_of[3], 1), 0, 1),
        "sample_at": with_ends(jax.random.randint(key_of[4], (ITEMS, SEG), 0, GRID), jax.random.fold_in(key_of[4], 1), 0, GRID - 1).astype(jnp.int32),
        "w_qkv": normal_values(key_of[5], (3, D, D), D ** -0.5, 0.21875, ((1, 16), (2, 2)), jnp.float32),
        "w_out": normal_values(key_of[6], (D, D), (D // 32) ** -0.5, 1.25, ((0, 2), (1, 16)), jnp.float32),
        "w_up": normal_values(key_of[7], (D, FF), D ** -0.5, 0.21875, ((0, 16), (1, 2)), jnp.float32),
        "w_down": normal_values(key_of[8], (FF, D), FF ** -0.5, 0.109375, ((0, 2), (1, 16)), jnp.float32),
        "gain_attn": jnp.clip(1.0 + 0.15 * jax.random.normal(key_of[9], (D,), jnp.float32), 0.25, 1.75),
        "gain_mlp": jnp.clip(1.0 + 0.15 * jax.random.normal(key_of[10], (D,), jnp.float32), 0.25, 1.75),
        "w_mean": normal_values(key_of[11], (HEADS, NB), NB ** -0.5, 0.375, ((0, 2), (1, 16)), jnp.float32),
        "w_var": normal_values(key_of[12], (HEADS, NB), NB ** -0.5, 0.375, ((0, 2), (1, 16)), jnp.float32),
        "cotangent": normal_values(key_of[13], (ITEMS, SEG, D), 1.0, 6.0, ((0, 32),)),
    }


EPSILON = 1e-05
VAR_SCALE = 0.01
RIDGE = 1.0
HIGHEST = lax.Precision.HIGHEST

@jax.custom_vjp
def low(v):
    return lax.optimization_barrier(v.astype(jnp.bfloat16)).astype(jnp.float32)

@jax.custom_vjp
def low_back(v):
    return v

def low_keep(v):
    return (low(v), None)

def low_pass(kept, grad):
    return (grad,)

def back_keep(v):
    return (v, None)

def back_low(kept, grad):
    return (low(grad),)
low.defvjp(low_keep, low_pass)
low_back.defvjp(back_keep, back_low)

def layer_norm(values, gain_vec):
    row_mean = lax.optimization_barrier(jnp.mean(values, axis=-1, keepdims=True))
    centred = values - row_mean
    spread = lax.optimization_barrier(jnp.mean(centred * centred, axis=-1, keepdims=True))
    return centred * lax.rsqrt(spread + EPSILON) * gain_vec

def basis_at(points, basis_count):
    centers = (jnp.arange(basis_count, dtype=jnp.float32) + 0.5) / basis_count
    offset = points[..., None] - centers
    return jnp.exp(-offset * offset * (0.5 * basis_count * basis_count))

def ridge_table(basis_count, samples):
    points = (jnp.arange(samples, dtype=jnp.float32) + 0.5) / samples
    design = basis_at(points, basis_count)
    gram_matrix = jnp.dot(design.T, design, precision=HIGHEST) + RIDGE * jnp.eye(basis_count, dtype=jnp.float32)
    factor = jnp.linalg.cholesky(gram_matrix)
    return jax.scipy.linalg.cho_solve((factor, True), design.T)

def density(raw_scores, w_mean, w_var):
    basis_count = w_mean.shape[-1]
    scaled = raw_scores * 0.125
    centers = (jnp.arange(basis_count, dtype=jnp.float32) + 0.5) / basis_count
    middle = jax.nn.sigmoid(jnp.dot(scaled, w_mean, precision=HIGHEST))
    variance = VAR_SCALE * jax.nn.softplus(jnp.dot(scaled, w_var, precision=HIGHEST)) + 1.0 / (basis_count * basis_count)
    offset = middle[:, None] - centers
    return jnp.exp(-offset * offset / (2.0 * variance[:, None])) * lax.rsqrt(2.0 * math.pi * variance)[:, None] / basis_count

def one_item(inputs_row, weights):
    tokens, earlier, coeffs, present, sample_at = inputs_row
    w_qkv, w_out, w_up, w_down, gain_attn, gain_mlp, w_mean, w_var, ridge = weights
    length = tokens.shape[0]
    basis_count = coeffs.shape[0]
    normed = low(layer_norm(tokens, gain_attn))
    normed_past = low(layer_norm(earlier, gain_attn))
    old_basis = low(basis_at((sample_at.astype(jnp.float32) + 0.5) / GRID, basis_count))
    samples = low(low_back(present.astype(jnp.float32) * jnp.dot(old_basis, low(coeffs), precision=HIGHEST)))
    memory = low(low_back(jnp.dot(ridge, jnp.concatenate([samples, normed_past], axis=0), precision=HIGHEST)))

    def project(source, matrix):
        return low(low_back(jnp.dot(source, matrix, precision=HIGHEST))).reshape(source.shape[0], HEADS, HD)
    queries = project(normed, w_qkv[0])
    keys_all = jnp.concatenate([project(normed_past, w_qkv[1]), project(normed, w_qkv[1])], axis=0)
    values_all = jnp.concatenate([project(normed_past, w_qkv[2]), project(normed, w_qkv[2])], axis=0)
    mem_keys = project(memory, w_qkv[1])
    mem_values = project(memory, w_qkv[2])
    raw_scores = jnp.einsum('shd,thd->hst', queries, keys_all, precision=HIGHEST)
    allowed = jnp.arange(2 * length)[None, :] <= length + jnp.arange(length)[:, None]
    scores = jnp.where(allowed[None], low_back(raw_scores) * 0.125, -1e+30)
    attn_probs = low(jax.nn.softmax(scores, axis=-1))
    near_part = jnp.einsum('hst,thd->shd', attn_probs, values_all, precision=HIGHEST)
    mem_raw = low_back(jnp.einsum('shd,jhd->hsj', queries, mem_keys, precision=HIGHEST))
    weights_mem = low(jax.vmap(density)(mem_raw, w_mean, w_var))
    recall = jnp.einsum('hsj,jhd->shd', weights_mem, mem_values, precision=HIGHEST)
    context = low(low_back((near_part + recall).reshape(length, HEADS * HD)))
    hidden = tokens + low_back(jnp.dot(context, w_out, precision=HIGHEST))
    normed_mlp = low(layer_norm(hidden, gain_mlp))
    pre_act = low_back(jnp.dot(normed_mlp, w_up, precision=HIGHEST))
    activation = low(jax.nn.gelu(pre_act, approximate=True))
    return hidden + jnp.dot(activation, w_down, precision=HIGHEST)

def reference(tokens, earlier, coeffs, present, sample_at, w_qkv, w_out, w_up, w_down, gain_attn, gain_mlp, w_mean, w_var, cotangent):
    float_tokens = tokens.astype(jnp.float32)
    float_earlier = earlier.astype(jnp.float32)

    def forward(token_in, coeff_in, qkv_in, out_in, up_in, down_in, gain_first, gain_second, mean_in, var_in):
        ridge = low(ridge_table(NB, 2 * SEG))
        weights = (low(qkv_in), low(out_in), low(up_in), low(down_in), low(gain_first), low(gain_second), low(mean_in), low(var_in), ridge)

        def run_item(inputs_row):
            return one_item(inputs_row, weights)
        return lax.map(jax.checkpoint(run_item), (token_in, float_earlier, coeff_in, present, sample_at))
    output, pull_back = jax.vjp(forward, float_tokens, coeffs, w_qkv, w_out, w_up, w_down, gain_attn, gain_mlp, w_mean, w_var)
    gradients = pull_back(cotangent.astype(jnp.float32))
    return (output.astype(jnp.bfloat16), gradients[0], gradients[1], gradients[2], gradients[3], gradients[4], gradients[5], gradients[6], gradients[7], gradients[8], gradients[9])
```

```python
import math

import jax
import jax.numpy as jnp
import numpy as np
from jax import lax
from jax.experimental import pallas as pl
from jax.experimental.pallas import tpu as pltpu
from jax.sharding import PartitionSpec as P

HD = 64
GRID = 1024
EPSILON = 1e-05
VAR_SCALE = 0.01
RIDGE = 1.0
LANES = 128
ROWS = 256
NEG = -1e30
bf16 = jnp.bfloat16
f32 = jnp.float32


def dot(a, b, ca, cb):
    return lax.dot_general(a, b, (((ca,), (cb,)), ((), ())), preferred_element_type=f32)


def layer_norm(values, gain_vec):
    row_mean = jnp.mean(values, axis=-1, keepdims=True)
    centred = values - row_mean
    spread = jnp.mean(centred * centred, axis=-1, keepdims=True)
    return centred * lax.rsqrt(spread + EPSILON) * gain_vec


def basis_at(points, basis_count):
    centers = (jnp.arange(basis_count, dtype=f32) + 0.5) / basis_count
    offset = points[..., None] - centers
    return jnp.exp(-offset * offset * (0.5 * basis_count * basis_count))


def ridge_table(basis_count, samples):
    points = (np.arange(samples) + 0.5) / samples
    centers = (np.arange(basis_count) + 0.5) / basis_count
    design = np.exp(-((points[:, None] - centers) ** 2) * (0.5 * basis_count * basis_count))
    gram = design.T @ design + RIDGE * np.eye(basis_count)
    factor = np.linalg.cholesky(gram)
    table = np.linalg.solve(factor.T, np.linalg.solve(factor, design.T))
    return jnp.asarray(table.astype(np.float32)).astype(bf16)


def gelu_tanh(values):
    return jax.nn.gelu(values, approximate=True)


def near_scores(q_rows, keys, block):
    reach = keys.shape[0] // 2 + (block + 1) * ROWS
    scores = dot(q_rows, keys[:reach], 1, 1)
    row = lax.broadcasted_iota(jnp.int32, (ROWS, ROWS), 0)
    col = lax.broadcasted_iota(jnp.int32, (ROWS, ROWS), 1)
    edge = jnp.where(col <= row, scores[:, reach - ROWS :], NEG)
    return jnp.concatenate([scores[:, : reach - ROWS], edge], axis=1), reach


def density_parts(scaled, w_mean, w_var):
    basis_count = scaled.shape[1]
    index = lax.broadcasted_iota(jnp.int32, (1, basis_count), 1).astype(f32)
    centers = (index + 0.5) / basis_count
    middle = jax.nn.sigmoid(jnp.sum(scaled * w_mean, axis=1, keepdims=True))
    var_raw = jnp.sum(scaled * w_var, axis=1, keepdims=True)
    softplus = jnp.maximum(var_raw, 0.0) + jnp.log1p(jnp.exp(-jnp.abs(var_raw)))
    variance = VAR_SCALE * softplus + 1.0 / (basis_count * basis_count)
    offset = middle - centers
    inv_var = 1.0 / variance
    square = offset * offset * inv_var
    scale = lax.rsqrt(2.0 * math.pi * variance) / basis_count
    weights = jnp.exp(-0.5 * square) * scale
    return weights, middle, var_raw, inv_var, offset, square


def attn_fwd_kernel(q_ref, k_ref, v_ref, mk_ref, mv_ref, wm_ref, wv_ref, ctx_ref, lse_ref):
    half = lax.broadcasted_iota(jnp.int32, (1, LANES), 1) < HD
    length = q_ref.shape[0]
    keys, values = k_ref[...], v_ref[...]
    mem_keys, mem_values = mk_ref[...], mv_ref[...]
    for block in range(length // ROWS):
        rows = slice(block * ROWS, (block + 1) * ROWS)
        q_rows = q_ref[rows, :] * jnp.asarray(0.125, bf16)
        outs, sums = [], []
        for head in range(2):
            mine = half if head == 0 else jnp.logical_not(half)
            q_head = jnp.where(mine, q_rows, jnp.zeros_like(q_rows))
            scores, reach = near_scores(q_head, keys, block)
            top = jnp.max(scores, axis=1, keepdims=True)
            raw = jnp.exp(scores - top)
            total = jnp.sum(raw, axis=1, keepdims=True)
            probs = (raw * (1.0 / total)).astype(bf16)
            near = dot(probs, values[:reach], 1, 0)
            scaled = dot(q_head, mem_keys, 1, 1)
            weights = density_parts(
                scaled, wm_ref[0, head : head + 1, :], wv_ref[0, head : head + 1, :]
            )[0]
            outs.append(near + dot(weights.astype(bf16), mem_values, 1, 0))
            sums.append(top + jnp.log(total))
        ctx_ref[rows, :] = jnp.where(half, outs[0], outs[1]).astype(bf16)
        lse_ref[rows, :] = jnp.where(half, sums[0], sums[1])


def attn_bwd_kernel(
    q_ref, k_ref, v_ref, mk_ref, mv_ref, wm_ref, wv_ref, lse_ref, do_ref,
    dq_ref, dk_ref, dv_ref, gm_ref, gv_ref, acck_ref, accv_ref,
):
    half = lax.broadcasted_iota(jnp.int32, (1, LANES), 1) < HD
    length = q_ref.shape[0]
    near_rows = k_ref.shape[0]
    keys, values = k_ref[...], v_ref[...]
    mem_keys, mem_values = mk_ref[...], mv_ref[...]
    for block in reversed(range(length // ROWS)):
        rows = slice(block * ROWS, (block + 1) * ROWS)
        q_full, do_full = q_ref[rows, :], do_ref[rows, :]
        q_rows = q_full * jnp.asarray(0.125, bf16)
        q_turn, do_turn = q_full.T, do_full.T
        outs = []
        for head in range(2):
            part = slice(head * HD, (head + 1) * HD)
            mine = half if head == 0 else jnp.logical_not(half)
            q_head = jnp.where(mine, q_rows, jnp.zeros_like(q_rows))
            do_head = jnp.where(mine, do_full, jnp.zeros_like(do_full))
            scores, reach = near_scores(q_head, keys, block)
            probs = jnp.exp(scores - lse_ref[rows, head * HD : head * HD + 1])
            grad_probs = dot(do_head, values[:reach], 1, 1)
            inner = jnp.sum(probs * grad_probs, axis=1, keepdims=True)
            grad_raw = (0.125 * probs * (grad_probs - inner)).astype(bf16)
            probs_low = probs.astype(bf16)
            dk_part = dot(q_turn[part], grad_raw, 1, 0)
            dv_part = dot(do_turn[part], probs_low, 1, 0)
            out = dot(grad_raw, keys[:reach], 1, 0)
            w_mean, w_var = wm_ref[0, head : head + 1, :], wv_ref[0, head : head + 1, :]
            scaled = dot(q_head, mem_keys, 1, 1)
            weights, middle, var_raw, inv_var, offset, square = density_parts(scaled, w_mean, w_var)
            grad_w = dot(do_head, mem_values, 1, 1) * weights
            d_mid = -jnp.sum(grad_w * offset, axis=1, keepdims=True) * inv_var
            d_var = jnp.sum(grad_w * (square - 1.0), axis=1, keepdims=True) * (0.5 * inv_var)
            d_mid = d_mid * middle * (1.0 - middle)
            d_var = d_var * VAR_SCALE * jax.nn.sigmoid(var_raw)
            gm_part = jnp.sum(scaled * d_mid, axis=0, keepdims=True)
            gv_part = jnp.sum(scaled * d_var, axis=0, keepdims=True)
            grad_mem = (0.125 * (d_mid * w_mean + d_var * w_var)).astype(bf16)
            outs.append(out + dot(grad_mem, mem_keys, 1, 0))
            dmk_part = dot(q_turn[part], grad_mem, 1, 0)
            dmv_part = dot(do_turn[part], weights.astype(bf16), 1, 0)
            if block == length // ROWS - 1:
                acck_ref[part, :near_rows] = dk_part
                accv_ref[part, :near_rows] = dv_part
                acck_ref[part, near_rows:] = dmk_part
                accv_ref[part, near_rows:] = dmv_part
                gm_ref[0, head : head + 1, :] = gm_part
                gv_ref[0, head : head + 1, :] = gv_part
            else:
                acck_ref[part, :reach] += dk_part
                accv_ref[part, :reach] += dv_part
                acck_ref[part, near_rows:] += dmk_part
                accv_ref[part, near_rows:] += dmv_part
                gm_ref[0, head : head + 1, :] += gm_part
                gv_ref[0, head : head + 1, :] += gv_part
        dq_ref[rows, :] = jnp.where(half, outs[0], outs[1]).astype(bf16)
    dk_ref[...] = acck_ref[...].T.astype(bf16)
    dv_ref[...] = accv_ref[...].T.astype(bf16)


def attn_specs(length, basis_count, pairs, place):
    near_rows = 2 * length
    spec = pl.BlockSpec
    return [
        spec((length, LANES), lambda p: (0, place(p))),
        spec((near_rows, LANES), lambda p: (0, place(p))),
        spec((near_rows, LANES), lambda p: (0, pairs + place(p))),
        spec((basis_count, LANES), lambda p: (near_rows // basis_count, place(p))),
        spec((basis_count, LANES), lambda p: (near_rows // basis_count, pairs + place(p))),
        spec((1, 2, basis_count), lambda p: (place(p), 0, 0)),
        spec((1, 2, basis_count), lambda p: (place(p), 0, 0)),
    ]


def attn_forward(queries, kv, w_mean, w_var):
    length, width = queries.shape
    basis_count = w_mean.shape[-1]
    pairs = width // LANES
    return pl.pallas_call(
        attn_fwd_kernel,
        grid=(pairs,),
        in_specs=attn_specs(length, basis_count, pairs, lambda p: p),
        out_specs=[
            pl.BlockSpec((length, LANES), lambda p: (0, p)),
            pl.BlockSpec((length, LANES), lambda p: (0, p)),
        ],
        out_shape=[
            jax.ShapeDtypeStruct((length, width), bf16),
            jax.ShapeDtypeStruct((length, width), f32),
        ],
        compiler_params=pltpu.CompilerParams(vmem_limit_bytes=48 << 20),
        cost_estimate=pl.CostEstimate(
            flops=8 * length * length * width, bytes_accessed=8 << 20, transcendentals=0
        ),
        name="attn_forward",
    )(queries, kv, kv, kv, kv, w_mean, w_var)


def attn_backward(queries, kv, w_mean, w_var, lse, grad_ctx, group, groups):
    length, width = queries.shape
    basis_count = w_mean.shape[-1]
    pairs = width // LANES
    count = pairs // groups
    if groups == 1:
        place = lambda p: p
    else:
        place = lambda p: p * groups + group
    all_rows = kv.shape[0]
    out_width = count * LANES
    return pl.pallas_call(
        attn_bwd_kernel,
        grid=(count,),
        in_specs=attn_specs(length, basis_count, pairs, place)
        + [
            pl.BlockSpec((length, LANES), lambda p: (0, place(p))),
            pl.BlockSpec((length, LANES), lambda p: (0, place(p))),
        ],
        out_specs=[
            pl.BlockSpec((length, LANES), lambda p: (0, p)),
            pl.BlockSpec((all_rows, LANES), lambda p: (0, p)),
            pl.BlockSpec((all_rows, LANES), lambda p: (0, p)),
            pl.BlockSpec((1, 2, basis_count), lambda p: (p, 0, 0)),
            pl.BlockSpec((1, 2, basis_count), lambda p: (p, 0, 0)),
        ],
        out_shape=[
            jax.ShapeDtypeStruct((length, out_width), bf16),
            jax.ShapeDtypeStruct((all_rows, out_width), bf16),
            jax.ShapeDtypeStruct((all_rows, out_width), bf16),
            jax.ShapeDtypeStruct((count, 2, basis_count), f32),
            jax.ShapeDtypeStruct((count, 2, basis_count), f32),
        ],
        scratch_shapes=[
            pltpu.VMEM((LANES, all_rows), f32),
            pltpu.VMEM((LANES, all_rows), f32),
        ],
        compiler_params=pltpu.CompilerParams(vmem_limit_bytes=48 << 20),
        cost_estimate=pl.CostEstimate(
            flops=20 * length * length * out_width, bytes_accessed=8 << 20, transcendentals=0
        ),
        name="attn_backward",
    )(queries, kv, kv, kv, kv, w_mean, w_var, lse, grad_ctx)


class Links:
    def __init__(self, sizes):
        self.count = sizes["items"]
        self.bits = self.count.bit_length() - 1
        self.index = lax.axis_index("items")
        self.side = lax.axis_index("heads")

    def swap(self, value, stage):
        if stage == "h":
            return lax.ppermute(value, "heads", [(0, 1), (1, 0)])
        mask = 1 << stage
        return lax.ppermute(value, "items", [(i, i ^ mask) for i in range(self.count)])

    def bit(self, stage):
        return self.side if stage == "h" else (self.index >> stage) & 1

    def gather(self, value, lead, stages):
        have = []
        for stage in stages:
            other = self.swap(value, stage)
            mine_first = self.bit(stage) == 0
            first = jnp.where(mine_first, value, other)
            second = jnp.where(mine_first, other, value)
            if stage == "h":
                value = jnp.concatenate([first, second], axis=-1)
            else:
                place = sum(1 for b in have if b > stage)
                value = jnp.stack([first, second], axis=lead + place)
                have.append(stage)
        return value

    def reduce(self, value, lead, stages, wire):
        shape = value.shape
        value = value.reshape(shape[:lead] + (2,) * self.bits + shape[lead + 1 :])
        left = list(range(self.bits))[::-1]
        for stage in stages:
            bit = self.bit(stage)
            if stage == "h":
                width = value.shape[-1] // 2
                take = lambda b: lax.dynamic_slice_in_dim(value, b * width, width, axis=value.ndim - 1)
            else:
                axis = lead + left.index(stage)
                left.remove(stage)
                take = lambda b: lax.dynamic_index_in_dim(value, b, axis, keepdims=False)
            send = take(1 - bit).astype(wire)
            value = take(bit) + self.swap(send, stage).astype(f32)
        return value


def shards(
    tokens, earlier, coeffs, present, sample_at, w_qkv, w_out, w_up, w_down,
    gain_attn, gain_mlp, w_mean, w_var, cotangent, sizes, groups,
):
    links = Links(sizes)
    high = list(range(2, links.bits))
    count = links.count
    tokens, earlier, coeffs, cotangent = tokens[0], earlier[0], coeffs[0], cotangent[0]
    length, width = tokens.shape
    basis_count = coeffs.shape[0]
    rows, side = w_qkv.shape[1], w_qkv.shape[2]
    ff_side = w_up.shape[1]
    local_heads, mem_part = w_mean.shape

    small = jnp.concatenate(
        [gain_attn, gain_mlp, w_mean.reshape(-1), w_var.reshape(-1)]
    ).astype(bf16)
    small_size = small.shape[0]
    small = jnp.pad(small, (0, -small_size % LANES)).reshape(1, -1)
    small_h = links.swap(small, "h")
    first = jnp.where(links.side == 0, small, small_h)
    second = jnp.where(links.side == 0, small_h, small)
    small = links.gather(jnp.concatenate([first, second], axis=0), 0, high + [1, 0])
    small = small.reshape(count, 2, -1).astype(f32)
    gain_a = small[:, 0, :rows].reshape(-1)
    gain_m = small[:, 0, rows : 2 * rows].reshape(-1)

    def head_map(start):
        part = small[:, :, start : start + local_heads * mem_part]
        part = part.reshape(count, 2, local_heads, mem_part).transpose(1, 2, 0, 3)
        return part.reshape(local_heads, 2, basis_count)

    mean_full = head_map(2 * rows)
    var_full = head_map(2 * rows + local_heads * mem_part)

    qkv_full = links.gather(w_qkv.astype(bf16), 1, high + [1, "h", 0])
    qkv_full = qkv_full.reshape(3, width, width)
    rest = jnp.concatenate([w_out.T, w_up, w_down.T], axis=1).astype(bf16)
    rest = lax.all_gather(rest, ("items", "heads"), axis=0, tiled=False)
    rest = rest.reshape(count, 2, rows, -1)

    def whole(start, size):
        return rest[..., start : start + size].transpose(0, 2, 1, 3).reshape(width, 2 * size)

    out_turn = whole(0, side)
    up_full = whole(side, ff_side)
    down_turn = whole(side + ff_side, ff_side)

    ridge = ridge_table(basis_count, 2 * length)
    tokens32, earlier32 = tokens.astype(f32), earlier.astype(f32)
    normed = layer_norm(tokens32, gain_a).astype(bf16)
    past = layer_norm(earlier32, gain_a).astype(bf16)
    old_basis = basis_at((sample_at[0].astype(f32) + 0.5) / GRID, basis_count).astype(bf16)
    here = present[0].astype(f32)
    samples = (here * dot(old_basis, coeffs.astype(bf16), 1, 0)).astype(bf16)
    memory = dot(ridge, jnp.concatenate([samples, past], axis=0), 1, 0).astype(bf16)
    sources = jnp.concatenate([past, normed, memory], axis=0)
    queries = dot(normed, qkv_full[0], 1, 0).astype(bf16)
    kv = jnp.concatenate(
        [dot(sources, qkv_full[1], 1, 0), dot(sources, qkv_full[2], 1, 0)], axis=1
    ).astype(bf16)
    context, lse = attn_forward(queries, kv, mean_full, var_full)
    hidden = tokens32 + dot(context, out_turn, 1, 1)
    normed_mlp, mlp_pull = jax.vjp(layer_norm, hidden, gain_m)
    normed_mlp = normed_mlp.astype(bf16)
    pre_act = dot(normed_mlp, up_full, 1, 0)
    activation = gelu_tanh(pre_act).astype(bf16)
    output = (hidden + dot(activation, down_turn, 1, 1)).astype(bf16)

    grad_act = dot(cotangent, down_turn, 1, 0)
    _, gelu_pull = jax.vjp(gelu_tanh, pre_act)
    grad_pre = gelu_pull(grad_act)[0].astype(bf16)
    g_down = dot(cotangent, activation, 0, 0).reshape(count, rows, -1)
    g_up = dot(normed_mlp, grad_pre, 0, 0).reshape(count, rows, -1)
    down = high[::-1]
    r_down = links.reduce(g_down, 0, [0, "h", 1] + down, bf16)
    r_up = links.reduce(g_up, 0, [0, 1, "h"] + down, bf16)
    grad_hidden_norm, gain_m_grad = mlp_pull(dot(grad_pre, up_full, 1, 1))
    grad_hidden = cotangent.astype(f32) + grad_hidden_norm
    grad_branch = grad_hidden.astype(bf16)
    g_out = dot(grad_branch, context, 0, 0).reshape(count, rows, -1)
    r_out = links.reduce(g_out, 0, [0, 1, "h"] + down, bf16)
    grad_ctx = dot(grad_branch, out_turn, 1, 0).astype(bf16)

    grad_sources = 0.0
    grad_normed = 0.0
    r_qkv, mean_grads, var_grads = [], [], []
    pairs = width // LANES
    for group in range(groups):
        dq, dk, dv, gm, gv = attn_backward(
            queries, kv, mean_full, var_full, lse, grad_ctx, group, groups
        )
        grads = [dot(normed, dq, 0, 0), dot(sources, dk, 0, 0), dot(sources, dv, 0, 0)]
        g_qkv = jnp.stack(grads).reshape(3, count, rows, -1)
        order = [0, "h", 1] if group % 2 == 0 else [0, 1, "h"]
        r_qkv.append(links.reduce(g_qkv, 1, order + down, bf16))
        mean_grads.append(gm)
        var_grads.append(gv)
        part = qkv_full.reshape(3, width, pairs // groups, groups, LANES)[:, :, :, group]
        part = part.reshape(3, width, -1)
        grad_normed = grad_normed + dot(dq, part[0], 1, 1)
        grad_sources = grad_sources + dot(dk, part[1], 1, 1) + dot(dv, part[2], 1, 1)
    grad_normed = grad_normed + grad_sources[length : 2 * length]
    grad_memory = grad_sources[2 * length :].astype(bf16)
    grad_fit = dot(ridge, grad_memory, 0, 0)
    grad_samples = grad_fit[:length].astype(bf16)
    grad_coeffs = here * dot(old_basis, grad_samples, 0, 0)
    grad_past = grad_sources[:length] + grad_fit[length:]
    _, first_pull = jax.vjp(layer_norm, tokens32, gain_a)
    grad_tokens_norm, gain_one = first_pull(grad_normed)
    _, past_pull = jax.vjp(layer_norm, earlier32, gain_a)
    _, gain_two = past_pull(grad_past)
    grad_tokens = grad_hidden + grad_tokens_norm

    def by_owner(gain):
        return gain.reshape(count, 2, -1)

    def map_owner(parts):
        full = jnp.stack(parts, axis=1).reshape(2, local_heads, count, mem_part)
        return full.transpose(2, 0, 1, 3).reshape(count, 2, -1)

    tiny = jnp.concatenate(
        [by_owner(gain_one + gain_two), by_owner(gain_m_grad), map_owner(mean_grads), map_owner(var_grads)],
        axis=2,
    )
    gain_part = width // (2 * count)
    map_part = local_heads * mem_part
    tiny = jnp.pad(tiny, ((0, 0), (0, 0), (0, -tiny.shape[2] % LANES)))
    tiny = links.reduce(tiny.reshape(count, 1, -1), 0, [0, "h", 1] + down, f32).reshape(-1)
    gain_a_out = tiny[:gain_part]
    gain_m_out = tiny[gain_part : 2 * gain_part]
    mean_out = tiny[2 * gain_part : 2 * gain_part + map_part].reshape(local_heads, mem_part)
    var_out = tiny[2 * gain_part + map_part : 2 * gain_part + 2 * map_part]
    var_out = var_out.reshape(local_heads, mem_part)
    return (
        output[None],
        grad_tokens[None],
        grad_coeffs[None],
        jnp.concatenate(r_qkv, axis=2),
        r_out.T,
        r_up,
        r_down.T,
        gain_a_out,
        gain_m_out,
        mean_out,
        var_out,
    )


def solution(mesh):
    sizes = dict(mesh.shape)
    both = ("items", "heads")
    in_specs = (
        P(both, None, None),
        P(both, None, None),
        P(both, None, None),
        P(both),
        P(both, None),
        P(None, "items", "heads"),
        P("heads", "items"),
        P("items", "heads"),
        P("heads", "items"),
        P("items"),
        P("items"),
        P("heads", "items"),
        P("heads", "items"),
        P(both, None, None),
    )
    out_specs = (
        P(both, None, None),
        P(both, None, None),
        P(both, None, None),
        P(None, "items", "heads"),
        P("heads", "items"),
        P("items", "heads"),
        P("heads", "items"),
        P(both),
        P(both),
        P("heads", "items"),
        P("heads", "items"),
    )

    def body(*args):
        return shards(*args, sizes=sizes, groups=3)

    return jax.shard_map(body, mesh=mesh, in_specs=in_specs, out_specs=out_specs, check_vma=False)
```

```python
import math

import jax
import jax.numpy as jnp
import numpy as np
from jax import lax
from jax.experimental import pallas as pl
from jax.experimental.pallas import tpu as pltpu
from jax.sharding import Mesh
from jax.sharding import PartitionSpec as P

HD = 64
GRID = 1024
EPSILON = 1e-05
VAR_SCALE = 0.01
RIDGE = 1.0
LANES = 128
ROWS = 256
NEG = -1e30
bf16 = jnp.bfloat16
f32 = jnp.float32


def dot(a, b, ca, cb):
    return lax.dot_general(a, b, (((ca,), (cb,)), ((), ())), preferred_element_type=f32)


def layer_norm(values, gain_vec):
    row_mean = jnp.mean(values, axis=-1, keepdims=True)
    centred = values - row_mean
    spread = jnp.mean(centred * centred, axis=-1, keepdims=True)
    return centred * lax.rsqrt(spread + EPSILON) * gain_vec


def basis_at(points, basis_count):
    centers = (jnp.arange(basis_count, dtype=f32) + 0.5) / basis_count
    offset = points[..., None] - centers
    return jnp.exp(-offset * offset * (0.5 * basis_count * basis_count))


def ridge_table(basis_count, samples):
    points = (np.arange(samples) + 0.5) / samples
    centers = (np.arange(basis_count) + 0.5) / basis_count
    design = np.exp(-((points[:, None] - centers) ** 2) * (0.5 * basis_count * basis_count))
    gram = design.T @ design + RIDGE * np.eye(basis_count)
    factor = np.linalg.cholesky(gram)
    table = np.linalg.solve(factor.T, np.linalg.solve(factor, design.T))
    return jnp.asarray(table.astype(np.float32)).astype(bf16)


def gelu_tanh(values):
    return jax.nn.gelu(values, approximate=True)


def near_scores(q_rows, keys, block):
    reach = keys.shape[0] // 2 + (block + 1) * ROWS
    scores = dot(q_rows, keys[:reach], 1, 1)
    row = lax.broadcasted_iota(jnp.int32, (ROWS, ROWS), 0)
    col = lax.broadcasted_iota(jnp.int32, (ROWS, ROWS), 1)
    edge = jnp.where(col <= row, scores[:, reach - ROWS :], NEG)
    return jnp.concatenate([scores[:, : reach - ROWS], edge], axis=1), reach


def density_parts(scaled, w_mean, w_var):
    basis_count = scaled.shape[1]
    index = lax.broadcasted_iota(jnp.int32, (1, basis_count), 1).astype(f32)
    centers = (index + 0.5) / basis_count
    middle = jax.nn.sigmoid(jnp.sum(scaled * w_mean, axis=1, keepdims=True))
    var_raw = jnp.sum(scaled * w_var, axis=1, keepdims=True)
    softplus = jnp.maximum(var_raw, 0.0) + jnp.log1p(jnp.exp(-jnp.abs(var_raw)))
    variance = VAR_SCALE * softplus + 1.0 / (basis_count * basis_count)
    offset = middle - centers
    inv_var = 1.0 / variance
    square = offset * offset * inv_var
    scale = lax.rsqrt(2.0 * math.pi * variance) / basis_count
    weights = jnp.exp(-0.5 * square) * scale
    return weights, middle, var_raw, inv_var, offset, square


def attn_fwd_kernel(q_ref, k_ref, v_ref, mk_ref, mv_ref, wm_ref, wv_ref, ctx_ref, lse_ref):
    half = lax.broadcasted_iota(jnp.int32, (1, LANES), 1) < HD
    length = q_ref.shape[0]
    keys, values = k_ref[...], v_ref[...]
    mem_keys, mem_values = mk_ref[...], mv_ref[...]
    for block in range(length // ROWS):
        rows = slice(block * ROWS, (block + 1) * ROWS)
        q_rows = q_ref[rows, :] * jnp.asarray(0.125, bf16)
        outs, sums = [], []
        for head in range(2):
            mine = half if head == 0 else jnp.logical_not(half)
            q_head = jnp.where(mine, q_rows, jnp.zeros_like(q_rows))
            scores, reach = near_scores(q_head, keys, block)
            top = jnp.max(scores, axis=1, keepdims=True)
            raw = jnp.exp(scores - top)
            total = jnp.sum(raw, axis=1, keepdims=True)
            probs = (raw * (1.0 / total)).astype(bf16)
            near = dot(probs, values[:reach], 1, 0)
            scaled = dot(q_head, mem_keys, 1, 1)
            weights = density_parts(
                scaled, wm_ref[0, head : head + 1, :], wv_ref[0, head : head + 1, :]
            )[0]
            outs.append(near + dot(weights.astype(bf16), mem_values, 1, 0))
            sums.append(top + jnp.log(total))
        ctx_ref[rows, :] = jnp.where(half, outs[0], outs[1]).astype(bf16)
        lse_ref[rows, :] = jnp.where(half, sums[0], sums[1])


def attn_bwd_kernel(
    order, rows_own, place_ref,
    q_ref, k_ref, v_ref, mk_ref, mv_ref, wm_ref, wv_ref, lse_ref, do_ref, turned_ref,
    dq_ref, dk_ref, dv_ref, maps_ref, send_ref, keep_ref, acck_ref, accv_ref,
):
    half = lax.broadcasted_iota(jnp.int32, (1, LANES), 1) < HD
    length = q_ref.shape[0]
    near_rows = k_ref.shape[0]
    keys, values = k_ref[...], v_ref[...]
    mem_keys, mem_values = mk_ref[...], mv_ref[...]
    for block in reversed(range(length // ROWS)):
        rows = slice(block * ROWS, (block + 1) * ROWS)
        q_full, do_full = q_ref[rows, :], do_ref[rows, :]
        q_rows = q_full * jnp.asarray(0.125, bf16)
        q_turn, do_turn = q_full.T, do_full.T
        outs = []
        for head in range(2):
            part = slice(head * HD, (head + 1) * HD)
            mine = half if head == 0 else jnp.logical_not(half)
            q_head = jnp.where(mine, q_rows, jnp.zeros_like(q_rows))
            do_head = jnp.where(mine, do_full, jnp.zeros_like(do_full))
            scores, reach = near_scores(q_head, keys, block)
            probs = jnp.exp(scores - lse_ref[rows, head * HD : head * HD + 1])
            grad_probs = dot(do_head, values[:reach], 1, 1)
            inner = jnp.sum(probs * grad_probs, axis=1, keepdims=True)
            grad_raw = (0.125 * probs * (grad_probs - inner)).astype(bf16)
            probs_low = probs.astype(bf16)
            dk_part = dot(q_turn[part], grad_raw, 1, 0)
            dv_part = dot(do_turn[part], probs_low, 1, 0)
            out = dot(grad_raw, keys[:reach], 1, 0)
            w_mean, w_var = wm_ref[0, head : head + 1, :], wv_ref[0, head : head + 1, :]
            scaled = dot(q_head, mem_keys, 1, 1)
            weights, middle, var_raw, inv_var, offset, square = density_parts(scaled, w_mean, w_var)
            grad_w = dot(do_head, mem_values, 1, 1) * weights
            d_mid = -jnp.sum(grad_w * offset, axis=1, keepdims=True) * inv_var
            d_var = jnp.sum(grad_w * (square - 1.0), axis=1, keepdims=True) * (0.5 * inv_var)
            d_mid = d_mid * middle * (1.0 - middle)
            d_var = d_var * VAR_SCALE * jax.nn.sigmoid(var_raw)
            gm_part = jnp.sum(scaled * d_mid, axis=0, keepdims=True)
            gv_part = jnp.sum(scaled * d_var, axis=0, keepdims=True)
            grad_mem = (0.125 * (d_mid * w_mean + d_var * w_var)).astype(bf16)
            outs.append(out + dot(grad_mem, mem_keys, 1, 0))
            dmk_part = dot(q_turn[part], grad_mem, 1, 0)
            dmv_part = dot(do_turn[part], weights.astype(bf16), 1, 0)
            if block == length // ROWS - 1:
                acck_ref[part, :near_rows] = dk_part
                accv_ref[part, :near_rows] = dv_part
                acck_ref[part, near_rows:] = dmk_part
                accv_ref[part, near_rows:] = dmv_part
                maps_ref[0, head : head + 1, :] = gm_part
                maps_ref[0, 2 + head : 3 + head, :] = gv_part
            else:
                acck_ref[part, :reach] += dk_part
                accv_ref[part, :reach] += dv_part
                acck_ref[part, near_rows:] += dmk_part
                accv_ref[part, near_rows:] += dmv_part
                maps_ref[0, head : head + 1, :] += gm_part
                maps_ref[0, 2 + head : 3 + head, :] += gv_part
        dq_ref[rows, :] = jnp.where(half, outs[0], outs[1]).astype(bf16)
    dk_ref[...] = acck_ref[...].T.astype(bf16)
    dv_ref[...] = accv_ref[...].T.astype(bf16)
    turned = turned_ref[...]
    grads = (
        dot(turned[:, length : 2 * length], dq_ref[...], 1, 0),
        dot(turned, dk_ref[...], 1, 0),
        dot(turned, dv_ref[...], 1, 0),
    )
    for at, grad in enumerate(grads):
        send, keep = cut_core(grad, place_ref[0], rows_own, order)
        send_ref[:, at], keep_ref[:, at] = send.astype(bf16), keep


def attn_specs(length, basis_count, place):
    near_rows = 2 * length
    near = pl.BlockSpec((near_rows, LANES), lambda p, *_: (0, place(p)))
    far = pl.BlockSpec((basis_count, LANES), lambda p, *_: (near_rows // basis_count, place(p)))
    maps = pl.BlockSpec((1, 2, basis_count), lambda p, *_: (place(p), 0, 0))
    return [pl.BlockSpec((length, LANES), lambda p, *_: (0, place(p))), near, near, far, far, maps, maps]


def attn_forward(queries, keys, values, w_mean, w_var):
    length, width = queries.shape
    basis_count = w_mean.shape[-1]
    pairs = width // LANES
    return pl.pallas_call(
        attn_fwd_kernel,
        grid=(pairs,),
        in_specs=attn_specs(length, basis_count, lambda p: p),
        out_specs=[
            pl.BlockSpec((length, LANES), lambda p: (0, p)),
            pl.BlockSpec((length, LANES), lambda p: (0, p)),
        ],
        out_shape=[
            jax.ShapeDtypeStruct((length, width), bf16),
            jax.ShapeDtypeStruct((length, width), f32),
        ],
        compiler_params=pltpu.CompilerParams(vmem_limit_bytes=60 << 20),
        cost_estimate=pl.CostEstimate(
            flops=8 * length * length * width, bytes_accessed=8 << 20, transcendentals=0
        ),
        name="attn_forward",
    )(queries, keys, values, keys, values, w_mean, w_var)


def attn_backward(place, queries, keys, values, w_mean, w_var, lse, grad_ctx, turned, group, groups, order, rows, span, into):
    length, width = queries.shape
    basis_count = w_mean.shape[-1]
    pairs = width // LANES
    count = pairs // groups
    where = lambda p: p * groups + group
    all_rows = keys.shape[0]
    wide = count * LANES
    by_pair = lambda *shape: pl.BlockSpec(shape + (LANES,), lambda p, _: (0,) * len(shape) + (p,))
    maps = pl.BlockSpec((1, 4, basis_count), lambda p, _: (p, 0, 0))
    ours = pl.BlockSpec((length, LANES), lambda p, _: (0, where(p)))
    cut = (len(order), 3, rows)
    mine = pl.BlockSpec(cut + (LANES,), lambda p, _: (0, 0, 0, p * len(span) + group - span[0]))
    specs = attn_specs(length, basis_count, where) + [ours, ours, whole_spec(*turned.shape)]
    held = [pl.BlockSpec(memory_space=pl.ANY)] * len(into)

    def kernel(*refs):
        at = 1 + len(specs)
        attn_bwd_kernel(order, rows, *refs[:at], *refs[at + len(into) :])

    return call(
        kernel, "attn_backward", (count,),
        specs + held,
        [
            (by_pair(length), struct(bf16, length, wide)),
            (by_pair(all_rows), struct(bf16, all_rows, wide)),
            (by_pair(all_rows), struct(bf16, all_rows, wide)),
            (maps, struct(f32, count, 4, basis_count)),
            (mine, struct(bf16, *cut, wide * len(span))),
            (mine, struct(f32, *cut, wide * len(span))),
        ],
        scratch=[pltpu.VMEM((LANES, all_rows), f32), pltpu.VMEM((LANES, all_rows), f32)],
        vmem=60,
        aliases={1 + len(specs) + i: 4 + i for i in range(len(into))},
    )(place, queries, keys, values, keys, values, w_mean, w_var, lse, grad_ctx, turned, *into)


def norm_stats(values):
    centred = values - jnp.mean(values, axis=-1, keepdims=True)
    spread = jnp.mean(centred * centred, axis=-1, keepdims=True)
    inverse = lax.rsqrt(spread + EPSILON)
    return centred * inverse, inverse


def norm_back(grad, hat, inverse, gain):
    scaled = grad * gain
    inner = jnp.mean(scaled * hat, axis=-1, keepdims=True)
    return inverse * (scaled - jnp.mean(scaled, axis=-1, keepdims=True) - hat * inner)


def side_block(ref):
    chips, cores, _, rows, cols = ref.shape
    return ref[...].reshape(chips * cores * rows, cols)


def block_order(bits):
    chips = []
    for place in range(1 << len(bits)):
        chip = 0
        for at, bit in enumerate(reversed(bits)):
            chip |= ((place >> at) & 1) << (bit - 1)
        chips.append(chip)
    return chips


def cut_core(value, core, rows, order):
    split = value.reshape(value.shape[0] // (2 * rows), 2, rows, value.shape[1])
    low = jnp.stack([split[chip, 0] for chip in order])
    high = jnp.stack([split[chip, 1] for chip in order])
    return jnp.where(core == 0, high, low), jnp.where(core == 0, low, high)


def mix_kernel(ctx_ref, tokens_ref, w0_ref, w1_ref, gain_ref, hidden_ref, normed_ref):
    side = w0_ref.shape[4]
    ctx = ctx_ref[...]
    mixed = dot(ctx[:, :side], side_block(w0_ref), 1, 1)
    mixed = mixed + dot(ctx[:, side:], side_block(w1_ref), 1, 1)
    hidden = tokens_ref[...].astype(f32) + mixed
    hidden_ref[...] = hidden
    normed_ref[...] = (norm_stats(hidden)[0] * gain_ref[...]).astype(bf16)


def feed_kernel(
    order, place_ref, normed_ref, normed2_ref, cot_ref, cot2_ref, up_ref, down_ref,
    mlp_ref, mlp2_ref, gn_ref, gn2_ref, down_send_ref, down_keep_ref, up_send_ref, up_keep_ref,
    nt_ref, ct_ref, act_ref, pre_ref, acc_ref,
):
    step = pl.program_id(0)
    length, width = normed_ref.shape
    block = up_ref.shape[1] * up_ref.shape[3]
    w_up, w_down = side_block(up_ref), side_block(down_ref)
    slope = math.sqrt(2.0 / math.pi)

    @pl.when(step == 0)
    def _():
        nt_ref[:, :length] = normed_ref[...].T
        nt_ref[:, length:] = normed2_ref[...].T
        ct_ref[:, :length] = cot_ref[...].T
        ct_ref[:, length:] = cot2_ref[...].T

    for half in range(2):
        rows = slice(half * length, (half + 1) * length)
        normed = (normed_ref, normed2_ref)[half][...]
        cot = (cot_ref, cot2_ref)[half][...]
        pre = dot(normed, w_up, 1, 0)
        square = pre * pre
        bend = jnp.tanh(slope * pre * (1.0 + 0.044715 * square))
        lift = 0.5 + 0.5 * bend
        act = (pre * lift).astype(bf16)
        rise = lift + 0.5 * pre * (1.0 - bend * bend) * (slope + (3.0 * 0.044715 * slope) * square)
        grad_pre = (dot(cot, w_down, 1, 0) * rise).astype(bf16)
        act_ref[rows, :] = act
        pre_ref[rows, :] = grad_pre
        mlp = dot(act, w_down, 1, 1)
        grad_normed = dot(grad_pre, w_up, 1, 1)

        @pl.when(step == 0)
        def _():
            acc_ref[2 * half] = mlp
            acc_ref[2 * half + 1] = grad_normed

        @pl.when(step == 1)
        def _():
            if half == 0:
                mlp_ref[...] = acc_ref[0] + mlp
                gn_ref[...] = acc_ref[1] + grad_normed
            else:
                mlp2_ref[...] = (acc_ref[2] + mlp).astype(bf16)
                gn2_ref[...] = (acc_ref[3] + grad_normed).astype(bf16)

    g_down = dot(ct_ref[...], act_ref[...], 1, 0).reshape(width // block, block, -1)
    g_down = jnp.stack([g_down[chip] for chip in order])

    @pl.when(step == 0)
    def _():
        down_send_ref[...] = g_down.astype(bf16)

    @pl.when(step == 1)
    def _():
        down_keep_ref[...] = g_down

    g_up = dot(nt_ref[...], pre_ref[...], 1, 0).reshape(width // block, block, -1)
    low = jnp.stack([g_up[chip] for chip in order[: len(order) // 2]])
    high = jnp.stack([g_up[chip] for chip in order[len(order) // 2 :]])
    first = place_ref[1] == 0
    up_send_ref[...] = jnp.where(first, high, low).astype(bf16)
    up_keep_ref[...] = jnp.where(first, low, high)


def turn_kernel(
    order, place_ref, hidden_ref, gn_ref, gn2_ref, mlp_ref, mlp2_ref, cot_ref, ctx_ref, w0_ref, w1_ref, gain_ref,
    gh_ref, gain_grad_ref, gc_ref, out_ref, send_ref, keep_ref,
):
    side = w0_ref.shape[4]
    hidden = hidden_ref[...]
    hat, inverse = norm_stats(hidden)
    grad = gn_ref[...] + gn2_ref[...].astype(f32)
    out_ref[...] = (hidden + (mlp_ref[...] + mlp2_ref[...].astype(f32))).astype(bf16)
    gain_grad_ref[...] = jnp.sum(grad * hat, axis=0, keepdims=True)
    grad_hidden = cot_ref[...].astype(f32) + norm_back(grad, hat, inverse, gain_ref[...])
    gh_ref[...] = grad_hidden
    branch = grad_hidden.astype(bf16)
    gc_ref[:, :side] = dot(branch, side_block(w0_ref), 1, 0).astype(bf16)
    gc_ref[:, side:] = dot(branch, side_block(w1_ref), 1, 0).astype(bf16)
    send, keep = cut_core(dot(branch, ctx_ref[...], 0, 0), place_ref[0], w0_ref.shape[3], order)
    send_ref[...], keep_ref[...] = send.astype(bf16), keep


def sources_kernel(groups, *refs):
    grads, (wq_ref, wk_ref, wv_ref) = refs[: 3 * groups], refs[3 * groups : 3 * groups + 3]
    ridge_ref, earlier_ref, tokens_ref, gain_m_ref = refs[3 * groups + 3 : 3 * groups + 7]
    maps = refs[3 * groups + 7 : 4 * groups + 7]
    normed_ref, samples_ref, small_ref = refs[4 * groups + 7 :]
    length, width = tokens_ref.shape
    count = maps[0].shape[0]
    basis_count = maps[0].shape[2]
    heads = 2 * count * groups

    def rows(at, start, size):
        parts = [grads[3 * g + at][start : start + size, :] for g in range(groups)]
        half = parts[0].shape[1] // 2
        return jnp.concatenate([p[:, :half] for p in parts] + [p[:, half:] for p in parts], axis=1)

    def part(start, size):
        out = dot(rows(1, start, size), wk_ref[...], 1, 1)
        return out + dot(rows(2, start, size), wv_ref[...], 1, 1)

    memory = part(2 * length, ridge_ref.shape[0]).astype(bf16)
    samples_ref[...] = dot(ridge_ref[:, :length], memory, 0, 0).astype(bf16)
    past = part(0, length) + dot(ridge_ref[:, length:], memory, 0, 0)
    gain = jnp.sum(past * norm_stats(earlier_ref[...].astype(f32))[0], axis=0, keepdims=True)
    grad = part(length, length) + dot(rows(0, 0, length), wq_ref[...], 1, 1)
    normed_ref[...] = grad
    gain = gain + jnp.sum(grad * norm_stats(tokens_ref[...].astype(f32))[0], axis=0, keepdims=True)
    small_ref[...] = jnp.zeros_like(small_ref)
    for group in range(groups):
        for p in range(count):
            head = 2 * (p * groups + group)
            small_ref[head : head + 2, :] = maps[group][p, 0:2, :]
            small_ref[heads + head : heads + head + 2, :] = maps[group][p, 2:4, :]
    for at in range(width // basis_count):
        cols = slice(at * basis_count, (at + 1) * basis_count)
        row = 2 * heads + 2 * at
        small_ref[row : row + 1, :] = gain[:, cols]
        small_ref[row + 1 : row + 2, :] = gain_m_ref[:, cols]


def last_kernel(grad_ref, samples_ref, basis_ref, tokens_ref, gh_ref, gain_ref, here_ref, gt_ref, gc_ref):
    gc_ref[...] = here_ref[0] * dot(basis_ref[...], samples_ref[...], 0, 0)
    hat, inverse = norm_stats(tokens_ref[...].astype(f32))
    gt_ref[...] = gh_ref[...] + norm_back(grad_ref[...], hat, inverse, gain_ref[...])


def whole_spec(*shape):
    return pl.BlockSpec(shape, lambda *_: (0,) * len(shape))


def struct(kind, *shape):
    return jax.ShapeDtypeStruct(shape, kind)


def call(kernel, name, grid, in_specs, outs, scratch=(), scalars=1, flops=0, vmem=60, aliases={}):
    return pl.pallas_call(
        kernel,
        grid_spec=pltpu.PrefetchScalarGridSpec(
            num_scalar_prefetch=scalars,
            grid=grid,
            in_specs=in_specs,
            out_specs=[whole_spec(*out.shape) if spec is None else spec for spec, out in outs],
            scratch_shapes=scratch,
        ),
        out_shape=[out for _, out in outs],
        input_output_aliases=aliases,
        compiler_params=pltpu.CompilerParams(vmem_limit_bytes=vmem << 20),
        cost_estimate=pl.CostEstimate(flops=flops, bytes_accessed=1 << 20, transcendentals=0),
        name=name,
    )


def mix(context, tokens, rest, gain, side):
    length, width = tokens.shape
    big = whole_spec(length, width)
    return call(
        mix_kernel, "mix", (1,),
        [big, big] + out_weights(rest, side) + [whole_spec(1, width)],
        [(None, struct(f32, length, width)), (None, struct(bf16, length, width))],
        scalars=0,
    )(context, tokens, rest, rest, gain)


def out_weights(rest, side):
    chips, cores, _, rows, wide = rest.shape
    last = wide // side - 1
    return [
        pl.BlockSpec((chips, cores, 1, rows, side), lambda *_, h=h: (0, 0, h, 0, last)) for h in range(2)
    ]


def feed(place, normed, normed2, cot, cot2, rest, tile, order):
    length, width = normed.shape
    chips, cores, _, rows, _ = rest.shape
    block = cores * rows
    big = whole_spec(length, width)

    def weights(at):
        return pl.BlockSpec(
            (chips, cores, 1, rows, tile), lambda s, p: (0, 0, (s + 1 + p[2]) % 2, 0, at + p[0])
        )

    half = (chips // 2, block, 2 * tile)
    turned = pl.BlockSpec((chips // 2, block, tile), lambda s, p: (0, 0, (s + 1 + p[2]) % 2))
    return call(
        lambda *refs: feed_kernel(order, *refs), "feed", (2,),
        [big, big, big, big, weights(0), weights(2)],
        [
            (None, struct(f32, length, width)),
            (None, struct(bf16, length, width)),
            (None, struct(f32, length, width)),
            (None, struct(bf16, length, width)),
            (None, struct(bf16, chips, block, tile)),
            (None, struct(f32, chips, block, tile)),
            (turned, struct(bf16, *half)),
            (turned, struct(f32, *half)),
        ],
        scratch=[
            pltpu.VMEM((width, 2 * length), bf16),
            pltpu.VMEM((width, 2 * length), bf16),
            pltpu.VMEM((2 * length, tile), bf16),
            pltpu.VMEM((2 * length, tile), bf16),
            pltpu.VMEM((4, length, width), f32),
        ],
        vmem=60,
    )(place, normed, normed2, cot, cot2, rest, rest)


def turn(place, hidden, gn, gn2, mlp, mlp2, cot, context, rest, gain, side, order):
    length, width = hidden.shape
    big = whole_spec(length, width)
    cut = (rest.shape[0], rest.shape[3], width)
    return call(
        lambda *refs: turn_kernel(order, *refs), "turn", (1,),
        [big] * 7 + out_weights(rest, side) + [whole_spec(1, width)],
        [
            (None, struct(f32, length, width)),
            (None, struct(f32, 1, width)),
            (None, struct(bf16, length, width)),
            (None, struct(bf16, length, width)),
            (None, struct(bf16, *cut)),
            (None, struct(f32, *cut)),
        ],
    )(place, hidden, gn, gn2, mlp, mlp2, cot, context, rest, rest, gain)


def grad_sources_of(parts, weights, ridge, earlier, tokens, gain_m_grad, maps):
    flat = [x for part in parts for x in part]
    length, width = tokens.shape
    basis_count = ridge.shape[0]
    heads = 4 * len(maps) * maps[0].shape[0]
    args = (*flat, *weights, ridge, earlier, tokens, gain_m_grad, *maps)
    small = heads + 2 * (width // basis_count)
    return call(
        lambda *refs: sources_kernel(len(parts), *refs), "grad_sources", (1,),
        [whole_spec(*x.shape) for x in args],
        [
            (None, struct(f32, length, width)),
            (None, struct(bf16, length, width)),
            (None, struct(f32, small + (-small) % 8, basis_count)),
        ],
        scalars=0,
    )(*args)


def last(grad, samples, basis, tokens, grad_hidden, gain, here):
    length, width = tokens.shape
    args = (grad, samples, basis, tokens, grad_hidden, gain)
    return call(
        last_kernel, "last", (1,),
        [whole_spec(*x.shape) for x in args] + [pl.BlockSpec(memory_space=pltpu.SMEM)],
        [(None, struct(f32, length, width)), (None, struct(f32, basis.shape[1], width))],
        scalars=0,
    )(*args, here)


class Links:
    def __init__(self, sizes):
        self.chips = sizes["chips"]
        self.bits = self.chips.bit_length()
        self.chip = lax.axis_index("chips")
        self.core = lax.axis_index("core")
        self.side = lax.axis_index("heads")

    def swap(self, value, stage):
        if stage in ("h", 0):
            return lax.ppermute(value, "heads" if stage == "h" else "core", [(0, 1), (1, 0)])
        mask = 1 << (stage - 1)
        return lax.ppermute(value, "chips", [(i, i ^ mask) for i in range(self.chips)])

    def bit(self, stage):
        if stage == "h":
            return self.side
        return self.core if stage == 0 else (self.chip >> (stage - 1)) & 1

    def gather(self, value, lead, stages, have=()):
        have = list(have)
        for stage in stages:
            other = self.swap(value, stage)
            if stage == "h":
                value = self.gather_with(value, other, stage, None)
            else:
                place = lead + sum(1 for b in have if b > stage)
                value = self.gather_with(value, other, stage, place)
                have.append(stage)
        return value

    def gather_with(self, value, other, stage, axis=0):
        mine_first = self.bit(stage) == 0
        first = jnp.where(mine_first, value, other)
        second = jnp.where(mine_first, other, value)
        if axis is None:
            return jnp.concatenate([first, second], axis=-1)
        return jnp.stack([first, second], axis=axis)

    def whole_rows(self, value, rows):
        value = value.reshape(2, rows, -1)
        mine = lax.dynamic_index_in_dim(value, self.core, 0, keepdims=False)
        other = self.swap(lax.dynamic_index_in_dim(value, 1 - self.core, 0, keepdims=False), 0)
        return self.gather_with(mine, other, 0, None)


def tie(value, *earlier):
    return lax.optimization_barrier((value,) + earlier)[0]


class Chain:
    def __init__(self, links, stages, send, keep, wire=bf16):
        self.links, self.wire = links, wire
        self.stage, self.stages = stages[0], list(stages[1:])
        self.left = [stage for stage in self.stages if stage != "h"]
        self.send, self.keep = self.spread(send), self.spread(keep)

    def spread(self, value):
        return value.reshape((2,) * len(self.left) + value.shape[1:])

    def cut(self):
        value = self.keep + self.came.astype(f32)
        self.stage = self.stages.pop(0) if self.stages else None
        if self.stage is None:
            self.value = value
            return
        bit = self.links.bit(self.stage)
        if self.stage == "h":
            width = value.shape[-1] // 2
            take = lambda b: lax.dynamic_slice_in_dim(value, b * width, width, axis=value.ndim - 1)
        else:
            axis = self.left.index(self.stage)
            self.left.pop(axis)
            take = lambda b: lax.dynamic_index_in_dim(value, b, axis, keepdims=False)
        self.send = take(1 - bit).astype(self.wire)
        self.keep = take(bit)


def together(values):
    return list(lax.optimization_barrier(tuple(values)))


def start(chains):
    chains = [chain for chain in chains if chain.stage is not None]
    if chains:
        for chain, send in zip(chains, together([chain.send for chain in chains])):
            chain.send = send
            chain.came = chain.links.swap(send, chain.stage)


def arrive(chains, *after):
    chains = [chain for chain in chains if chain.stage is not None]
    if chains:
        came = together([chain.came for chain in chains] + list(after))
        for chain, value in zip(chains, came):
            chain.came = value
            chain.cut()


def shards(
    tokens, earlier, coeffs, present, sample_at, w_qkv, w_out, w_up, w_down,
    gain_attn, gain_mlp, w_mean, w_var, cotangent, sizes, groups,
):
    links = Links(sizes)
    high = list(range(2, links.bits))
    count = 2 * links.chips
    tokens, earlier, coeffs, cotangent = tokens[0], earlier[0], coeffs[0], cotangent[0]
    length, width = tokens.shape
    basis_count = coeffs.shape[0]
    rows, side = w_qkv.shape[1], w_qkv.shape[2]
    ff_side = w_up.shape[1]
    local_heads, mem_part = w_mean.shape

    rest = jnp.concatenate([w_up, w_down.T, w_out.T], axis=1).astype(bf16)
    rest = lax.all_gather(rest, ("chips", "core", "heads"), axis=0, tiled=False)
    rest = rest.reshape(links.chips, 2, 2, rows, -1)
    tile = ff_side // 2
    small = jnp.concatenate(
        [gain_attn, gain_mlp, w_mean.reshape(-1), w_var.reshape(-1)]
    ).astype(bf16)
    small_size = small.shape[0]
    small = jnp.pad(small, (0, -small_size % LANES)).reshape(1, -1)
    small_h = links.swap(small, "h")
    first = jnp.where(links.side == 0, small, small_h)
    second = jnp.where(links.side == 0, small_h, small)
    far = high[1:][::-1]
    parts = links.gather(w_qkv.astype(bf16), 1, far)
    small = links.gather(jnp.concatenate([first, second], axis=0), 0, far)
    small, parts = together([small, parts])
    turns = ([2, 1, "h"], [1, "h", 2], ["h", 2, 1])
    parts = [parts[c] for c in range(3)]
    have = list(far)
    haves = [list(far) for _ in range(3)]
    for step in range(3):
        small = links.gather(small, 0, [2 - step], have)
        have.append(2 - step)
        for c in range(3):
            parts[c] = links.gather(parts[c], 0, [turns[c][step]], haves[c])
            if turns[c][step] != "h":
                haves[c].append(turns[c][step])
        if step < 2:
            small, *parts = together([small] + parts)
    qkv_full = [links.gather(parts[c], 0, [0], haves[c]).reshape(width, width) for c in range(3)]
    small = small.reshape(count, 2, -1).astype(f32)
    gain_a = small[:, 0, :rows].reshape(-1)
    gain_m = small[:, 0, rows : 2 * rows].reshape(-1)

    def head_map(start):
        part = small[:, :, start : start + local_heads * mem_part]
        part = part.reshape(count, 2, local_heads, mem_part).transpose(1, 2, 0, 3)
        return part.reshape(local_heads, 2, basis_count)

    mean_full = head_map(2 * rows)
    var_full = head_map(2 * rows + local_heads * mem_part)

    cot2 = links.swap(cotangent, 0)
    place = jnp.stack([links.core, links.bit(1), links.side]).astype(jnp.int32)

    ridge = ridge_table(basis_count, 2 * length)
    tokens32, earlier32 = tokens.astype(f32), earlier.astype(f32)
    normed = layer_norm(tokens32, gain_a).astype(bf16)
    past = layer_norm(earlier32, gain_a).astype(bf16)
    old_basis = basis_at((sample_at[0].astype(f32) + 0.5) / GRID, basis_count).astype(bf16)
    here = present[0].astype(f32)
    samples = (here * dot(old_basis, coeffs.astype(bf16), 1, 0)).astype(bf16)
    memory = dot(ridge, jnp.concatenate([samples, past], axis=0), 1, 0).astype(bf16)
    sources = jnp.concatenate([past, normed, memory], axis=0)
    queries = dot(normed, qkv_full[0], 1, 0).astype(bf16)
    keys = dot(sources, qkv_full[1], 1, 0).astype(bf16)
    values = dot(sources, qkv_full[2], 1, 0).astype(bf16)
    context, lse = attn_forward(queries, keys, values, mean_full, var_full)
    context, turned = together([context, sources.T])
    gain_row = gain_m.reshape(1, -1)
    hidden, normed_mlp = mix(context, tokens, rest, gain_row, side)
    normed_mlp2 = links.swap(normed_mlp, 0)
    lows = [2] + high[1:]
    order = block_order([1] + lows)
    mlp, mlp2, gn, gn2, down_send, down_keep, up_send, up_keep = feed(
        place, normed_mlp, normed_mlp2, cotangent, cot2, rest, tile, order
    )
    gn2 = links.swap(gn2, 0)
    mlp2 = links.swap(mlp2, 0)
    c_down = Chain(links, ["h", 1] + lows, down_send, down_keep)
    c_up = Chain(links, [1, "h"] + lows, up_send, up_keep)
    start([c_down, c_up])
    turned_order = block_order([2, 1] + high[1:])
    grad_hidden, gain_m_grad, grad_ctx, output, out_send, out_keep = turn(
        place, hidden, gn, gn2, mlp, mlp2, cotangent, context, rest, gain_row, side, turned_order
    )
    c_out = Chain(links, [0, 2, "h", 1] + high[1:], out_send, out_keep)
    start([c_out])

    maps, head_grads, c_qkv = [], [], []
    chains = [c_down, c_up, c_out]
    spans = [list(range(groups - 1)), [groups - 1]]
    plans = ([2, 1, "h"], [1, "h", 2])
    into = ()
    for group in range(groups):
        at = 0 if group < groups - 1 else 1
        plan = plans[at] + high[1:]
        dq, dk, dv, small_maps, send, keep = attn_backward(
            place, queries, keys, values, mean_full, var_full, lse, grad_ctx, turned, group, groups,
            block_order([b for b in plan if b != "h"]), rows, spans[at], into,
        )
        into = (send, keep)
        head_grads.append((dq, dk, dv))
        maps.append(small_maps)
        arrive(chains, dq)
        if group == spans[at][-1]:
            into = ()
            chain = Chain(links, [0] + plan, send, keep)
            chain.send = tie(chain.send, *[c.send for c in chains if c.stage is not None])
            start([chain])
            start(chains)
            arrive([chain])
            start([chain])
            chains.append(chain)
            c_qkv.append(chain)
        else:
            start(chains)
        sends = [c.send for c in chains if c.stage is not None]
        grad_ctx = tie(grad_ctx, *sends)
    first_grads = tie(head_grads[0][0], *sends)
    head_grads[0] = (first_grads,) + head_grads[0][1:]
    grad_normed, grad_samples, tiny = grad_sources_of(
        head_grads, qkv_full, ridge, earlier, tokens, gain_m_grad, maps
    )
    arrive(chains, grad_samples)

    def add_all(value, stages):
        for stage in stages:
            value = value + links.swap(value, stage)
        return value

    start(chains)
    tiny = add_all(tiny, [0, "h"])
    tiny, grad_samples = together([tiny, tie(grad_samples, *[c.send for c in chains if c.stage is not None])])
    tiny = add_all(tiny, [1])
    grad_tokens, grad_coeffs = last(
        grad_normed, grad_samples, old_basis, tokens, grad_hidden, gain_a.reshape(1, -1), here.reshape(1)
    )
    arrive(chains, grad_coeffs)
    for stage in lows:
        start(chains)
        tiny = add_all(tiny, [stage])
        arrive(chains)
    while any(chain.stage is not None for chain in chains):
        start(chains)
        arrive(chains)
    r_down, r_up = links.whole_rows(c_down.value, rows), links.whole_rows(c_up.value, rows)
    r_out = c_out.value
    r_qkv = [chain.value for chain in c_qkv]
    heads = 2 * local_heads
    item = 2 * links.chip + links.core
    pick_map = lambda first: lax.dynamic_slice(
        tiny, (first + local_heads * links.side, item * mem_part), (local_heads, mem_part)
    )
    mean_out, var_out = pick_map(0), pick_map(heads)
    gains = tiny[2 * heads : 2 * heads + 2 * (width // basis_count)].reshape(-1, 2, basis_count)
    gain_part = width // (2 * count)
    pick_gain = lambda at: lax.dynamic_slice(
        gains[:, at].reshape(-1), ((2 * item + links.side) * gain_part,), (gain_part,)
    )
    gain_a_out, gain_m_out = pick_gain(0), pick_gain(1)
    return (
        output[None],
        grad_tokens[None],
        grad_coeffs[None],
        jnp.concatenate(r_qkv, axis=2),
        r_out.T,
        r_up,
        r_down.T,
        gain_a_out,
        gain_m_out,
        mean_out,
        var_out,
    )


def solution(mesh):
    sizes = dict(mesh.shape)
    both = ("items", "heads")
    in_specs = (
        P(both, None, None),
        P(both, None, None),
        P(both, None, None),
        P(both),
        P(both, None),
        P(None, "items", "heads"),
        P("heads", "items"),
        P("items", "heads"),
        P("heads", "items"),
        P("items"),
        P("items"),
        P("heads", "items"),
        P("heads", "items"),
        P(both, None, None),
    )
    out_specs = (
        P(both, None, None),
        P(both, None, None),
        P(both, None, None),
        P(None, "items", "heads"),
        P("heads", "items"),
        P("items", "heads"),
        P("heads", "items"),
        P(both),
        P(both),
        P("heads", "items"),
        P("heads", "items"),
    )

    chips = sizes["items"] // 2
    split = Mesh(mesh.devices.reshape(chips, 2, sizes["heads"]), ("chips", "core", "heads"))

    def respec(spec):
        def axis(entry):
            names = entry if isinstance(entry, tuple) else (entry,)
            flat = tuple(n for name in names for n in (("chips", "core") if name == "items" else (name,)))
            return flat if flat != (None,) else None

        return P(*(axis(entry) for entry in spec))

    def body(*args):
        return shards(*args, sizes=dict(split.shape), groups=3)

    return jax.shard_map(
        body,
        mesh=split,
        in_specs=tuple(respec(spec) for spec in in_specs),
        out_specs=tuple(respec(spec) for spec in out_specs),
        check_vma=False,
    )
```

```python
import math

import jax
import jax.numpy as jnp
import numpy as np
from jax import lax
from jax.experimental import pallas as pl
from jax.experimental.pallas import tpu as pltpu
from jax.sharding import Mesh
from jax.sharding import PartitionSpec as P

HD = 64
GRID = 1024
EPSILON = 1e-05
VAR_SCALE = 0.01
RIDGE = 1.0
LANES = 128
ROWS = 256
NEG = -1e30
bf16 = jnp.bfloat16
f32 = jnp.float32


def dot(a, b, ca, cb):
    return lax.dot_general(a, b, (((ca,), (cb,)), ((), ())), preferred_element_type=f32)


def layer_norm(values, gain_vec):
    row_mean = jnp.mean(values, axis=-1, keepdims=True)
    centred = values - row_mean
    spread = jnp.mean(centred * centred, axis=-1, keepdims=True)
    return centred * lax.rsqrt(spread + EPSILON) * gain_vec


def basis_at(points, basis_count):
    centers = (jnp.arange(basis_count, dtype=f32) + 0.5) / basis_count
    offset = points[..., None] - centers
    return jnp.exp(-offset * offset * (0.5 * basis_count * basis_count))


def ridge_table(basis_count, samples):
    points = (np.arange(samples) + 0.5) / samples
    centers = (np.arange(basis_count) + 0.5) / basis_count
    design = np.exp(-((points[:, None] - centers) ** 2) * (0.5 * basis_count * basis_count))
    gram = design.T @ design + RIDGE * np.eye(basis_count)
    factor = np.linalg.cholesky(gram)
    table = np.linalg.solve(factor.T, np.linalg.solve(factor, design.T))
    return jnp.asarray(table.astype(np.float32)).astype(bf16)


def gelu_tanh(values):
    return jax.nn.gelu(values, approximate=True)


def near_scores(q_rows, keys, block):
    reach = keys.shape[0] // 2 + (block + 1) * ROWS
    scores = dot(q_rows, keys[:reach], 1, 1)
    row = lax.broadcasted_iota(jnp.int32, (ROWS, ROWS), 0)
    col = lax.broadcasted_iota(jnp.int32, (ROWS, ROWS), 1)
    edge = jnp.where(col <= row, scores[:, reach - ROWS :], NEG)
    return jnp.concatenate([scores[:, : reach - ROWS], edge], axis=1), reach


def density_parts(scaled, w_mean, w_var):
    basis_count = scaled.shape[1]
    index = lax.broadcasted_iota(jnp.int32, (1, basis_count), 1).astype(f32)
    centers = (index + 0.5) / basis_count
    middle = jax.nn.sigmoid(jnp.sum(scaled * w_mean, axis=1, keepdims=True))
    var_raw = jnp.sum(scaled * w_var, axis=1, keepdims=True)
    softplus = jnp.maximum(var_raw, 0.0) + jnp.log1p(jnp.exp(-jnp.abs(var_raw)))
    variance = VAR_SCALE * softplus + 1.0 / (basis_count * basis_count)
    offset = middle - centers
    inv_var = 1.0 / variance
    square = offset * offset * inv_var
    scale = lax.rsqrt(2.0 * math.pi * variance) / basis_count
    weights = jnp.exp(-0.5 * square) * scale
    return weights, middle, var_raw, inv_var, offset, square


def attn_fwd_kernel(q_ref, k_ref, v_ref, mk_ref, mv_ref, wm_ref, wv_ref, ctx_ref, lse_ref):
    half = lax.broadcasted_iota(jnp.int32, (1, LANES), 1) < HD
    length = q_ref.shape[0]
    keys, values = k_ref[...], v_ref[...]
    mem_keys, mem_values = mk_ref[...], mv_ref[...]
    for block in range(length // ROWS):
        rows = slice(block * ROWS, (block + 1) * ROWS)
        q_rows = q_ref[rows, :] * jnp.asarray(0.125, bf16)
        outs, sums = [], []
        for head in range(2):
            mine = half if head == 0 else jnp.logical_not(half)
            q_head = jnp.where(mine, q_rows, jnp.zeros_like(q_rows))
            scores, reach = near_scores(q_head, keys, block)
            top = jnp.max(scores, axis=1, keepdims=True)
            raw = jnp.exp(scores - top)
            total = jnp.sum(raw, axis=1, keepdims=True)
            near = dot((raw * (1.0 / total)).astype(bf16), values[:reach], 1, 0)
            sums.append(top + jnp.log(total))
            scaled = dot(q_head, mem_keys, 1, 1)
            weights = density_parts(
                scaled, wm_ref[0, head : head + 1, :], wv_ref[0, head : head + 1, :]
            )[0]
            outs.append(near + dot(weights.astype(bf16), mem_values, 1, 0))
        ctx_ref[rows, :] = jnp.where(half, outs[0], outs[1]).astype(bf16)
        lse_ref[rows, :] = jnp.where(half, sums[0], sums[1])


def attn_bwd_kernel(
    order, rows_own, place_ref,
    q_ref, k_ref, v_ref, mk_ref, mv_ref, wm_ref, wv_ref, lse_ref, do_ref, ctx_ref, far_turned_ref, far_branch_ref,
    dq_ref, dk_ref, dv_ref, maps_ref, send_ref, keep_ref, acck_ref, accv_ref, turned_ref, branch_ref, sems, rides,
):
    fetches = (
        pltpu.make_async_copy(far_turned_ref, turned_ref, sems.at[0]),
        pltpu.make_async_copy(far_branch_ref, branch_ref, sems.at[1]),
    )

    @pl.when(pl.program_id(0) == 0)
    def _():
        for fetch in fetches:
            fetch.start()
        for ride in rides:
            ride.fetch()

    @pl.when(pl.program_id(0) == 1)
    def _():
        for ride in rides:
            ride.add()

    half = lax.broadcasted_iota(jnp.int32, (1, LANES), 1) < HD
    length = q_ref.shape[0]
    near_rows = k_ref.shape[0]
    keys, values = k_ref[...], v_ref[...]
    mem_keys, mem_values = mk_ref[...], mv_ref[...]
    for block in reversed(range(length // ROWS)):
        rows = slice(block * ROWS, (block + 1) * ROWS)
        q_full, do_full = q_ref[rows, :], do_ref[rows, :]
        q_rows = q_full * jnp.asarray(0.125, bf16)
        q_turn, do_turn = q_full.T, do_full.T
        outs = []
        for head in range(2):
            part = slice(head * HD, (head + 1) * HD)
            mine = half if head == 0 else jnp.logical_not(half)
            q_head = jnp.where(mine, q_rows, jnp.zeros_like(q_rows))
            do_head = jnp.where(mine, do_full, jnp.zeros_like(do_full))
            scores, reach = near_scores(q_head, keys, block)
            probs = jnp.exp(scores - lse_ref[rows, head * HD : head * HD + 1])
            grad_probs = dot(do_head, values[:reach], 1, 1)
            inner = jnp.sum(probs * grad_probs, axis=1, keepdims=True)
            grad_raw = (0.125 * probs * (grad_probs - inner)).astype(bf16)
            probs_low = probs.astype(bf16)
            dk_part = dot(q_turn[part], grad_raw, 1, 0)
            dv_part = dot(do_turn[part], probs_low, 1, 0)
            out = dot(grad_raw, keys[:reach], 1, 0)
            w_mean, w_var = wm_ref[0, head : head + 1, :], wv_ref[0, head : head + 1, :]
            scaled = dot(q_head, mem_keys, 1, 1)
            weights, middle, var_raw, inv_var, offset, square = density_parts(scaled, w_mean, w_var)
            grad_w = dot(do_head, mem_values, 1, 1) * weights
            d_mid = -jnp.sum(grad_w * offset, axis=1, keepdims=True) * inv_var
            d_var = jnp.sum(grad_w * (square - 1.0), axis=1, keepdims=True) * (0.5 * inv_var)
            d_mid = d_mid * middle * (1.0 - middle)
            d_var = d_var * VAR_SCALE * jax.nn.sigmoid(var_raw)
            gm_part = jnp.sum(scaled * d_mid, axis=0, keepdims=True)
            gv_part = jnp.sum(scaled * d_var, axis=0, keepdims=True)
            grad_mem = (0.125 * (d_mid * w_mean + d_var * w_var)).astype(bf16)
            outs.append(out + dot(grad_mem, mem_keys, 1, 0))
            dmk_part = dot(q_turn[part], grad_mem, 1, 0)
            dmv_part = dot(do_turn[part], weights.astype(bf16), 1, 0)
            if block == length // ROWS - 1:
                acck_ref[part, :near_rows] = dk_part
                accv_ref[part, :near_rows] = dv_part
                acck_ref[part, near_rows:] = dmk_part
                accv_ref[part, near_rows:] = dmv_part
                maps_ref[0, head : head + 1, :] = gm_part
                maps_ref[0, 2 + head : 3 + head, :] = gv_part
            else:
                acck_ref[part, :reach] += dk_part
                accv_ref[part, :reach] += dv_part
                acck_ref[part, near_rows:] += dmk_part
                accv_ref[part, near_rows:] += dmv_part
                maps_ref[0, head : head + 1, :] += gm_part
                maps_ref[0, 2 + head : 3 + head, :] += gv_part
        dq_ref[rows, :] = jnp.where(half, outs[0], outs[1]).astype(bf16)
    dk_ref[...] = acck_ref[...].T.astype(bf16)
    dv_ref[...] = accv_ref[...].T.astype(bf16)

    @pl.when(pl.program_id(0) == 0)
    def _():
        for fetch in fetches:
            fetch.wait()

    turned = turned_ref[...]
    grads = (
        dot(turned[:, length : 2 * length], dq_ref[...], 1, 0),
        dot(turned, dk_ref[...], 1, 0),
        dot(turned, dv_ref[...], 1, 0),
        dot(branch_ref[...], ctx_ref[...], 1, 0),
    )
    for at, grad in enumerate(grads):
        send, keep = cut_core(grad, place_ref[0], rows_own, order)
        send_ref[:, at], keep_ref[:, at] = send.astype(bf16), keep

    @pl.when(pl.program_id(0) == pl.num_programs(0) - 1)
    def _():
        for ride in rides:
            ride.done()


class Ride:
    def __init__(self, cut, bit, ins, outs, scratch):
        keep, came = ins
        width = keep.shape[-1] // 2

        def half(ref, b):
            return ref.at[:, :, pl.ds(pl.multiple_of(b * width, LANES), width)] if cut == "h" else ref.at[b]

        self.far, self.near, sems = scratch[:2], scratch[2:4], scratch[4]
        copy = pltpu.make_async_copy
        self.fetches = [
            copy(half(keep, 1 - bit), scratch[0], sems.at[0]),
            copy(half(came, 1 - bit), scratch[1], sems.at[1]),
            copy(half(keep, bit), scratch[2], sems.at[2]),
            copy(half(came, bit), scratch[3], sems.at[3]),
        ]
        self.writes = [copy(scratch[1], outs[0], sems.at[4]), copy(scratch[2], outs[1], sems.at[5])]

    def fetch(self):
        for one in self.fetches:
            one.start()

    def add(self):
        for one in self.fetches:
            one.wait()
        keep, came = self.far
        came[...] = (keep[...] + came[...].astype(f32)).astype(bf16)
        keep, came = self.near
        keep[...] = keep[...] + came[...].astype(f32)
        for one in self.writes:
            one.start()

    def done(self):
        for one in self.writes:
            one.wait()


def attn_specs(length, basis_count, place):
    near_rows = 2 * length
    near = pl.BlockSpec((near_rows, LANES), lambda p, *_: (0, place(p)))
    far = pl.BlockSpec((basis_count, LANES), lambda p, *_: (near_rows // basis_count, place(p)))
    maps = pl.BlockSpec((1, 2, basis_count), lambda p, *_: (place(p), 0, 0))
    return [pl.BlockSpec((length, LANES), lambda p, *_: (0, place(p))), near, near, far, far, maps, maps]


def attn_forward(queries, keys, values, w_mean, w_var):
    length, width = queries.shape
    basis_count = w_mean.shape[-1]
    pairs = width // LANES
    return call(
        attn_fwd_kernel, "attn_forward", (pairs,),
        attn_specs(length, basis_count, lambda p: p),
        [
            (pl.BlockSpec((length, LANES), lambda p: (0, p)), struct(bf16, length, width)),
            (pl.BlockSpec((length, LANES), lambda p: (0, p)), struct(f32, length, width)),
        ],
        scalars=0,
    )(queries, keys, values, keys, values, w_mean, w_var)


def attn_backward(
    place, queries, keys, values, w_mean, w_var, lse, grad_ctx, context, turned, branch, group, groups, order, rows,
    span, into, riders,
):
    length, width = queries.shape
    basis_count = w_mean.shape[-1]
    pairs = width // LANES
    count = pairs // groups
    where = lambda p: p * groups + group
    all_rows = keys.shape[0]
    ours = lambda size: pl.BlockSpec((size, LANES), lambda p, _: (0, where(p)))
    cut = (len(order), 4, rows)
    mine = pl.BlockSpec(cut + (LANES,), lambda p, _: (0, 0, 0, p * len(span) + group - span[0]))
    specs = attn_specs(length, basis_count, where) + [ours(length)] * 3
    specs += [pl.BlockSpec(memory_space=pl.ANY)] * 2
    held = [pl.BlockSpec(memory_space=pl.ANY)] * len(into)

    others = Riders(riders)
    outs = [
        (ours(length), struct(bf16, length, width)),
        (ours(all_rows), struct(bf16, all_rows, width)),
        (ours(all_rows), struct(bf16, all_rows, width)),
        (pl.BlockSpec((1, 4, basis_count), lambda p, _: (where(p), 0, 0)), struct(f32, pairs, 4, basis_count)),
        (mine, struct(bf16, *cut, count * LANES * len(span))),
        (mine, struct(f32, *cut, count * LANES * len(span))),
    ]
    scratch = [
        pltpu.VMEM((LANES, all_rows), f32),
        pltpu.VMEM((LANES, all_rows), f32),
        pltpu.VMEM(turned.shape, bf16),
        pltpu.VMEM(branch.shape, bf16),
        pltpu.SemaphoreType.DMA((2,)),
    ]
    own = (1 + len(specs), len(outs), len(scratch))

    def kernel(*refs):
        first = own[0] + len(into)
        out = first + len(others.arrays)
        room = out + own[1] + len(others.outs)
        rides = others.going(refs[0], refs[first:out], refs[out + own[1] : room], refs[room + own[2] :])
        attn_bwd_kernel(order, rows, *refs[: own[0]], *refs[out : out + own[1]], *refs[room : room + own[2]], rides)

    results = call(
        kernel, "attn_backward", (count,),
        specs + held + others.specs,
        outs + others.outs,
        scratch=scratch + others.scratch,
        vmem=40 if riders else 24,
        aliases={own[0] + i: i for i in range(len(into))},
        near=tuple(range(own[0], own[0] + len(into))),
    )(
        place, queries, keys, values, keys, values, w_mean, w_var, lse, grad_ctx, context, turned, branch, *into,
        *others.arrays,
    )
    for i, rider in enumerate(riders):
        rider.rode(*results[own[1] + 2 * i : own[1] + 2 * i + 2])
    return results[: own[1]]


def turn_over_kernel(rows_ref, turned_ref):
    turned_ref[...] = rows_ref[...].T


def turn_over(rows):
    size, width = rows.shape
    return call(
        turn_over_kernel, "turn_over", (size // ROWS,),
        [pl.BlockSpec((ROWS, width), lambda s: (s, 0))],
        [(pl.BlockSpec((width, ROWS), lambda s: (0, s)), struct(bf16, width, size))],
        scalars=0,
    )(rows)[0]


def norm_stats(values):
    centred = values - jnp.mean(values, axis=-1, keepdims=True)
    spread = jnp.mean(centred * centred, axis=-1, keepdims=True)
    inverse = lax.rsqrt(spread + EPSILON)
    return centred * inverse, inverse


def norm_back(grad, hat, inverse, gain):
    scaled = grad * gain
    inner = jnp.mean(scaled * hat, axis=-1, keepdims=True)
    return inverse * (scaled - jnp.mean(scaled, axis=-1, keepdims=True) - hat * inner)


def side_block(ref):
    chips, cores, _, rows, cols = ref.shape
    return ref[...].reshape(chips * cores * rows, cols)


def block_order(bits):
    chips = []
    for place in range(1 << len(bits)):
        chip = 0
        for at, bit in enumerate(reversed(bits)):
            chip |= ((place >> at) & 1) << (bit - 1)
        chips.append(chip)
    return chips


def cut_core(value, core, rows, order):
    split = value.reshape(value.shape[0] // (2 * rows), 2, rows, value.shape[1])
    low = jnp.stack([split[chip, 0] for chip in order])
    high = jnp.stack([split[chip, 1] for chip in order])
    return jnp.where(core == 0, high, low), jnp.where(core == 0, low, high)


def mix_kernel(ctx_ref, tokens_ref, w0_ref, w1_ref, gain_ref, hidden_ref, normed_ref):
    side = w0_ref.shape[4]
    ctx = ctx_ref[...]
    mixed = dot(ctx[:, :side], side_block(w0_ref), 1, 1)
    mixed = mixed + dot(ctx[:, side:], side_block(w1_ref), 1, 1)
    hidden = tokens_ref[...].astype(f32) + mixed
    hidden_ref[...] = hidden
    normed_ref[...] = (norm_stats(hidden)[0] * gain_ref[...]).astype(bf16)


def feed_kernel(
    order, place_ref, normed_ref, normed2_ref, cot_ref, cot2_ref, up_ref, down_ref,
    mlp_ref, mlp2_ref, gn_ref, gn2_ref, down_send_ref, down_keep_ref, up_send_ref, up_keep_ref,
    nt_ref, ct_ref, act_ref, pre_ref, acc_ref,
):
    step = pl.program_id(0)
    length, width = normed_ref.shape
    block = up_ref.shape[1] * up_ref.shape[3]
    w_up, w_down = side_block(up_ref), side_block(down_ref)
    slope = math.sqrt(2.0 / math.pi)

    @pl.when(step == 0)
    def _():
        nt_ref[:, :length] = normed_ref[...].T
        nt_ref[:, length:] = normed2_ref[...].T
        ct_ref[:, :length] = cot_ref[...].T
        ct_ref[:, length:] = cot2_ref[...].T

    for half in range(2):
        rows = slice(half * length, (half + 1) * length)
        normed = (normed_ref, normed2_ref)[half][...]
        cot = (cot_ref, cot2_ref)[half][...]
        pre = dot(normed, w_up, 1, 0)
        square = pre * pre
        bend = jnp.tanh(slope * pre * (1.0 + 0.044715 * square))
        lift = 0.5 + 0.5 * bend
        act = (pre * lift).astype(bf16)
        rise = lift + 0.5 * pre * (1.0 - bend * bend) * (slope + (3.0 * 0.044715 * slope) * square)
        grad_pre = (dot(cot, w_down, 1, 0) * rise).astype(bf16)
        act_ref[rows, :] = act
        pre_ref[rows, :] = grad_pre
        mlp = dot(act, w_down, 1, 1)
        grad_normed = dot(grad_pre, w_up, 1, 1)

        @pl.when(step == 0)
        def _():
            acc_ref[2 * half] = mlp
            acc_ref[2 * half + 1] = grad_normed

        @pl.when(step == 1)
        def _():
            if half == 0:
                mlp_ref[...] = acc_ref[0] + mlp
                gn_ref[...] = acc_ref[1] + grad_normed
            else:
                mlp2_ref[...] = (acc_ref[2] + mlp).astype(bf16)
                gn2_ref[...] = (acc_ref[3] + grad_normed).astype(bf16)

    g_down = dot(ct_ref[...], act_ref[...], 1, 0).reshape(width // block, block, -1)
    g_down = jnp.stack([g_down[chip] for chip in order])

    @pl.when(step == 0)
    def _():
        down_send_ref[...] = g_down.astype(bf16)

    @pl.when(step == 1)
    def _():
        down_keep_ref[...] = g_down

    g_up = dot(nt_ref[...], pre_ref[...], 1, 0).reshape(width // block, block, -1)
    low = jnp.stack([g_up[chip] for chip in order[: len(order) // 2]])
    high = jnp.stack([g_up[chip] for chip in order[len(order) // 2 :]])
    first = place_ref[1] == 0
    up_send_ref[...] = jnp.where(first, high, low).astype(bf16)
    up_keep_ref[...] = jnp.where(first, low, high)


def turn_kernel(
    hidden_ref, gn_ref, gn2_ref, mlp_ref, mlp2_ref, cot_ref, w0_ref, w1_ref, gain_ref,
    gh_ref, gain_grad_ref, gc_ref, out_ref, branch_ref,
):
    step = pl.program_id(0)
    side = w0_ref.shape[4]
    hidden = hidden_ref[...]
    hat, inverse = norm_stats(hidden)
    grad = gn_ref[...] + gn2_ref[...].astype(f32)
    out_ref[...] = (hidden + (mlp_ref[...] + mlp2_ref[...].astype(f32))).astype(bf16)
    grad_hidden = cot_ref[...].astype(f32) + norm_back(grad, hat, inverse, gain_ref[...])
    gh_ref[...] = grad_hidden
    branch = grad_hidden.astype(bf16)
    branch_ref[...] = branch.T
    gc_ref[:, :side] = dot(branch, side_block(w0_ref), 1, 0).astype(bf16)
    gc_ref[:, side:] = dot(branch, side_block(w1_ref), 1, 0).astype(bf16)

    @pl.when(step == 0)
    def _():
        gain_grad_ref[...] = jnp.zeros_like(gain_grad_ref)

    gain_grad_ref[...] += jnp.sum(grad * hat, axis=0, keepdims=True)


def finish_kernel(
    blocks, rides, dq_ref, dk_ref, dv_ref, wq_ref, wk_ref, wv_ref, ridge_ref, basis_ref, earlier_ref, tokens_ref, gh_ref,
    gain_ref, gain_m_ref, maps_ref, here_ref, gt_ref, gc_ref, small_ref, fit_ref, grad_ref,
):
    step = pl.program_id(0)
    length = ridge_ref.shape[1] // 2

    @pl.when(step == 0)
    def _():
        for ride in rides:
            ride.fetch()

    @pl.when(step == blocks + 1)
    def _():
        for ride in rides:
            ride.add()

    part = dot(dk_ref[...], wk_ref[...], 1, 1) + dot(dv_ref[...], wv_ref[...], 1, 1)

    @pl.when(step == 0)
    def _():
        memory = part.astype(bf16)
        samples = dot(ridge_ref[:, :length], memory, 0, 0).astype(bf16)
        gc_ref[...] = here_ref[0] * dot(basis_ref[...], samples, 0, 0)
        fit_ref[...] = dot(ridge_ref[:, length:], memory, 0, 0)
        grad_ref[...] = jnp.zeros_like(grad_ref)

    @pl.when(jnp.logical_and(step > 0, step <= blocks))
    def _():
        past = part + fit_ref[pl.ds(pl.multiple_of((step - 1) * ROWS, ROWS), ROWS), :]
        hat = norm_stats(earlier_ref[...].astype(f32))[0]
        grad_ref[...] += jnp.sum(past * hat, axis=0, keepdims=True)

    @pl.when(step > blocks)
    def _():
        grad = part + dot(dq_ref[...], wq_ref[...], 1, 1)
        hat, inverse = norm_stats(tokens_ref[...].astype(f32))
        grad_ref[...] += jnp.sum(grad * hat, axis=0, keepdims=True)
        gt_ref[...] = gh_ref[...] + norm_back(grad, hat, inverse, gain_ref[...])

    @pl.when(step == 2 * blocks)
    def _():
        small_ref[...] = jnp.zeros_like(small_ref)
        pairs, _, basis_count = maps_ref.shape
        for p in range(pairs):
            small_ref[2 * p : 2 * p + 2, :] = maps_ref[p, 0:2, :]
            small_ref[2 * (pairs + p) : 2 * (pairs + p) + 2, :] = maps_ref[p, 2:4, :]
        for at in range(grad_ref.shape[1] // basis_count):
            cols = slice(at * basis_count, (at + 1) * basis_count)
            row = 4 * pairs + 2 * at
            small_ref[row : row + 1, :] = grad_ref[:, cols]
            small_ref[row + 1 : row + 2, :] = gain_m_ref[:, cols]
        for ride in rides:
            ride.done()


def whole_spec(*shape):
    return pl.BlockSpec(shape, lambda *_: (0,) * len(shape))


def struct(kind, *shape):
    return jax.ShapeDtypeStruct(shape, kind)


def call(kernel, name, grid, in_specs, outs, scratch=(), scalars=1, vmem=24, aliases={}, near=(), near_outs=()):
    def place_of(at, out):
        return out if math.prod(out.shape) <= 1 << 16 or at in near_outs else pltpu.HBM(out.shape, out.dtype)

    run = pl.pallas_call(
        kernel,
        grid_spec=pltpu.PrefetchScalarGridSpec(
            num_scalar_prefetch=scalars,
            grid=grid,
            in_specs=in_specs,
            out_specs=[whole_spec(*out.shape) if spec is None else spec for spec, out in outs],
            scratch_shapes=scratch,
        ),
        out_shape=[place_of(at, out) for at, (_, out) in enumerate(outs)],
        input_output_aliases=aliases,
        compiler_params=pltpu.CompilerParams(vmem_limit_bytes=vmem << 20),
        cost_estimate=pl.CostEstimate(flops=0, bytes_accessed=1 << 20, transcendentals=0),
        name=name,
    )

    def put(at, x):
        return x if x.size <= 1 << 16 or at in near else pltpu.with_memory_space_constraint(x, pltpu.HBM)

    return lambda *args: run(*(put(at, x) for at, x in enumerate(args)))


def row_spec(width):
    return pl.BlockSpec((ROWS, width), lambda s, *_: (s, 0))


def mix(context, tokens, rest, gain, side):
    length, width = tokens.shape
    some = row_spec(width)
    return call(
        mix_kernel, "mix", (length // ROWS,),
        [some, some] + out_weights(rest, side) + [whole_spec(1, width)],
        [(some, struct(f32, length, width)), (some, struct(bf16, length, width))],
        scalars=0,
        near_outs=(1,),
    )(context, tokens, rest, rest, gain)


def out_weights(rest, side):
    chips, cores, _, rows, wide = rest.shape
    last = wide // side - 1
    return [
        pl.BlockSpec((chips, cores, 1, rows, side), lambda *_, h=h: (0, 0, h, 0, last)) for h in range(2)
    ]


def feed(place, normed, normed2, cot, cot2, rest, tile, order):
    length, width = normed.shape
    chips, cores, _, rows, _ = rest.shape
    block = cores * rows
    big = whole_spec(length, width)

    def weights(at):
        return pl.BlockSpec(
            (chips, cores, 1, rows, tile), lambda s, p: (0, 0, (s + 1 + p[2]) % 2, 0, at + p[0])
        )

    half = (chips // 2, block, 2 * tile)
    turned = pl.BlockSpec((chips // 2, block, tile), lambda s, p: (0, 0, (s + 1 + p[2]) % 2))
    return call(
        lambda *refs: feed_kernel(order, *refs), "feed", (2,),
        [big, big, big, big, weights(0), weights(2)],
        [
            (None, struct(f32, length, width)),
            (None, struct(bf16, length, width)),
            (None, struct(f32, length, width)),
            (None, struct(bf16, length, width)),
            (None, struct(bf16, chips, block, tile)),
            (None, struct(f32, chips, block, tile)),
            (turned, struct(bf16, *half)),
            (turned, struct(f32, *half)),
        ],
        scratch=[
            pltpu.VMEM((width, 2 * length), bf16),
            pltpu.VMEM((width, 2 * length), bf16),
            pltpu.VMEM((2 * length, tile), bf16),
            pltpu.VMEM((2 * length, tile), bf16),
            pltpu.VMEM((4, length, width), f32),
        ],
        vmem=44,
        near=(1, 2, 4),
        near_outs=(0, 1, 2, 3),
    )(place, normed, normed2, cot, cot2, rest, rest)


def turn(hidden, gn, gn2, mlp, mlp2, cot, rest, gain, side):
    length, width = hidden.shape
    some = row_spec(width)
    return call(
        turn_kernel, "turn", (length // ROWS,),
        [some] * 6 + out_weights(rest, side) + [whole_spec(1, width)],
        [
            (some, struct(f32, length, width)),
            (None, struct(f32, 1, width)),
            (some, struct(bf16, length, width)),
            (some, struct(bf16, length, width)),
            (pl.BlockSpec((width, ROWS), lambda s: (0, s)), struct(bf16, width, length)),
        ],
        scalars=0,
        near=(1, 2, 3, 4),
    )(hidden, gn, gn2, mlp, mlp2, cot, rest, rest, gain)


def finish(
    place, dq, dk, dv, weights, ridge, basis, earlier, tokens, grad_hidden, gain, gain_m_grad, maps, here, riders
):
    length, width = tokens.shape
    basis_count = ridge.shape[0]
    blocks = length // ROWS
    small = 4 * maps.shape[0] + 2 * (width // basis_count)
    all_rows = pl.BlockSpec((ROWS, width), lambda s, _: (jnp.where(s == 0, 2 * blocks, s - 1), 0))
    past = pl.BlockSpec((ROWS, width), lambda s, _: (jnp.clip(s - 1, 0, blocks - 1), 0))
    now = pl.BlockSpec((ROWS, width), lambda s, _: (jnp.maximum(s - 1 - blocks, 0), 0))
    args = (gain, gain_m_grad, maps)
    others = Riders(riders)
    outs = [
        (now, struct(f32, length, width)),
        (None, struct(f32, basis_count, width)),
        (None, struct(f32, small + (-small) % 8, basis_count)),
    ]
    scratch = [pltpu.VMEM((length, width), f32), pltpu.VMEM((1, width), f32)]
    ins = 3 + len(weights) + 2 + 3 + 3 + 1

    def kernel(place_ref, *refs):
        out = ins + len(others.arrays)
        room = out + 3 + len(others.outs)
        rides = others.going(place_ref, refs[ins:out], refs[out + 3 : room], refs[room + 2 :])
        finish_kernel(blocks, rides, *refs[:ins], *refs[out : out + 3], *refs[room : room + 2])

    results = call(
        kernel, "finish", (2 * blocks + 1,),
        [now, all_rows, all_rows]
        + [whole_spec(*x.shape) for x in (*weights, ridge, basis)]
        + [past, now, now]
        + [whole_spec(*x.shape) for x in args]
        + [pl.BlockSpec(memory_space=pltpu.SMEM)]
        + others.specs,
        outs + others.outs,
        scratch=scratch + others.scratch,
        vmem=40,
    )(place, dq, dk, dv, *weights, ridge, basis, earlier, tokens, grad_hidden, *args, here, *others.arrays)
    for i, rider in enumerate(riders):
        rider.rode(*results[3 + 2 * i : 5 + 2 * i])
    return results[:3]


class Links:
    def __init__(self, sizes):
        self.chips = sizes["chips"]
        self.bits = self.chips.bit_length()
        self.chip = lax.axis_index("chips")
        self.core = lax.axis_index("core")
        self.side = lax.axis_index("heads")
        self.places = [0, 1, "h", 2]

    def swap(self, value, stage):
        if stage in ("h", 0):
            return lax.ppermute(value, "heads" if stage == "h" else "core", [(0, 1), (1, 0)])
        mask = 1 << (stage - 1)
        return lax.ppermute(value, "chips", [(i, i ^ mask) for i in range(self.chips)])

    def bit(self, stage):
        if stage == "h":
            return self.side
        return self.core if stage == 0 else (self.chip >> (stage - 1)) & 1

    def gather(self, value, lead, stages, have=()):
        have = list(have)
        for stage in stages:
            other = self.swap(value, stage)
            if stage == "h":
                value = self.gather_with(value, other, stage, None)
            else:
                place = lead + sum(1 for b in have if b > stage)
                value = self.gather_with(value, other, stage, place)
                have.append(stage)
        return value

    def gather_with(self, value, other, stage, axis=0):
        mine_first = self.bit(stage) == 0
        first = jnp.where(mine_first, value, other)
        second = jnp.where(mine_first, other, value)
        if axis is None:
            return jnp.concatenate([first, second], axis=-1)
        return jnp.stack([first, second], axis=axis)

    def whole_rows(self, value, rows):
        value = value.reshape(2, rows, -1)
        mine = lax.dynamic_index_in_dim(value, self.core, 0, keepdims=False)
        other = self.swap(lax.dynamic_index_in_dim(value, 1 - self.core, 0, keepdims=False), 0)
        return self.gather_with(mine, other, 0, None)


def tie(value, *earlier):
    return lax.optimization_barrier((value,) + earlier)[0]


class Chain:
    def __init__(self, links, stages, send, keep, wire=bf16):
        self.links, self.wire = links, wire
        self.stage, self.stages = stages[0], list(stages[1:])
        self.left = [stage for stage in self.stages if stage != "h"]
        self.send, self.keep = self.spread(send), self.spread(keep)

    def spread(self, value):
        return value.reshape((2,) * len(self.left) + value.shape[1:])

    def cut(self):
        keep, came = self.keep, self.came
        self.stage = self.stages.pop(0) if self.stages else None
        if self.stage is None:
            self.value = keep + came.astype(f32)
            return
        bit = self.links.bit(self.stage)
        if self.stage == "h":
            width = keep.shape[-1] // 2
            take = lambda x, b: lax.dynamic_slice_in_dim(x, b * width, width, axis=x.ndim - 1)
        else:
            axis = self.left.index(self.stage)
            self.left.pop(axis)
            take = lambda x, b: lax.dynamic_index_in_dim(x, b, axis, keepdims=False)
        self.send = (take(keep, 1 - bit) + take(came, 1 - bit).astype(f32)).astype(self.wire)
        self.keep = take(keep, bit) + take(came, bit).astype(f32)

    def ride(self):
        self.stage = self.stages.pop(0)
        at = self.links.places.index(self.stage)
        tail = self.keep.shape[len(self.left) :]
        rows, cols = math.prod(tail[:-1]), tail[-1]
        if self.stage == "h":
            whole = (self.keep.size // (rows * cols), rows, cols)
            half = whole[:2] + (cols // 2,)
        else:
            self.left.pop(self.left.index(self.stage))
            whole = (2, self.keep.size // (2 * rows * cols), rows, cols)
            half = whole[1:]
        self.tail = tail[:-1] + half[-1:]
        return self.stage, at, [self.keep.reshape(whole), self.came.reshape(whole)], half

    def rode(self, send, keep):
        shape = (2,) * len(self.left) + self.tail
        self.send, self.keep = send.reshape(shape), keep.reshape(shape)


def together(values):
    return list(lax.optimization_barrier(tuple(values)))


class Riders:
    def __init__(self, chains):
        self.rides = [chain.ride() for chain in chains]
        anywhere = pl.BlockSpec(memory_space=pl.ANY)
        self.arrays = [x for _, _, arrays, _ in self.rides for x in arrays]
        self.specs = [anywhere] * len(self.arrays)
        self.outs, self.scratch = [], []
        for _, _, _, shape in self.rides:
            self.outs += [(anywhere, struct(bf16, *shape)), (anywhere, struct(f32, *shape))]
            self.scratch += [pltpu.VMEM(shape, kind) for kind in (f32, bf16, f32, bf16)]
            self.scratch += [pltpu.SemaphoreType.DMA((6,))]

    def going(self, place_ref, ins, outs, scratch):
        return [
            Ride(how, place_ref[at], ins[2 * i : 2 * i + 2], outs[2 * i : 2 * i + 2], scratch[5 * i : 5 * i + 5])
            for i, (how, at, _, _) in enumerate(self.rides)
        ]


def hold(chains, *after):
    came = together([chain.came for chain in chains] + list(after))
    for chain, value in zip(chains, came):
        chain.came = value


def start(chains):
    chains = [chain for chain in chains if chain.stage is not None]
    if chains:
        for chain, send in zip(chains, together([chain.send for chain in chains])):
            chain.send = send
            chain.came = chain.links.swap(send, chain.stage)


def arrive(chains, *after):
    chains = [chain for chain in chains if chain.stage is not None]
    if chains:
        came = together([chain.came for chain in chains] + list(after))
        for chain, value in zip(chains, came):
            chain.came = value
            chain.cut()


def shards(
    tokens, earlier, coeffs, present, sample_at, w_qkv, w_out, w_up, w_down,
    gain_attn, gain_mlp, w_mean, w_var, cotangent, sizes, groups,
):
    links = Links(sizes)
    high = list(range(2, links.bits))
    count = 2 * links.chips
    tokens, earlier, coeffs, cotangent = tokens[0], earlier[0], coeffs[0], cotangent[0]
    length, width = tokens.shape
    basis_count = coeffs.shape[0]
    rows, side = w_qkv.shape[1], w_qkv.shape[2]
    ff_side = w_up.shape[1]
    local_heads, mem_part = w_mean.shape

    rest = jnp.concatenate([w_up, w_down.T, w_out.T], axis=1).astype(bf16)
    rest = lax.all_gather(rest, ("chips", "core", "heads"), axis=0, tiled=False)
    rest = rest.reshape(links.chips, 2, 2, rows, -1)
    tile = ff_side // 2
    small = jnp.concatenate(
        [gain_attn, gain_mlp, w_mean.reshape(-1), w_var.reshape(-1)]
    ).astype(bf16)
    small_size = small.shape[0]
    small = jnp.pad(small, (0, -small_size % LANES)).reshape(1, -1)
    small_h = links.swap(small, "h")
    first = jnp.where(links.side == 0, small, small_h)
    second = jnp.where(links.side == 0, small_h, small)
    far = high[1:][::-1]
    parts = links.gather(w_qkv.astype(bf16), 1, far)
    small = links.gather(jnp.concatenate([first, second], axis=0), 0, far)
    small, parts = together([small, parts])
    turns = ([2, 1, "h"], [1, "h", 2], ["h", 2, 1])
    parts = [parts[c] for c in range(3)]
    have = list(far)
    haves = [list(far) for _ in range(3)]
    for step in range(3):
        small = links.gather(small, 0, [2 - step], have)
        have.append(2 - step)
        for c in range(3):
            parts[c] = links.gather(parts[c], 0, [turns[c][step]], haves[c])
            if turns[c][step] != "h":
                haves[c].append(turns[c][step])
        if step < 2:
            small, *parts = together([small] + parts)
    qkv_full = [links.gather(parts[c], 0, [0], haves[c]).reshape(width, width) for c in range(3)]
    small = small.reshape(count, 2, -1).astype(f32)
    gain_a = small[:, 0, :rows].reshape(-1)
    gain_m = small[:, 0, rows : 2 * rows].reshape(-1)

    def head_map(start):
        part = small[:, :, start : start + local_heads * mem_part]
        part = part.reshape(count, 2, local_heads, mem_part).transpose(1, 2, 0, 3)
        return part.reshape(local_heads, 2, basis_count)

    mean_full = head_map(2 * rows)
    var_full = head_map(2 * rows + local_heads * mem_part)

    cot2 = links.swap(cotangent, 0)
    place = jnp.stack([links.bit(stage) for stage in links.places]).astype(jnp.int32)

    ridge = ridge_table(basis_count, 2 * length)
    tokens32, earlier32 = tokens.astype(f32), earlier.astype(f32)
    normed = layer_norm(tokens32, gain_a).astype(bf16)
    past = layer_norm(earlier32, gain_a).astype(bf16)
    old_basis = basis_at((sample_at[0].astype(f32) + 0.5) / GRID, basis_count).astype(bf16)
    here = present[0].astype(f32)
    samples = (here * dot(old_basis, coeffs.astype(bf16), 1, 0)).astype(bf16)
    memory = dot(ridge, jnp.concatenate([samples, past], axis=0), 1, 0).astype(bf16)
    sources = jnp.concatenate([past, normed, memory], axis=0)
    queries = dot(normed, qkv_full[0], 1, 0).astype(bf16)
    keys = dot(sources, qkv_full[1], 1, 0).astype(bf16)
    values = dot(sources, qkv_full[2], 1, 0).astype(bf16)
    context, lse = attn_forward(queries, keys, values, mean_full, var_full)
    context, turned, old_basis = together([context, turn_over(sources), old_basis])
    gain_row = gain_m.reshape(1, -1)
    hidden, normed_mlp = mix(context, tokens, rest, gain_row, side)
    normed_mlp2 = links.swap(normed_mlp, 0)
    lows = [2] + high[1:]
    order = block_order([1] + lows)
    mlp, mlp2, gn, gn2, down_send, down_keep, up_send, up_keep = feed(
        place, normed_mlp, normed_mlp2, cotangent, cot2, rest, tile, order
    )
    gn2 = links.swap(gn2, 0)
    mlp2 = links.swap(mlp2, 0)
    c_down = Chain(links, ["h", 1] + lows, down_send, down_keep)
    c_up = Chain(links, [1, 2] + high[1:] + ["h"], up_send, up_keep)
    start([c_down, c_up])
    grad_hidden, gain_m_grad, grad_ctx, output, branch = turn(
        hidden, gn, gn2, mlp, mlp2, cotangent, rest, gain_row, side
    )

    plans = (["h", 1, 2], [1, 2, "h"])
    spans = [list(range(groups - 1)), [groups - 1]]
    feeds, c_qkv = [c_down, c_up], []
    into = ()
    for group in range(groups):
        late = group == groups - 1
        plan = plans[late] + high[1:]
        if late:
            into = into[:4]
        riders = c_qkv if late else feeds if group == 1 else []
        if riders:
            hold(riders, into[0])
        into = attn_backward(
            place, queries, keys, values, mean_full, var_full, lse, grad_ctx, context, turned, branch, group, groups,
            block_order([b for b in plan if b != "h"]), rows, spans[late], into, riders,
        )
        if group == spans[late][-1]:
            c_qkv = c_qkv + [Chain(links, [0] + plan, into[4], into[5])]
        sends = [c.send for c in riders]
        if not late:
            start(riders)
            if c_qkv:
                c_qkv[0].send = tie(c_qkv[0].send, *sends)
                start(c_qkv)
                sends = [c_qkv[0].send]
        grad_ctx = tie(grad_ctx, into[0], *sends)
    arrive(feeds, into[0])
    chains = feeds + c_qkv
    last = chains[-1]
    last.send = tie(last.send, *[c.send for c in feeds])
    start([last])
    start(chains[:-1])
    arrive([last])
    start([last])
    dq, dk, dv, maps = into[:4]
    dq = tie(dq, *[c.send for c in chains])
    grad_tokens, grad_coeffs, tiny = finish(
        place, dq, dk, dv, qkv_full, ridge, old_basis, earlier, tokens, grad_hidden, gain_a.reshape(1, -1),
        gain_m_grad, maps, here.reshape(1), [],
    )

    def add(value, stage):
        return value + links.swap(value, stage)

    tiny_stages = [["h", 1]] + [[stage] for stage in lows]
    arrive(chains, tiny)
    tiny = tie(tiny, *[c.send for c in chains])
    tiny = add(tiny, 0)
    while tiny_stages or any(chain.stage is not None for chain in chains):
        going = [c for c in chains if c.stage is not None]
        start(going)
        for stage in tiny_stages.pop(0) if tiny_stages else []:
            tiny = add(tiny, stage)
        *came, tiny = together([c.came for c in going] + [tiny])
        for chain, value in zip(going, came):
            chain.came = value
            chain.cut()
    r_down, r_up = links.whole_rows(c_down.value, rows), links.whole_rows(c_up.value, rows)
    r_proj = jnp.concatenate([chain.value for chain in c_qkv], axis=2)
    heads = 2 * local_heads
    item = 2 * links.chip + links.core
    pick_map = lambda first: lax.dynamic_slice(
        tiny, (first + local_heads * links.side, item * mem_part), (local_heads, mem_part)
    )
    mean_out, var_out = pick_map(0), pick_map(heads)
    gains = tiny[2 * heads : 2 * heads + 2 * (width // basis_count)].reshape(-1, 2, basis_count)
    gain_part = width // (2 * count)
    pick_gain = lambda at: lax.dynamic_slice(
        gains[:, at].reshape(-1), ((2 * item + links.side) * gain_part,), (gain_part,)
    )
    gain_a_out, gain_m_out = pick_gain(0), pick_gain(1)
    return (
        output[None],
        grad_tokens[None],
        grad_coeffs[None],
        r_proj[:3],
        r_proj[3].T,
        r_up,
        r_down.T,
        gain_a_out,
        gain_m_out,
        mean_out,
        var_out,
    )


def solution(mesh):
    sizes = dict(mesh.shape)
    both = ("items", "heads")
    in_specs = (
        P(both, None, None),
        P(both, None, None),
        P(both, None, None),
        P(both),
        P(both, None),
        P(None, "items", "heads"),
        P("heads", "items"),
        P("items", "heads"),
        P("heads", "items"),
        P("items"),
        P("items"),
        P("heads", "items"),
        P("heads", "items"),
        P(both, None, None),
    )
    out_specs = (
        P(both, None, None),
        P(both, None, None),
        P(both, None, None),
        P(None, "items", "heads"),
        P("heads", "items"),
        P("items", "heads"),
        P("heads", "items"),
        P(both),
        P(both),
        P("heads", "items"),
        P("heads", "items"),
    )

    chips = sizes["items"] // 2
    split = Mesh(mesh.devices.reshape(chips, 2, sizes["heads"]), ("chips", "core", "heads"))

    def respec(spec):
        def axis(entry):
            names = entry if isinstance(entry, tuple) else (entry,)
            flat = tuple(n for name in names for n in (("chips", "core") if name == "items" else (name,)))
            return flat if flat != (None,) else None

        return P(*(axis(entry) for entry in spec))

    def body(*args):
        return shards(*args, sizes=dict(split.shape), groups=3)

    return jax.shard_map(
        body,
        mesh=split,
        in_specs=tuple(respec(spec) for spec in in_specs),
        out_specs=tuple(respec(spec) for spec in out_specs),
        check_vma=False,
    )
```

```python
import math

import jax
import jax.numpy as jnp
import numpy as np
from jax import lax
from jax.experimental import pallas as pl
from jax.experimental.pallas import tpu as pltpu
from jax.sharding import Mesh
from jax.sharding import PartitionSpec as P

HD = 64
GRID = 1024
EPSILON = 1e-05
VAR_SCALE = 0.01
RIDGE = 1.0
LANES = 128
ROWS = 256
NEG = -1e30
bf16 = jnp.bfloat16
f32 = jnp.float32


def dot(a, b, ca, cb):
    return lax.dot_general(a, b, (((ca,), (cb,)), ((), ())), preferred_element_type=f32)


def layer_norm(values, gain_vec):
    row_mean = jnp.mean(values, axis=-1, keepdims=True)
    centred = values - row_mean
    spread = jnp.mean(centred * centred, axis=-1, keepdims=True)
    return centred * lax.rsqrt(spread + EPSILON) * gain_vec


def basis_at(points, basis_count):
    centers = (jnp.arange(basis_count, dtype=f32) + 0.5) / basis_count
    offset = points[..., None] - centers
    return jnp.exp(-offset * offset * (0.5 * basis_count * basis_count))


def ridge_table(basis_count, samples):
    points = (np.arange(samples) + 0.5) / samples
    centers = (np.arange(basis_count) + 0.5) / basis_count
    design = np.exp(-((points[:, None] - centers) ** 2) * (0.5 * basis_count * basis_count))
    gram = design.T @ design + RIDGE * np.eye(basis_count)
    factor = np.linalg.cholesky(gram)
    table = np.linalg.solve(factor.T, np.linalg.solve(factor, design.T))
    return jnp.asarray(table.astype(np.float32)).astype(bf16)


def gelu_tanh(values):
    return jax.nn.gelu(values, approximate=True)


def near_scores(q_rows, keys, block):
    reach = keys.shape[0] // 2 + (block + 1) * ROWS
    scores = dot(q_rows, keys[:reach], 1, 1)
    row = lax.broadcasted_iota(jnp.int32, (q_rows.shape[0], ROWS), 0) % ROWS
    col = lax.broadcasted_iota(jnp.int32, (q_rows.shape[0], ROWS), 1)
    edge = jnp.where(col <= row, scores[:, reach - ROWS :], NEG)
    return jnp.concatenate([scores[:, : reach - ROWS], edge], axis=1), reach


def density_parts(scaled, w_mean, w_var):
    basis_count = scaled.shape[1]
    index = lax.broadcasted_iota(jnp.int32, (1, basis_count), 1).astype(f32)
    centers = (index + 0.5) / basis_count
    middle = jax.nn.sigmoid(jnp.sum(scaled * w_mean, axis=1, keepdims=True))
    var_raw = jnp.sum(scaled * w_var, axis=1, keepdims=True)
    softplus = jnp.maximum(var_raw, 0.0) + jnp.log1p(jnp.exp(-jnp.abs(var_raw)))
    variance = VAR_SCALE * softplus + 1.0 / (basis_count * basis_count)
    offset = middle - centers
    inv_var = 1.0 / variance
    square = offset * offset * inv_var
    scale = lax.rsqrt(2.0 * math.pi * variance) / basis_count
    weights = jnp.exp(-0.5 * square) * scale
    return weights, middle, var_raw, inv_var, offset, square


def attn_fwd_kernel(
    q_ref, k_ref, v_ref, mk_ref, mv_ref, wm_ref, wv_ref, rows_ref, ctx_ref, lse_ref, turned_ref
):
    turned_ref[...] = rows_ref[...].T
    half = lax.broadcasted_iota(jnp.int32, (1, LANES), 1) < HD
    length = q_ref.shape[0]
    keys, values = k_ref[...], v_ref[...]
    mem_keys, mem_values = mk_ref[...], mv_ref[...]
    for block in range(length // ROWS):
        rows = slice(block * ROWS, (block + 1) * ROWS)
        q_rows = q_ref[rows, :] * jnp.asarray(0.125, bf16)
        outs, sums = [], []
        for head in range(2):
            mine = half if head == 0 else jnp.logical_not(half)
            q_head = jnp.where(mine, q_rows, jnp.zeros_like(q_rows))
            scores, reach = near_scores(q_head, keys, block)
            top = jnp.max(scores, axis=1, keepdims=True)
            raw = jnp.exp(scores - top)
            total = jnp.sum(raw, axis=1, keepdims=True)
            near = dot((raw * (1.0 / total)).astype(bf16), values[:reach], 1, 0)
            sums.append(top + jnp.log(total))
            scaled = dot(q_head, mem_keys, 1, 1)
            weights = density_parts(
                scaled, wm_ref[0, head : head + 1, :], wv_ref[0, head : head + 1, :]
            )[0]
            outs.append(near + dot(weights.astype(bf16), mem_values, 1, 0))
        ctx_ref[rows, :] = jnp.where(half, outs[0], outs[1]).astype(bf16)
        lse_ref[rows, :] = jnp.where(half, sums[0], sums[1])


def attn_bwd_kernel(
    order, rows_own, place_ref,
    q_ref, k_ref, v_ref, mk_ref, mv_ref, wm_ref, wv_ref, lse_ref, do_ref, ctx_ref, far_turned_ref, far_branch_ref,
    dq_ref, dk_ref, dv_ref, maps_ref, send_ref, keep_ref, acck_ref, accv_ref, turned_ref, branch_ref, sems, rides,
):
    fetches = (
        pltpu.make_async_copy(far_turned_ref, turned_ref, sems.at[0]),
        pltpu.make_async_copy(far_branch_ref, branch_ref, sems.at[1]),
    )

    @pl.when(pl.program_id(0) == 0)
    def _():
        for fetch in fetches:
            fetch.start()
        for ride in rides:
            ride.fetch()

    @pl.when(pl.program_id(0) == 1)
    def _():
        for ride in rides:
            ride.add()

    half = lax.broadcasted_iota(jnp.int32, (1, LANES), 1) < HD
    length = q_ref.shape[0]
    near_rows = k_ref.shape[0]
    keys, values = k_ref[...], v_ref[...]
    mem_keys, mem_values = mk_ref[...], mv_ref[...]
    other = jnp.logical_not(half)
    both = lambda x: jnp.concatenate(
        [jnp.where(half, x, jnp.zeros_like(x)), jnp.where(other, x, jnp.zeros_like(x))], axis=0
    )
    by_head = lambda ref: jnp.concatenate(
        [jnp.broadcast_to(ref[0, head : head + 1, :], (length, ref.shape[2])) for head in range(2)], axis=0
    )
    w_mean, w_var = by_head(wm_ref), by_head(wv_ref)
    early = near_rows - ROWS
    q_full, do_full = q_ref[...], do_ref[...]
    q_turn, do_turn = q_full.T, do_full.T
    q_both = both(q_full * jnp.asarray(0.125, bf16))
    do_both = both(do_full)

    def late(x):
        return jnp.concatenate([x[ROWS:length], x[length + ROWS :]], axis=0)

    row = lax.broadcasted_iota(jnp.int32, (2 * length, ROWS), 0) % length
    col = lax.broadcasted_iota(jnp.int32, (2 * length, ROWS), 1)
    scores = dot(q_both, keys[:early], 1, 1)
    edge = jnp.where(col <= row, scores[:, early - ROWS :], NEG)
    scores = jnp.concatenate([scores[:, : early - ROWS], edge], axis=1)
    row = lax.broadcasted_iota(jnp.int32, (length, ROWS), 0) % ROWS
    col = lax.broadcasted_iota(jnp.int32, (length, ROWS), 1)
    tail = jnp.where(col <= row, dot(late(q_both), keys[early:], 1, 1), NEG)
    lse = jnp.concatenate([lse_ref[:, 0:1], lse_ref[:, HD : HD + 1]], axis=0)
    probs, probs_tail = jnp.exp(scores - lse), jnp.exp(tail - late(lse))
    grad_probs = dot(do_both, values[:early], 1, 1)
    grad_tail = dot(late(do_both), values[early:], 1, 1)
    inner = jnp.sum(probs * grad_probs, axis=1, keepdims=True)
    more = jnp.sum(probs_tail * grad_tail, axis=1, keepdims=True)
    inner_late = late(inner) + more
    inner = jnp.concatenate(
        [inner[:ROWS], inner_late[:ROWS], inner[length : length + ROWS], inner_late[ROWS:]], axis=0
    )
    grad_raw = (0.125 * probs * (grad_probs - inner)).astype(bf16)
    raw_tail = (0.125 * probs_tail * (grad_tail - inner_late)).astype(bf16)
    probs_low, low_tail = probs.astype(bf16), probs_tail.astype(bf16)
    scaled = dot(q_both, mem_keys, 1, 1)
    weights, middle, var_raw, inv_var, offset, square = density_parts(scaled, w_mean, w_var)
    grad_w = dot(do_both, mem_values, 1, 1) * weights
    d_mid = -jnp.sum(grad_w * offset, axis=1, keepdims=True) * inv_var
    d_var = jnp.sum(grad_w * (square - 1.0), axis=1, keepdims=True) * (0.5 * inv_var)
    d_mid = d_mid * middle * (1.0 - middle)
    d_var = d_var * VAR_SCALE * jax.nn.sigmoid(var_raw)
    gm, gv = scaled * d_mid, scaled * d_var
    grad_mem = (0.125 * (d_mid * w_mean + d_var * w_var)).astype(bf16)
    weights_low = weights.astype(bf16)
    out = dot(grad_raw, keys[:early], 1, 0) + dot(grad_mem, mem_keys, 1, 0)
    out_tail = dot(raw_tail, keys[early:], 1, 0)
    for head in range(2):
        part = slice(head * HD, (head + 1) * HD)
        mine = slice(head * length, (head + 1) * length)
        ends = slice(head * ROWS, (head + 1) * ROWS)
        acck_ref[part, :early] = dot(q_turn[part], grad_raw[mine], 1, 0)
        accv_ref[part, :early] = dot(do_turn[part], probs_low[mine], 1, 0)
        acck_ref[part, early:near_rows] = dot(q_turn[part, ROWS:], raw_tail[ends], 1, 0)
        accv_ref[part, early:near_rows] = dot(do_turn[part, ROWS:], low_tail[ends], 1, 0)
        acck_ref[part, near_rows:] = dot(q_turn[part], grad_mem[mine], 1, 0)
        accv_ref[part, near_rows:] = dot(do_turn[part], weights_low[mine], 1, 0)
        maps_ref[0, head : head + 1, :] = jnp.sum(gm[mine], axis=0, keepdims=True)
        maps_ref[0, 2 + head : 3 + head, :] = jnp.sum(gv[mine], axis=0, keepdims=True)
    dq_ref[:ROWS, :] = jnp.where(half, out[:ROWS], out[length : length + ROWS]).astype(bf16)
    out = late(out) + out_tail
    dq_ref[ROWS:, :] = jnp.where(half, out[:ROWS], out[ROWS:]).astype(bf16)
    dk_ref[...] = acck_ref[...].T.astype(bf16)
    dv_ref[...] = accv_ref[...].T.astype(bf16)

    @pl.when(pl.program_id(0) == 0)
    def _():
        for fetch in fetches:
            fetch.wait()

    turned = turned_ref[...]
    grads = (
        dot(turned[:, length : 2 * length], dq_ref[...], 1, 0),
        dot(turned, dk_ref[...], 1, 0),
        dot(turned, dv_ref[...], 1, 0),
        dot(branch_ref[...], ctx_ref[...], 1, 0),
    )
    for at, grad in enumerate(grads):
        send, keep = cut_core(grad, place_ref[0], rows_own, order)
        send_ref[:, at], keep_ref[:, at] = send.astype(bf16), keep

    @pl.when(pl.program_id(0) == pl.num_programs(0) - 1)
    def _():
        for ride in rides:
            ride.done()


class Ride:
    def __init__(self, cut, bit, ins, outs, scratch):
        keep, came = ins
        width = keep.shape[-1] // 2

        def half(ref, b):
            return ref.at[:, :, pl.ds(pl.multiple_of(b * width, LANES), width)] if cut == "h" else ref.at[b]

        self.far, self.near, sems = scratch[:2], scratch[2:4], scratch[4]
        copy = pltpu.make_async_copy
        self.fetches = [
            copy(half(keep, 1 - bit), scratch[0], sems.at[0]),
            copy(half(came, 1 - bit), scratch[1], sems.at[1]),
            copy(half(keep, bit), scratch[2], sems.at[2]),
            copy(half(came, bit), scratch[3], sems.at[3]),
        ]
        self.writes = [copy(scratch[1], outs[0], sems.at[4]), copy(scratch[2], outs[1], sems.at[5])]

    def fetch(self):
        for one in self.fetches:
            one.start()

    def add(self):
        for one in self.fetches:
            one.wait()
        keep, came = self.far
        came[...] = (keep[...] + came[...].astype(f32)).astype(bf16)
        keep, came = self.near
        keep[...] = keep[...] + came[...].astype(f32)
        for one in self.writes:
            one.start()

    def done(self):
        for one in self.writes:
            one.wait()


def attn_specs(length, basis_count, place):
    near_rows = 2 * length
    near = pl.BlockSpec((near_rows, LANES), lambda p, *_: (0, place(p)))
    far = pl.BlockSpec((basis_count, LANES), lambda p, *_: (near_rows // basis_count, place(p)))
    maps = pl.BlockSpec((1, 2, basis_count), lambda p, *_: (place(p), 0, 0))
    return [pl.BlockSpec((length, LANES), lambda p, *_: (0, place(p))), near, near, far, far, maps, maps]


def attn_forward(queries, keys, values, w_mean, w_var, rows):
    length, width = queries.shape
    basis_count = w_mean.shape[-1]
    pairs = width // LANES
    size = rows.shape[0]
    ours = pl.BlockSpec((length, LANES), lambda p: (0, p))
    return call(
        attn_fwd_kernel, "attn_forward", (pairs,),
        attn_specs(length, basis_count, lambda p: p) + [pl.BlockSpec((size, LANES), lambda p: (0, p))],
        [
            (ours, struct(bf16, length, width)),
            (ours, struct(f32, length, width)),
            (pl.BlockSpec((LANES, size), lambda p: (p, 0)), struct(bf16, width, size)),
        ],
        scalars=0,
    )(queries, keys, values, keys, values, w_mean, w_var, rows)


def attn_backward(
    place, queries, keys, values, w_mean, w_var, lse, grad_ctx, context, turned, branch, group, groups, order, rows,
    span, into, riders,
):
    length, width = queries.shape
    basis_count = w_mean.shape[-1]
    pairs = width // LANES
    count = pairs // groups
    where = lambda p: p * groups + group
    all_rows = keys.shape[0]
    ours = lambda size: pl.BlockSpec((size, LANES), lambda p, _: (0, where(p)))
    cut = (len(order), 4, rows)
    mine = pl.BlockSpec(cut + (LANES,), lambda p, _: (0, 0, 0, p * len(span) + group - span[0]))
    specs = attn_specs(length, basis_count, where) + [ours(length)] * 3
    specs += [pl.BlockSpec(memory_space=pl.ANY)] * 2
    held = [pl.BlockSpec(memory_space=pl.ANY)] * len(into)

    others = Riders(riders)
    outs = [
        (ours(length), struct(bf16, length, width)),
        (ours(all_rows), struct(bf16, all_rows, width)),
        (ours(all_rows), struct(bf16, all_rows, width)),
        (pl.BlockSpec((1, 4, basis_count), lambda p, _: (where(p), 0, 0)), struct(f32, pairs, 4, basis_count)),
        (mine, struct(bf16, *cut, count * LANES * len(span))),
        (mine, struct(f32, *cut, count * LANES * len(span))),
    ]
    scratch = [
        pltpu.VMEM((LANES, all_rows), f32),
        pltpu.VMEM((LANES, all_rows), f32),
        pltpu.VMEM(turned.shape, bf16),
        pltpu.VMEM(branch.shape, bf16),
        pltpu.SemaphoreType.DMA((2,)),
    ]
    own = (1 + len(specs), len(outs), len(scratch))

    def kernel(*refs):
        first = own[0] + len(into)
        out = first + len(others.arrays)
        room = out + own[1] + len(others.outs)
        rides = others.going(refs[0], refs[first:out], refs[out + own[1] : room], refs[room + own[2] :])
        attn_bwd_kernel(order, rows, *refs[: own[0]], *refs[out : out + own[1]], *refs[room : room + own[2]], rides)

    results = call(
        kernel, "attn_backward", (count,),
        specs + held + others.specs,
        outs + others.outs,
        scratch=scratch + others.scratch,
        vmem=32 if riders else 22,
        aliases={own[0] + i: i for i in range(len(into))},
        near=tuple(range(own[0], own[0] + len(into))) + others.near(own[0] + len(into)),
    )(
        place, queries, keys, values, keys, values, w_mean, w_var, lse, grad_ctx, context, turned, branch, *into,
        *others.arrays,
    )
    for i, rider in enumerate(riders):
        rider.rode(*results[own[1] + 2 * i : own[1] + 2 * i + 2])
    return results[: own[1]]


def norm_stats(values):
    centred = values - jnp.mean(values, axis=-1, keepdims=True)
    spread = jnp.mean(centred * centred, axis=-1, keepdims=True)
    inverse = lax.rsqrt(spread + EPSILON)
    return centred * inverse, inverse


def norm_back(grad, hat, inverse, gain):
    scaled = grad * gain
    inner = jnp.mean(scaled * hat, axis=-1, keepdims=True)
    return inverse * (scaled - jnp.mean(scaled, axis=-1, keepdims=True) - hat * inner)


def side_block(ref):
    chips, cores, _, rows, cols = ref.shape
    return ref[...].reshape(chips * cores * rows, cols)


def block_order(bits):
    chips = []
    for place in range(1 << len(bits)):
        chip = 0
        for at, bit in enumerate(reversed(bits)):
            chip |= ((place >> at) & 1) << (bit - 1)
        chips.append(chip)
    return chips


def cut_core(value, core, rows, order):
    split = value.reshape(value.shape[0] // (2 * rows), 2, rows, value.shape[1])
    low = jnp.stack([split[chip, 0] for chip in order])
    high = jnp.stack([split[chip, 1] for chip in order])
    return jnp.where(core == 0, high, low), jnp.where(core == 0, low, high)


def mix_kernel(ctx_ref, tokens_ref, w_ref, gain_ref, hidden_ref, normed_ref):
    hidden = tokens_ref[...].astype(f32) + dot(ctx_ref[...], w_ref[...], 1, 1)
    hidden_ref[...] = hidden
    normed_ref[...] = (norm_stats(hidden)[0] * gain_ref[...]).astype(bf16)


def feed_kernel(
    order, place_ref, normed_ref, normed2_ref, cot_ref, cot2_ref, up_ref, down_ref,
    mlp_ref, mlp2_ref, gn_ref, gn2_ref, down_send_ref, down_keep_ref, up_send_ref, up_keep_ref,
    nt_ref, ct_ref, act_ref, pre_ref, acc_ref,
):
    step = pl.program_id(0)
    length, width = normed_ref.shape
    block = up_ref.shape[1] * up_ref.shape[3]
    w_up, w_down = side_block(up_ref), side_block(down_ref)
    slope = math.sqrt(2.0 / math.pi)

    @pl.when(step == 0)
    def _():
        nt_ref[:, :length] = normed_ref[...].T
        nt_ref[:, length:] = normed2_ref[...].T
        ct_ref[:, :length] = cot_ref[...].T
        ct_ref[:, length:] = cot2_ref[...].T

    for half in range(2):
        rows = slice(half * length, (half + 1) * length)
        normed = (normed_ref, normed2_ref)[half][...]
        cot = (cot_ref, cot2_ref)[half][...]
        pre = dot(normed, w_up, 1, 0)
        square = pre * pre
        bend = jnp.tanh(slope * pre * (1.0 + 0.044715 * square))
        lift = 0.5 + 0.5 * bend
        act = (pre * lift).astype(bf16)
        rise = lift + 0.5 * pre * (1.0 - bend * bend) * (slope + (3.0 * 0.044715 * slope) * square)
        grad_pre = (dot(cot, w_down, 1, 0) * rise).astype(bf16)
        act_ref[rows, :] = act
        pre_ref[rows, :] = grad_pre
        mlp = dot(act, w_down, 1, 1)
        grad_normed = dot(grad_pre, w_up, 1, 1)

        @pl.when(step == 0)
        def _():
            acc_ref[2 * half] = mlp
            acc_ref[2 * half + 1] = grad_normed

        @pl.when(step == 1)
        def _():
            if half == 0:
                mlp_ref[...] = acc_ref[0] + mlp
                gn_ref[...] = acc_ref[1] + grad_normed
            else:
                mlp2_ref[...] = (acc_ref[2] + mlp).astype(bf16)
                gn2_ref[...] = (acc_ref[3] + grad_normed).astype(bf16)

    g_down = dot(ct_ref[...], act_ref[...], 1, 0).reshape(width // block, block, -1)
    g_down = jnp.stack([g_down[chip] for chip in order])

    @pl.when(step == 0)
    def _():
        down_send_ref[...] = g_down.astype(bf16)

    @pl.when(step == 1)
    def _():
        down_keep_ref[...] = g_down

    g_up = dot(nt_ref[...], pre_ref[...], 1, 0).reshape(width // block, block, -1)
    low = jnp.stack([g_up[chip] for chip in order[: len(order) // 2]])
    high = jnp.stack([g_up[chip] for chip in order[len(order) // 2 :]])
    first = place_ref[1] == 0
    up_send_ref[...] = jnp.where(first, high, low).astype(bf16)
    up_keep_ref[...] = jnp.where(first, low, high)


def turn_kernel(
    hidden_ref, gn_ref, gn2_ref, cot_ref, w_ref, gain_ref, gh_ref, gain_grad_ref, gc_ref, branch_ref
):
    step = pl.program_id(0)
    hidden = hidden_ref[...]
    hat, inverse = norm_stats(hidden)
    grad = gn_ref[...] + gn2_ref[...].astype(f32)
    grad_hidden = cot_ref[...].astype(f32) + norm_back(grad, hat, inverse, gain_ref[...])
    gh_ref[...] = grad_hidden
    branch = grad_hidden.astype(bf16)
    branch_ref[...] = branch.T
    gc_ref[...] = dot(branch, w_ref[...], 1, 0).astype(bf16)

    @pl.when(step == 0)
    def _():
        gain_grad_ref[...] = jnp.zeros_like(gain_grad_ref)

    gain_grad_ref[...] += jnp.sum(grad * hat, axis=0, keepdims=True)


def finish_kernel(
    blocks, rides, dq_ref, dk_ref, dv_ref, wq_ref, wk_ref, wv_ref, ridge_ref, basis_ref, earlier_ref, tokens_ref, gh_ref,
    gain_ref, gain_m_ref, maps_ref, here_ref, gt_ref, gc_ref, small_ref, fit_ref, grad_ref,
):
    step = pl.program_id(0)
    length = ridge_ref.shape[1] // 2

    @pl.when(step == 0)
    def _():
        for ride in rides:
            ride.fetch()

    @pl.when(step == blocks + 1)
    def _():
        for ride in rides:
            ride.add()

    part = dot(dk_ref[...], wk_ref[...], 1, 1) + dot(dv_ref[...], wv_ref[...], 1, 1)

    @pl.when(step == 0)
    def _():
        memory = part.astype(bf16)
        samples = dot(ridge_ref[:, :length], memory, 0, 0).astype(bf16)
        gc_ref[...] = here_ref[0] * dot(basis_ref[...], samples, 0, 0)
        fit_ref[...] = dot(ridge_ref[:, length:], memory, 0, 0)
        grad_ref[...] = jnp.zeros_like(grad_ref)

    @pl.when(jnp.logical_and(step > 0, step <= blocks))
    def _():
        past = part + fit_ref[pl.ds(pl.multiple_of((step - 1) * ROWS, ROWS), ROWS), :]
        hat = norm_stats(earlier_ref[...].astype(f32))[0]
        grad_ref[...] += jnp.sum(past * hat, axis=0, keepdims=True)

    @pl.when(step > blocks)
    def _():
        grad = part + dot(dq_ref[...], wq_ref[...], 1, 1)
        hat, inverse = norm_stats(tokens_ref[...].astype(f32))
        grad_ref[...] += jnp.sum(grad * hat, axis=0, keepdims=True)
        gt_ref[...] = gh_ref[...] + norm_back(grad, hat, inverse, gain_ref[...])

    @pl.when(step == 2 * blocks)
    def _():
        small_ref[...] = jnp.zeros_like(small_ref)
        pairs, _, basis_count = maps_ref.shape
        for p in range(pairs):
            small_ref[2 * p : 2 * p + 2, :] = maps_ref[p, 0:2, :]
            small_ref[2 * (pairs + p) : 2 * (pairs + p) + 2, :] = maps_ref[p, 2:4, :]
        for at in range(grad_ref.shape[1] // basis_count):
            cols = slice(at * basis_count, (at + 1) * basis_count)
            row = 4 * pairs + 2 * at
            small_ref[row : row + 1, :] = grad_ref[:, cols]
            small_ref[row + 1 : row + 2, :] = gain_m_ref[:, cols]
        for ride in rides:
            ride.done()


def whole_spec(*shape):
    return pl.BlockSpec(shape, lambda *_: (0,) * len(shape))


def struct(kind, *shape):
    return jax.ShapeDtypeStruct(shape, kind)


def call(kernel, name, grid, in_specs, outs, scratch=(), scalars=1, vmem=24, aliases={}, near=(), near_outs=()):
    def place_of(at, out):
        return out if math.prod(out.shape) <= 1 << 16 or at in near_outs else pltpu.HBM(out.shape, out.dtype)

    run = pl.pallas_call(
        kernel,
        grid_spec=pltpu.PrefetchScalarGridSpec(
            num_scalar_prefetch=scalars,
            grid=grid,
            in_specs=in_specs,
            out_specs=[whole_spec(*out.shape) if spec is None else spec for spec, out in outs],
            scratch_shapes=scratch,
        ),
        out_shape=[place_of(at, out) for at, (_, out) in enumerate(outs)],
        input_output_aliases=aliases,
        compiler_params=pltpu.CompilerParams(vmem_limit_bytes=vmem << 20),
        cost_estimate=pl.CostEstimate(flops=0, bytes_accessed=1 << 20, transcendentals=0),
        name=name,
    )

    def put(at, x):
        return x if x.size <= 1 << 16 or at in near else pltpu.with_memory_space_constraint(x, pltpu.HBM)

    return lambda *args: run(*(put(at, x) for at, x in enumerate(args)))


def row_spec(width):
    return pl.BlockSpec((ROWS, width), lambda s, *_: (s, 0))


def mix(context, tokens, weights, gain):
    length, width = tokens.shape
    some = row_spec(width)
    return call(
        mix_kernel, "mix", (length // ROWS,),
        [some, some, whole_spec(width, width), whole_spec(1, width)],
        [(some, struct(f32, length, width)), (some, struct(bf16, length, width))],
        scalars=0,
        near_outs=(1,),
    )(context, tokens, weights, gain)


def feed(place, normed, normed2, cot, cot2, rest, tile, order):
    length, width = normed.shape
    chips, cores, _, rows, _ = rest.shape
    block = cores * rows
    big = whole_spec(length, width)

    def weights(at):
        return pl.BlockSpec(
            (chips, cores, 1, rows, tile), lambda s, p: (0, 0, (s + 1 + p[2]) % 2, 0, at + p[0])
        )

    half = (chips // 2, block, 2 * tile)
    turned = pl.BlockSpec((chips // 2, block, tile), lambda s, p: (0, 0, (s + 1 + p[2]) % 2))
    return call(
        lambda *refs: feed_kernel(order, *refs), "feed", (2,),
        [big, big, big, big, weights(0), weights(2)],
        [
            (None, struct(f32, length, width)),
            (None, struct(bf16, length, width)),
            (None, struct(f32, length, width)),
            (None, struct(bf16, length, width)),
            (None, struct(bf16, chips, block, tile)),
            (None, struct(f32, chips, block, tile)),
            (turned, struct(bf16, *half)),
            (turned, struct(f32, *half)),
        ],
        scratch=[
            pltpu.VMEM((width, 2 * length), bf16),
            pltpu.VMEM((width, 2 * length), bf16),
            pltpu.VMEM((2 * length, tile), bf16),
            pltpu.VMEM((2 * length, tile), bf16),
            pltpu.VMEM((4, length, width), f32),
        ],
        vmem=44,
        near=(1, 2, 4),
        near_outs=(2, 3),
    )(place, normed, normed2, cot, cot2, rest, rest)


def turn(hidden, gn, gn2, cot, weights, gain):
    length, width = hidden.shape
    some = row_spec(width)
    return call(
        turn_kernel, "turn", (length // ROWS,),
        [some] * 4 + [whole_spec(width, width), whole_spec(1, width)],
        [
            (some, struct(f32, length, width)),
            (None, struct(f32, 1, width)),
            (some, struct(bf16, length, width)),
            (pl.BlockSpec((width, ROWS), lambda s: (0, s)), struct(bf16, width, length)),
        ],
        scalars=0,
        near=(1, 2),
    )(hidden, gn, gn2, cot, weights, gain)


def finish(
    place, dq, dk, dv, weights, ridge, basis, earlier, tokens, grad_hidden, gain, gain_m_grad, maps, here, riders
):
    length, width = tokens.shape
    basis_count = ridge.shape[0]
    blocks = length // ROWS
    small = 4 * maps.shape[0] + 2 * (width // basis_count)
    all_rows = pl.BlockSpec((ROWS, width), lambda s, _: (jnp.where(s == 0, 2 * blocks, s - 1), 0))
    past = pl.BlockSpec((ROWS, width), lambda s, _: (jnp.clip(s - 1, 0, blocks - 1), 0))
    now = pl.BlockSpec((ROWS, width), lambda s, _: (jnp.maximum(s - 1 - blocks, 0), 0))
    args = (gain, gain_m_grad, maps)
    others = Riders(riders)
    outs = [
        (now, struct(f32, length, width)),
        (None, struct(f32, basis_count, width)),
        (None, struct(f32, small + (-small) % 8, basis_count)),
    ]
    scratch = [pltpu.VMEM((length, width), f32), pltpu.VMEM((1, width), f32)]
    ins = 3 + len(weights) + 2 + 3 + 3 + 1

    def kernel(place_ref, *refs):
        out = ins + len(others.arrays)
        room = out + 3 + len(others.outs)
        rides = others.going(place_ref, refs[ins:out], refs[out + 3 : room], refs[room + 2 :])
        finish_kernel(blocks, rides, *refs[:ins], *refs[out : out + 3], *refs[room : room + 2])

    results = call(
        kernel, "finish", (2 * blocks + 1,),
        [now, all_rows, all_rows]
        + [whole_spec(*x.shape) for x in (*weights, ridge, basis)]
        + [past, now, now]
        + [whole_spec(*x.shape) for x in args]
        + [pl.BlockSpec(memory_space=pltpu.SMEM)]
        + others.specs,
        outs + others.outs,
        scratch=scratch + others.scratch,
        vmem=22,
    )(place, dq, dk, dv, *weights, ridge, basis, earlier, tokens, grad_hidden, *args, here, *others.arrays)
    for i, rider in enumerate(riders):
        rider.rode(*results[3 + 2 * i : 5 + 2 * i])
    return results[:3]


class Links:
    def __init__(self, sizes):
        self.chips = sizes["chips"]
        self.bits = self.chips.bit_length()
        self.chip = lax.axis_index("chips")
        self.core = lax.axis_index("core")
        self.side = lax.axis_index("heads")
        self.places = [0, 1, "h"] + list(range(2, self.bits))

    def swap(self, value, stage):
        if stage in ("h", 0):
            return lax.ppermute(value, "heads" if stage == "h" else "core", [(0, 1), (1, 0)])
        mask = 1 << (stage - 1)
        return lax.ppermute(value, "chips", [(i, i ^ mask) for i in range(self.chips)])

    def bit(self, stage):
        if stage == "h":
            return self.side
        return self.core if stage == 0 else (self.chip >> (stage - 1)) & 1

    def gather(self, value, lead, stages, have=()):
        have = list(have)
        for stage in stages:
            other = self.swap(value, stage)
            if stage == "h":
                value = self.gather_with(value, other, stage, None)
            else:
                place = lead + sum(1 for b in have if b > stage)
                value = self.gather_with(value, other, stage, place)
                have.append(stage)
        return value

    def gather_with(self, value, other, stage, axis=0):
        mine_first = self.bit(stage) == 0
        first = jnp.where(mine_first, value, other)
        second = jnp.where(mine_first, other, value)
        if axis is None:
            return jnp.concatenate([first, second], axis=-1)
        return jnp.stack([first, second], axis=axis)

    def whole_rows(self, value, rows):
        value = value.reshape(2, rows, -1)
        mine = lax.dynamic_index_in_dim(value, self.core, 0, keepdims=False)
        other = self.swap(lax.dynamic_index_in_dim(value, 1 - self.core, 0, keepdims=False), 0)
        return self.gather_with(mine, other, 0, None)


def tie(value, *earlier):
    return lax.optimization_barrier((value,) + earlier)[0]


class Chain:
    def __init__(self, links, stages, send, keep, wire=bf16):
        self.links, self.wire = links, wire
        self.stage, self.stages = stages[0], list(stages[1:])
        self.left = [stage for stage in self.stages if stage != "h"]
        self.send, self.keep = self.spread(send), self.spread(keep)

    def spread(self, value):
        return value.reshape((2,) * len(self.left) + value.shape[1:])

    def cut(self):
        keep, came = self.keep, self.came
        self.stage = self.stages.pop(0) if self.stages else None
        if self.stage is None:
            self.value = keep + came.astype(f32)
            return
        bit = self.links.bit(self.stage)
        if self.stage == "h":
            width = keep.shape[-1] // 2
            take = lambda x, b: lax.dynamic_slice_in_dim(x, b * width, width, axis=x.ndim - 1)
        else:
            axis = self.left.index(self.stage)
            self.left.pop(axis)
            take = lambda x, b: lax.dynamic_index_in_dim(x, b, axis, keepdims=False)
        self.send = (take(keep, 1 - bit) + take(came, 1 - bit).astype(f32)).astype(self.wire)
        self.keep = take(keep, bit) + take(came, bit).astype(f32)

    def ride(self):
        self.stage = self.stages.pop(0)
        at = self.links.places.index(self.stage)
        tail = self.keep.shape[len(self.left) :]
        rows, cols = math.prod(tail[:-1]), tail[-1]
        if self.stage == "h":
            whole = (self.keep.size // (rows * cols), rows, cols)
            half = whole[:2] + (cols // 2,)
        else:
            self.left.pop(self.left.index(self.stage))
            whole = (2, self.keep.size // (2 * rows * cols), rows, cols)
            half = whole[1:]
        self.tail = tail[:-1] + half[-1:]
        return self.stage, at, [self.keep.reshape(whole), self.came.reshape(whole)], half

    def join(self, other):
        self.send = jnp.concatenate([self.send, other.send], axis=-1)
        self.keep = jnp.concatenate([self.keep, other.keep], axis=-1)

    def rode(self, send, keep):
        shape = (2,) * len(self.left) + self.tail
        self.send, self.keep = send.reshape(shape), keep.reshape(shape)


def together(values):
    return list(lax.optimization_barrier(tuple(values)))


class Riders:
    def __init__(self, chains):
        self.rides = [chain.ride() for chain in chains]
        anywhere = pl.BlockSpec(memory_space=pl.ANY)
        self.arrays = [x for _, _, arrays, _ in self.rides for x in arrays]
        self.specs = [anywhere] * len(self.arrays)
        self.outs, self.scratch = [], []
        for _, _, _, shape in self.rides:
            self.outs += [(anywhere, struct(bf16, *shape)), (anywhere, struct(f32, *shape))]
            self.scratch += [pltpu.VMEM(shape, kind) for kind in (f32, bf16, f32, bf16)]
            self.scratch += [pltpu.SemaphoreType.DMA((6,))]

    def near(self, first):
        return tuple(first + 1 + 2 * i for i in range(len(self.rides)))

    def going(self, place_ref, ins, outs, scratch):
        return [
            Ride(how, place_ref[at], ins[2 * i : 2 * i + 2], outs[2 * i : 2 * i + 2], scratch[5 * i : 5 * i + 5])
            for i, (how, at, _, _) in enumerate(self.rides)
        ]


def add_up(place, chains):
    others = Riders(chains)

    def kernel(place_ref, *refs):
        out = len(others.arrays)
        room = out + len(others.outs)
        rides = others.going(place_ref, refs[:out], refs[out:room], refs[room:])
        for ride in rides:
            ride.fetch()
        for ride in rides:
            ride.add()
        for ride in rides:
            ride.done()

    results = call(
        kernel, "add_up", (1,), others.specs, others.outs, scratch=others.scratch, vmem=24, near=others.near(1)
    )(place, *others.arrays)
    for i, chain in enumerate(chains):
        chain.rode(*results[2 * i : 2 * i + 2])


def hold(chains, *after):
    came = together([chain.came for chain in chains] + list(after))
    for chain, value in zip(chains, came):
        chain.came = value


def start(chains):
    chains = [chain for chain in chains if chain.stage is not None]
    if chains:
        for chain, send in zip(chains, together([chain.send for chain in chains])):
            chain.send = send
            chain.came = chain.links.swap(send, chain.stage)


def arrive(chains, *after):
    chains = [chain for chain in chains if chain.stage is not None]
    if chains:
        came = together([chain.came for chain in chains] + list(after))
        for chain, value in zip(chains, came):
            chain.came = value
            chain.cut()


def shards(
    tokens, earlier, coeffs, present, sample_at, w_qkv, w_out, w_up, w_down,
    gain_attn, gain_mlp, w_mean, w_var, cotangent, sizes, groups,
):
    links = Links(sizes)
    high = list(range(2, links.bits))
    count = 2 * links.chips
    tokens, earlier, coeffs, cotangent = tokens[0], earlier[0], coeffs[0], cotangent[0]
    length, width = tokens.shape
    basis_count = coeffs.shape[0]
    rows, side = w_qkv.shape[1], w_qkv.shape[2]
    ff_side = w_up.shape[1]
    local_heads, mem_part = w_mean.shape

    rest = jnp.concatenate([w_up, w_down.T], axis=1).astype(bf16)
    rest = lax.all_gather(rest, ("chips", "core", "heads"), axis=0, tiled=False)
    rest = rest.reshape(links.chips, 2, 2, rows, -1)
    tile = ff_side // 2
    small = jnp.concatenate(
        [gain_attn, gain_mlp, w_mean.reshape(-1), w_var.reshape(-1)]
    ).astype(bf16)
    small_size = small.shape[0]
    small = jnp.pad(small, (0, -small_size % LANES)).reshape(1, -1)
    small_h = links.swap(small, "h")
    first = jnp.where(links.side == 0, small, small_h)
    second = jnp.where(links.side == 0, small_h, small)
    far = high[1:][::-1]
    parts = jnp.concatenate([w_qkv, w_out.T[None]], axis=0).astype(bf16)
    parts = links.gather(parts, 1, far)
    small = links.gather(jnp.concatenate([first, second], axis=0), 0, far)
    small, parts = together([small, parts])
    turns = ([2, 1, "h"], [1, "h", 2], ["h", 2, 1], [1, 2, "h"])
    parts = [parts[c] for c in range(4)]
    have = list(far)
    haves = [list(far) for _ in range(4)]
    for step in range(3):
        small = links.gather(small, 0, [2 - step], have)
        have.append(2 - step)
        for c in range(4):
            parts[c] = links.gather(parts[c], 0, [turns[c][step]], haves[c])
            if turns[c][step] != "h":
                haves[c].append(turns[c][step])
        if step < 2:
            small, *parts = together([small] + parts)
    *qkv_full, out_full = [links.gather(parts[c], 0, [0], haves[c]).reshape(width, width) for c in range(4)]
    small = small.reshape(count, 2, -1).astype(f32)
    gain_a = small[:, 0, :rows].reshape(-1)
    gain_m = small[:, 0, rows : 2 * rows].reshape(-1)

    def head_map(start):
        part = small[:, :, start : start + local_heads * mem_part]
        part = part.reshape(count, 2, local_heads, mem_part).transpose(1, 2, 0, 3)
        return part.reshape(local_heads, 2, basis_count)

    mean_full = head_map(2 * rows)
    var_full = head_map(2 * rows + local_heads * mem_part)

    cot2 = links.swap(cotangent, 0)
    place = jnp.stack([links.bit(stage) for stage in links.places]).astype(jnp.int32)

    ridge = ridge_table(basis_count, 2 * length)
    tokens32, earlier32 = tokens.astype(f32), earlier.astype(f32)
    normed = layer_norm(tokens32, gain_a).astype(bf16)
    past = layer_norm(earlier32, gain_a).astype(bf16)
    old_basis = basis_at((sample_at[0].astype(f32) + 0.5) / GRID, basis_count).astype(bf16)
    here = present[0].astype(f32)
    samples = (here * dot(old_basis, coeffs.astype(bf16), 1, 0)).astype(bf16)
    memory = dot(ridge, jnp.concatenate([samples, past], axis=0), 1, 0).astype(bf16)
    sources = jnp.concatenate([past, normed, memory], axis=0)
    queries = dot(normed, qkv_full[0], 1, 0).astype(bf16)
    keys = dot(sources, qkv_full[1], 1, 0).astype(bf16)
    values = dot(sources, qkv_full[2], 1, 0).astype(bf16)
    old_basis, queries = together([old_basis, queries])
    context, lse, turned = attn_forward(queries, keys, values, mean_full, var_full, sources)
    gain_row = gain_m.reshape(1, -1)
    hidden, normed_mlp = mix(context, tokens, out_full, gain_row)
    normed_mlp2 = links.swap(normed_mlp, 0)
    lows = [2] + high[1:]
    order = block_order([1] + lows)
    mlp, mlp2, gn, gn2, down_send, down_keep, up_send, up_keep = feed(
        place, normed_mlp, normed_mlp2, cotangent, cot2, rest, tile, order
    )
    gn2 = links.swap(gn2, 0)
    mlp2 = links.swap(mlp2, 0)
    c_down = Chain(links, ["h", 1] + lows, down_send, down_keep)
    c_up = Chain(links, [1, 2] + high[1:] + ["h"], up_send, up_keep)
    start([c_down, c_up])
    grad_hidden, gain_m_grad, grad_ctx, branch = turn(hidden, gn, gn2, cotangent, out_full, gain_row)

    plans = (["h", 1, 2], [1, "h", 2])
    spans = [list(range(groups - 1)), [groups - 1]]
    feeds, c_qkv = [c_down, c_up], []
    into = ()
    for group in range(groups):
        late = group == groups - 1
        plan = plans[late] + high[1:]
        if late:
            into = into[:4]
        riders = c_qkv if late else feeds if group == 1 else []
        if riders:
            hold(riders, into[0])
        into = attn_backward(
            place, queries, keys, values, mean_full, var_full, lse, grad_ctx, context, turned, branch, group, groups,
            block_order([b for b in plan if b != "h"]), rows, spans[late], into, riders,
        )
        if group == spans[late][-1]:
            c_qkv = c_qkv + [Chain(links, [0] + plan, into[4], into[5])]
        sends = [c.send for c in riders]
        if not late:
            start(riders)
            if c_qkv:
                c_qkv[0].send = tie(c_qkv[0].send, *sends)
                start(c_qkv)
                sends = [c_qkv[0].send]
        grad_ctx = tie(grad_ctx, into[0], *sends)
    arrive(feeds, into[0])
    chains = feeds + c_qkv
    last = chains[-1]
    last.send = tie(last.send, *[c.send for c in feeds])
    start([last])
    start(chains[:-1])
    arrive([last])
    start([last])
    dq, dk, dv, maps = into[:4]
    dq = tie(dq, *[c.send for c in chains])
    grad_tokens, grad_coeffs, tiny = finish(
        place, dq, dk, dv, qkv_full, ridge, old_basis, earlier, tokens, grad_hidden, gain_a.reshape(1, -1),
        gain_m_grad, maps, here.reshape(1), [],
    )

    def add(value, stage):
        return value + links.swap(value, stage)

    tiny_stages = [["h", 1]] + [[stage] for stage in lows]
    hold(chains, tiny)
    add_up(place, chains)
    tiny = tie(tiny, *[c.send for c in chains])
    output = (tie(hidden, tiny) + (mlp + mlp2.astype(f32))).astype(bf16)
    tiny = add(tiny, 0)
    joined = False
    while tiny_stages or any(chain.stage is not None for chain in chains):
        going = [c for c in chains if c.stage is not None]
        start(going)
        for stage in tiny_stages.pop(0) if tiny_stages else []:
            tiny = add(tiny, stage)
        *came, tiny = together([c.came for c in going] + [tiny])
        for chain, value in zip(going, came):
            chain.came = value
        on = [c for c in going if c.stages]
        ends = [c for c in going if not c.stages]
        for chain in on:
            chain.cut()
        if not joined:
            joined = True
            c_qkv[0].join(c_qkv[1])
            chains.remove(c_qkv[1])
            on = [c for c in on if c is not c_qkv[1]]
        if on and ends:
            hold(ends, *[c.send for c in on])
        for chain in ends:
            chain.cut()
    r_down, r_up = links.whole_rows(c_down.value, rows), links.whole_rows(c_up.value, rows)
    r_proj = c_qkv[0].value
    heads = 2 * local_heads
    item = 2 * links.chip + links.core
    pick_map = lambda first: lax.dynamic_slice(
        tiny, (first + local_heads * links.side, item * mem_part), (local_heads, mem_part)
    )
    mean_out, var_out = pick_map(0), pick_map(heads)
    gains = tiny[2 * heads : 2 * heads + 2 * (width // basis_count)].reshape(-1, 2, basis_count)
    gain_part = width // (2 * count)
    pick_gain = lambda at: lax.dynamic_slice(
        gains[:, at].reshape(-1), ((2 * item + links.side) * gain_part,), (gain_part,)
    )
    gain_a_out, gain_m_out = pick_gain(0), pick_gain(1)
    return (
        output[None],
        grad_tokens[None],
        grad_coeffs[None],
        r_proj[:3],
        r_proj[3].T,
        r_up,
        r_down.T,
        gain_a_out,
        gain_m_out,
        mean_out,
        var_out,
    )


def solution(mesh):
    sizes = dict(mesh.shape)
    both = ("items", "heads")
    in_specs = (
        P(both, None, None),
        P(both, None, None),
        P(both, None, None),
        P(both),
        P(both, None),
        P(None, "items", "heads"),
        P("heads", "items"),
        P("items", "heads"),
        P("heads", "items"),
        P("items"),
        P("items"),
        P("heads", "items"),
        P("heads", "items"),
        P(both, None, None),
    )
    out_specs = (
        P(both, None, None),
        P(both, None, None),
        P(both, None, None),
        P(None, "items", "heads"),
        P("heads", "items"),
        P("items", "heads"),
        P("heads", "items"),
        P(both),
        P(both),
        P("heads", "items"),
        P("heads", "items"),
    )

    chips = sizes["items"] // 2
    split = Mesh(mesh.devices.reshape(chips, 2, sizes["heads"]), ("chips", "core", "heads"))

    def respec(spec):
        def axis(entry):
            names = entry if isinstance(entry, tuple) else (entry,)
            flat = tuple(n for name in names for n in (("chips", "core") if name == "items" else (name,)))
            return flat if flat != (None,) else None

        return P(*(axis(entry) for entry in spec))

    def body(*args):
        return shards(*args, sizes=dict(split.shape), groups=3)

    return jax.shard_map(
        body,
        mesh=split,
        in_specs=tuple(respec(spec) for spec in in_specs),
        out_specs=tuple(respec(spec) for spec in out_specs),
        check_vma=False,
    )
```

```python
import math

import jax
import jax.numpy as jnp
import numpy as np
from jax import lax
from jax.experimental import pallas as pl
from jax.experimental.pallas import tpu as pltpu
from jax.sharding import Mesh
from jax.sharding import PartitionSpec as P

HD = 64
GRID = 1024
EPSILON = 1e-05
VAR_SCALE = 0.01
RIDGE = 1.0
LANES = 128
ROWS = 256
NEG = -1e30
bf16 = jnp.bfloat16
f32 = jnp.float32


def dot(a, b, ca, cb):
    return lax.dot_general(a, b, (((ca,), (cb,)), ((), ())), preferred_element_type=f32)


def layer_norm(values, gain_vec):
    row_mean = jnp.mean(values, axis=-1, keepdims=True)
    centred = values - row_mean
    spread = jnp.mean(centred * centred, axis=-1, keepdims=True)
    return centred * lax.rsqrt(spread + EPSILON) * gain_vec


def basis_at(points, basis_count):
    centers = (jnp.arange(basis_count, dtype=f32) + 0.5) / basis_count
    offset = points[..., None] - centers
    return jnp.exp(-offset * offset * (0.5 * basis_count * basis_count))


def ridge_table(basis_count, samples):
    points = (np.arange(samples) + 0.5) / samples
    centers = (np.arange(basis_count) + 0.5) / basis_count
    design = np.exp(-((points[:, None] - centers) ** 2) * (0.5 * basis_count * basis_count))
    gram = design.T @ design + RIDGE * np.eye(basis_count)
    factor = np.linalg.cholesky(gram)
    table = np.linalg.solve(factor.T, np.linalg.solve(factor, design.T))
    return jnp.asarray(table.astype(np.float32)).astype(bf16)


def gelu_tanh(values):
    return jax.nn.gelu(values, approximate=True)


def near_scores(q_rows, keys, block):
    reach = keys.shape[0] // 2 + (block + 1) * ROWS
    scores = dot(q_rows, keys[:reach], 1, 1)
    row = lax.broadcasted_iota(jnp.int32, (q_rows.shape[0], ROWS), 0) % ROWS
    col = lax.broadcasted_iota(jnp.int32, (q_rows.shape[0], ROWS), 1)
    edge = jnp.where(col <= row, scores[:, reach - ROWS :], NEG)
    return jnp.concatenate([scores[:, : reach - ROWS], edge], axis=1), reach


def both_heads(x, half):
    none = jnp.zeros_like(x)
    return jnp.concatenate([jnp.where(half, x, none), jnp.where(half, none, x)], axis=0)


def by_head(ref, rows):
    return jnp.concatenate(
        [jnp.broadcast_to(ref[0, head : head + 1, :], (rows, ref.shape[2])) for head in range(2)], axis=0
    )


def density_parts(scaled, w_mean, w_var):
    basis_count = scaled.shape[1]
    index = lax.broadcasted_iota(jnp.int32, (1, basis_count), 1).astype(f32)
    centers = (index + 0.5) / basis_count
    middle = jax.nn.sigmoid(jnp.sum(scaled * w_mean, axis=1, keepdims=True))
    var_raw = jnp.sum(scaled * w_var, axis=1, keepdims=True)
    softplus = jnp.maximum(var_raw, 0.0) + jnp.log1p(jnp.exp(-jnp.abs(var_raw)))
    variance = VAR_SCALE * softplus + 1.0 / (basis_count * basis_count)
    offset = middle - centers
    inv_var = 1.0 / variance
    square = offset * offset * inv_var
    scale = lax.rsqrt(2.0 * math.pi * variance) / basis_count
    weights = jnp.exp(-0.5 * square) * scale
    return weights, middle, var_raw, inv_var, offset, square


def attn_fwd_kernel(
    q_ref, k_ref, v_ref, mk_ref, mv_ref, wm_ref, wv_ref, rows_ref, ctx_ref, lse_ref, turned_ref
):
    turned_ref[...] = rows_ref[...].T
    half = lax.broadcasted_iota(jnp.int32, (1, LANES), 1) < HD
    length = q_ref.shape[0]
    keys, values = k_ref[...], v_ref[...]
    mem_keys, mem_values = mk_ref[...], mv_ref[...]
    w_mean, w_var = by_head(wm_ref, ROWS), by_head(wv_ref, ROWS)
    for block in range(length // ROWS):
        rows = slice(block * ROWS, (block + 1) * ROWS)
        q_both = both_heads(q_ref[rows, :] * jnp.asarray(0.125, bf16), half)
        scores, reach = near_scores(q_both, keys, block)
        top = jnp.max(scores, axis=1, keepdims=True)
        raw = jnp.exp(scores - top)
        total = jnp.sum(raw, axis=1, keepdims=True)
        near = dot((raw * (1.0 / total)).astype(bf16), values[:reach], 1, 0)
        weights = density_parts(dot(q_both, mem_keys, 1, 1), w_mean, w_var)[0]
        out = near + dot(weights.astype(bf16), mem_values, 1, 0)
        logs = top + jnp.log(total)
        ctx_ref[rows, :] = jnp.where(half, out[:ROWS], out[ROWS:]).astype(bf16)
        lse_ref[rows, :] = jnp.where(half, logs[:ROWS], logs[ROWS:])


def attn_bwd_kernel(
    order, rows_own, place_ref,
    q_ref, k_ref, v_ref, mk_ref, mv_ref, wm_ref, wv_ref, lse_ref, do_ref, ctx_ref, far_turned_ref, far_branch_ref,
    dq_ref, dk_ref, dv_ref, maps_ref, send_ref, keep_ref, acck_ref, accv_ref, turned_ref, branch_ref, sems, rides,
):
    fetches = (
        pltpu.make_async_copy(far_turned_ref, turned_ref, sems.at[0]),
        pltpu.make_async_copy(far_branch_ref, branch_ref, sems.at[1]),
    )

    @pl.when(pl.program_id(0) == 0)
    def _():
        for fetch in fetches:
            fetch.start()
        for ride in rides:
            ride.fetch()

    @pl.when(pl.program_id(0) == 1)
    def _():
        for ride in rides:
            ride.add()

    half = lax.broadcasted_iota(jnp.int32, (1, LANES), 1) < HD
    length = q_ref.shape[0]
    near_rows = k_ref.shape[0]
    keys, values = k_ref[...], v_ref[...]
    mem_keys, mem_values = mk_ref[...], mv_ref[...]
    both = lambda x: both_heads(x, half)
    w_mean, w_var = by_head(wm_ref, length), by_head(wv_ref, length)
    early = near_rows - ROWS
    q_full, do_full = q_ref[...], do_ref[...]
    q_turn, do_turn = q_full.T, do_full.T
    q_both = both(q_full * jnp.asarray(0.125, bf16))
    do_both = both(do_full)

    def late(x):
        return jnp.concatenate([x[ROWS:length], x[length + ROWS :]], axis=0)

    row = lax.broadcasted_iota(jnp.int32, (2 * length, ROWS), 0) % length
    col = lax.broadcasted_iota(jnp.int32, (2 * length, ROWS), 1)
    scores = dot(q_both, keys[:early], 1, 1)
    edge = jnp.where(col <= row, scores[:, early - ROWS :], NEG)
    scores = jnp.concatenate([scores[:, : early - ROWS], edge], axis=1)
    row = lax.broadcasted_iota(jnp.int32, (length, ROWS), 0) % ROWS
    col = lax.broadcasted_iota(jnp.int32, (length, ROWS), 1)
    tail = jnp.where(col <= row, dot(late(q_both), keys[early:], 1, 1), NEG)
    lse = jnp.concatenate([lse_ref[:, 0:1], lse_ref[:, HD : HD + 1]], axis=0)
    probs, probs_tail = jnp.exp(scores - lse), jnp.exp(tail - late(lse))
    grad_probs = dot(do_both, values[:early], 1, 1)
    grad_tail = dot(late(do_both), values[early:], 1, 1)
    inner = jnp.sum(probs * grad_probs, axis=1, keepdims=True)
    more = jnp.sum(probs_tail * grad_tail, axis=1, keepdims=True)
    inner_late = late(inner) + more
    inner = jnp.concatenate(
        [inner[:ROWS], inner_late[:ROWS], inner[length : length + ROWS], inner_late[ROWS:]], axis=0
    )
    grad_raw = (0.125 * probs * (grad_probs - inner)).astype(bf16)
    raw_tail = (0.125 * probs_tail * (grad_tail - inner_late)).astype(bf16)
    probs_low, low_tail = probs.astype(bf16), probs_tail.astype(bf16)
    scaled = dot(q_both, mem_keys, 1, 1)
    weights, middle, var_raw, inv_var, offset, square = density_parts(scaled, w_mean, w_var)
    grad_w = dot(do_both, mem_values, 1, 1) * weights
    d_mid = -jnp.sum(grad_w * offset, axis=1, keepdims=True) * inv_var
    d_var = jnp.sum(grad_w * (square - 1.0), axis=1, keepdims=True) * (0.5 * inv_var)
    d_mid = d_mid * middle * (1.0 - middle)
    d_var = d_var * VAR_SCALE * jax.nn.sigmoid(var_raw)
    gm, gv = scaled * d_mid, scaled * d_var
    grad_mem = (0.125 * (d_mid * w_mean + d_var * w_var)).astype(bf16)
    weights_low = weights.astype(bf16)
    out = dot(grad_raw, keys[:early], 1, 0) + dot(grad_mem, mem_keys, 1, 0)
    out_tail = dot(raw_tail, keys[early:], 1, 0)
    for head in range(2):
        part = slice(head * HD, (head + 1) * HD)
        mine = slice(head * length, (head + 1) * length)
        ends = slice(head * ROWS, (head + 1) * ROWS)
        acck_ref[part, :early] = dot(q_turn[part], grad_raw[mine], 1, 0)
        accv_ref[part, :early] = dot(do_turn[part], probs_low[mine], 1, 0)
        acck_ref[part, early:near_rows] = dot(q_turn[part, ROWS:], raw_tail[ends], 1, 0)
        accv_ref[part, early:near_rows] = dot(do_turn[part, ROWS:], low_tail[ends], 1, 0)
        acck_ref[part, near_rows:] = dot(q_turn[part], grad_mem[mine], 1, 0)
        accv_ref[part, near_rows:] = dot(do_turn[part], weights_low[mine], 1, 0)
        maps_ref[0, head : head + 1, :] = jnp.sum(gm[mine], axis=0, keepdims=True)
        maps_ref[0, 2 + head : 3 + head, :] = jnp.sum(gv[mine], axis=0, keepdims=True)
    dq_ref[:ROWS, :] = jnp.where(half, out[:ROWS], out[length : length + ROWS]).astype(bf16)
    out = late(out) + out_tail
    dq_ref[ROWS:, :] = jnp.where(half, out[:ROWS], out[ROWS:]).astype(bf16)
    dk_ref[...] = acck_ref[...].T.astype(bf16)
    dv_ref[...] = accv_ref[...].T.astype(bf16)

    @pl.when(pl.program_id(0) == 0)
    def _():
        for fetch in fetches:
            fetch.wait()

    turned = turned_ref[...]
    grads = (
        dot(turned[:, length : 2 * length], dq_ref[...], 1, 0),
        dot(turned, dk_ref[...], 1, 0),
        dot(turned, dv_ref[...], 1, 0),
        dot(branch_ref[...], ctx_ref[...], 1, 0),
    )
    for at, grad in enumerate(grads):
        send, keep = cut_core(grad, place_ref[0], rows_own, order)
        send_ref[:, at], keep_ref[:, at] = send.astype(bf16), keep

    @pl.when(pl.program_id(0) == pl.num_programs(0) - 1)
    def _():
        for ride in rides:
            ride.done()


class Ride:
    def __init__(self, cut, bit, ins, outs, scratch):
        keep, came = ins
        width = keep.shape[-1] // 2

        def half(ref, b):
            return ref.at[:, :, pl.ds(pl.multiple_of(b * width, LANES), width)] if cut == "h" else ref.at[b]

        self.far, self.near, sems = scratch[:2], scratch[2:4], scratch[4]
        copy = pltpu.make_async_copy
        self.fetches = [
            copy(half(keep, 1 - bit), scratch[0], sems.at[0]),
            copy(half(came, 1 - bit), scratch[1], sems.at[1]),
            copy(half(keep, bit), scratch[2], sems.at[2]),
            copy(half(came, bit), scratch[3], sems.at[3]),
        ]
        self.writes = [copy(scratch[1], outs[0], sems.at[4]), copy(scratch[2], outs[1], sems.at[5])]

    def fetch(self):
        for one in self.fetches:
            one.start()

    def add(self):
        for one in self.fetches:
            one.wait()
        keep, came = self.far
        came[...] = (keep[...] + came[...].astype(f32)).astype(bf16)
        keep, came = self.near
        keep[...] = keep[...] + came[...].astype(f32)
        for one in self.writes:
            one.start()

    def done(self):
        for one in self.writes:
            one.wait()


def attn_specs(length, basis_count, place):
    near_rows = 2 * length
    near = pl.BlockSpec((near_rows, LANES), lambda p, *_: (0, place(p)))
    far = pl.BlockSpec((basis_count, LANES), lambda p, *_: (near_rows // basis_count, place(p)))
    maps = pl.BlockSpec((1, 2, basis_count), lambda p, *_: (place(p), 0, 0))
    return [pl.BlockSpec((length, LANES), lambda p, *_: (0, place(p))), near, near, far, far, maps, maps]


def attn_forward(queries, keys, values, w_mean, w_var, rows):
    length, width = queries.shape
    basis_count = w_mean.shape[-1]
    pairs = width // LANES
    size = rows.shape[0]
    ours = pl.BlockSpec((length, LANES), lambda p: (0, p))
    return call(
        attn_fwd_kernel, "attn_forward", (pairs,),
        attn_specs(length, basis_count, lambda p: p) + [pl.BlockSpec((size, LANES), lambda p: (0, p))],
        [
            (ours, struct(bf16, length, width)),
            (ours, struct(f32, length, width)),
            (pl.BlockSpec((LANES, size), lambda p: (p, 0)), struct(bf16, width, size)),
        ],
        scalars=0,
        near=tuple(range(8)),
    )(queries, keys, values, keys, values, w_mean, w_var, rows)


def attn_backward(
    place, queries, keys, values, w_mean, w_var, lse, grad_ctx, context, turned, branch, group, groups, order, rows,
    span, into, riders,
):
    length, width = queries.shape
    basis_count = w_mean.shape[-1]
    pairs = width // LANES
    count = pairs // groups
    where = lambda p: p * groups + group
    all_rows = keys.shape[0]
    ours = lambda size: pl.BlockSpec((size, LANES), lambda p, _: (0, where(p)))
    cut = (len(order), 4, rows)
    mine = pl.BlockSpec(cut + (LANES,), lambda p, _: (0, 0, 0, p * len(span) + group - span[0]))
    specs = attn_specs(length, basis_count, where) + [ours(length)] * 3
    specs += [pl.BlockSpec(memory_space=pl.ANY)] * 2
    held = [pl.BlockSpec(memory_space=pl.ANY)] * len(into)

    others = Riders(riders)
    outs = [
        (ours(length), struct(bf16, length, width)),
        (ours(all_rows), struct(bf16, all_rows, width)),
        (ours(all_rows), struct(bf16, all_rows, width)),
        (pl.BlockSpec((1, 4, basis_count), lambda p, _: (where(p), 0, 0)), struct(f32, pairs, 4, basis_count)),
        (mine, struct(bf16, *cut, count * LANES * len(span))),
        (mine, struct(f32, *cut, count * LANES * len(span))),
    ]
    scratch = [
        pltpu.VMEM((LANES, all_rows), f32),
        pltpu.VMEM((LANES, all_rows), f32),
        pltpu.VMEM(turned.shape, bf16),
        pltpu.VMEM(branch.shape, bf16),
        pltpu.SemaphoreType.DMA((2,)),
    ]
    own = (1 + len(specs), len(outs), len(scratch))

    def kernel(*refs):
        first = own[0] + len(into)
        out = first + len(others.arrays)
        room = out + own[1] + len(others.outs)
        rides = others.going(refs[0], refs[first:out], refs[out + own[1] : room], refs[room + own[2] :])
        attn_bwd_kernel(order, rows, *refs[: own[0]], *refs[out : out + own[1]], *refs[room : room + own[2]], rides)

    results = call(
        kernel, "attn_backward", (count,),
        specs + held + others.specs,
        outs + others.outs,
        scratch=scratch + others.scratch,
        vmem=32 if riders else 22,
        aliases={own[0] + i: i for i in range(len(into))},
        near=tuple(range(own[0], own[0] + len(into))) + others.near(own[0] + len(into)),
    )(
        place, queries, keys, values, keys, values, w_mean, w_var, lse, grad_ctx, context, turned, branch, *into,
        *others.arrays,
    )
    for i, rider in enumerate(riders):
        rider.rode(*results[own[1] + 2 * i : own[1] + 2 * i + 2])
    return results[: own[1]]


def norm_stats(values):
    centred = values - jnp.mean(values, axis=-1, keepdims=True)
    spread = jnp.mean(centred * centred, axis=-1, keepdims=True)
    inverse = lax.rsqrt(spread + EPSILON)
    return centred * inverse, inverse


def norm_back(grad, hat, inverse, gain):
    scaled = grad * gain
    inner = jnp.mean(scaled * hat, axis=-1, keepdims=True)
    return inverse * (scaled - jnp.mean(scaled, axis=-1, keepdims=True) - hat * inner)


def side_block(ref):
    chips, cores, _, rows, cols = ref.shape
    return ref[...].reshape(chips * cores * rows, cols)


def block_order(bits):
    chips = []
    for place in range(1 << len(bits)):
        chip = 0
        for at, bit in enumerate(reversed(bits)):
            chip |= ((place >> at) & 1) << (bit - 1)
        chips.append(chip)
    return chips


def cut_core(value, core, rows, order):
    split = value.reshape(value.shape[0] // (2 * rows), 2, rows, value.shape[1])
    low = jnp.stack([split[chip, 0] for chip in order])
    high = jnp.stack([split[chip, 1] for chip in order])
    return jnp.where(core == 0, high, low), jnp.where(core == 0, low, high)


def mix_kernel(ctx_ref, tokens_ref, w_ref, gain_ref, hidden_ref, normed_ref):
    hidden = tokens_ref[...].astype(f32) + dot(ctx_ref[...], w_ref[...], 1, 1)
    hidden_ref[...] = hidden
    normed_ref[...] = (norm_stats(hidden)[0] * gain_ref[...]).astype(bf16)


def feed_kernel(
    order, place_ref, normed_ref, normed2_ref, cot_ref, cot2_ref, up_ref, down_ref,
    mlp_ref, mlp2_ref, gn_ref, gn2_ref, down_send_ref, down_keep_ref, up_send_ref, up_keep_ref,
    nt_ref, ct_ref, act_ref, pre_ref, acc_ref, near_send_ref, near_keep_ref, sems,
):
    step = pl.program_id(0)
    length, width = normed_ref.shape
    block = up_ref.shape[1] * up_ref.shape[3]
    w_up, w_down = side_block(up_ref), side_block(down_ref)
    slope = math.sqrt(2.0 / math.pi)

    @pl.when(step == 0)
    def _():
        nt_ref[:, :length] = normed_ref[...].T
        nt_ref[:, length:] = normed2_ref[...].T
        ct_ref[:, :length] = cot_ref[...].T
        ct_ref[:, length:] = cot2_ref[...].T

    for half in range(2):
        rows = slice(half * length, (half + 1) * length)
        normed = (normed_ref, normed2_ref)[half][...]
        cot = (cot_ref, cot2_ref)[half][...]
        pre = dot(normed, w_up, 1, 0)
        square = pre * pre
        bend = jnp.tanh(slope * pre * (1.0 + 0.044715 * square))
        lift = 0.5 + 0.5 * bend
        act = (pre * lift).astype(bf16)
        rise = lift + 0.5 * pre * (1.0 - bend * bend) * (slope + (3.0 * 0.044715 * slope) * square)
        grad_pre = (dot(cot, w_down, 1, 0) * rise).astype(bf16)
        act_ref[rows, :] = act
        pre_ref[rows, :] = grad_pre
        mlp = dot(act, w_down, 1, 1)
        grad_normed = dot(grad_pre, w_up, 1, 1)

        @pl.when(step == 0)
        def _():
            acc_ref[2 * half] = mlp
            acc_ref[2 * half + 1] = grad_normed

        @pl.when(step == 1)
        def _():
            if half == 0:
                mlp_ref[...] = acc_ref[0] + mlp
                gn_ref[...] = acc_ref[1] + grad_normed
            else:
                mlp2_ref[...] = (acc_ref[2] + mlp).astype(bf16)
                gn2_ref[...] = (acc_ref[3] + grad_normed).astype(bf16)

    sent = pltpu.make_async_copy(near_send_ref, down_send_ref, sems.at[0])
    kept = pltpu.make_async_copy(near_keep_ref, down_keep_ref, sems.at[1])
    g_down = dot(ct_ref[...], act_ref[...], 1, 0).reshape(width // block, block, -1)
    g_down = jnp.stack([g_down[chip] for chip in order])

    @pl.when(step == 0)
    def _():
        near_send_ref[...] = g_down.astype(bf16)
        sent.start()

    @pl.when(step == 1)
    def _():
        near_keep_ref[...] = g_down
        kept.start()

    g_up = dot(nt_ref[...], pre_ref[...], 1, 0).reshape(width // block, block, -1)
    low = jnp.stack([g_up[chip] for chip in order[: len(order) // 2]])
    high = jnp.stack([g_up[chip] for chip in order[len(order) // 2 :]])
    first = place_ref[1] == 0
    up_send_ref[...] = jnp.where(first, high, low).astype(bf16)
    up_keep_ref[...] = jnp.where(first, low, high)

    @pl.when(step == 1)
    def _():
        sent.wait()
        kept.wait()


def turn_kernel(
    hidden_ref, gn_ref, gn2_ref, cot_ref, w_ref, gain_ref, gh_ref, gain_grad_ref, gc_ref, branch_ref
):
    step = pl.program_id(0)
    hidden = hidden_ref[...]
    hat, inverse = norm_stats(hidden)
    grad = gn_ref[...] + gn2_ref[...].astype(f32)
    grad_hidden = cot_ref[...].astype(f32) + norm_back(grad, hat, inverse, gain_ref[...])
    gh_ref[...] = grad_hidden
    branch = grad_hidden.astype(bf16)
    branch_ref[...] = branch.T
    gc_ref[...] = dot(branch, w_ref[...], 1, 0).astype(bf16)

    @pl.when(step == 0)
    def _():
        gain_grad_ref[...] = jnp.zeros_like(gain_grad_ref)

    gain_grad_ref[...] += jnp.sum(grad * hat, axis=0, keepdims=True)


def finish_kernel(
    blocks, rides, dq_ref, dk_ref, dv_ref, wq_ref, wk_ref, wv_ref, ridge_ref, basis_ref, earlier_ref, tokens_ref, gh_ref,
    gain_ref, gain_m_ref, maps_ref, here_ref, gt_ref, gc_ref, small_ref, fit_ref, grad_ref,
):
    step = pl.program_id(0)
    length = ridge_ref.shape[1] // 2

    @pl.when(step == 0)
    def _():
        for ride in rides:
            ride.fetch()

    @pl.when(step == blocks + 1)
    def _():
        for ride in rides:
            ride.add()

    part = dot(dk_ref[...], wk_ref[...], 1, 1) + dot(dv_ref[...], wv_ref[...], 1, 1)

    @pl.when(step == 0)
    def _():
        memory = part.astype(bf16)
        samples = dot(ridge_ref[:, :length], memory, 0, 0).astype(bf16)
        gc_ref[...] = here_ref[0] * dot(basis_ref[...], samples, 0, 0)
        fit_ref[...] = dot(ridge_ref[:, length:], memory, 0, 0)
        grad_ref[...] = jnp.zeros_like(grad_ref)

    @pl.when(jnp.logical_and(step > 0, step <= blocks))
    def _():
        past = part + fit_ref[pl.ds(pl.multiple_of((step - 1) * ROWS, ROWS), ROWS), :]
        hat = norm_stats(earlier_ref[...].astype(f32))[0]
        grad_ref[...] += jnp.sum(past * hat, axis=0, keepdims=True)

    @pl.when(step > blocks)
    def _():
        grad = part + dot(dq_ref[...], wq_ref[...], 1, 1)
        hat, inverse = norm_stats(tokens_ref[...].astype(f32))
        grad_ref[...] += jnp.sum(grad * hat, axis=0, keepdims=True)
        gt_ref[...] = gh_ref[...] + norm_back(grad, hat, inverse, gain_ref[...])

    @pl.when(step == 2 * blocks)
    def _():
        small_ref[...] = jnp.zeros_like(small_ref)
        pairs, _, basis_count = maps_ref.shape
        for p in range(pairs):
            small_ref[2 * p : 2 * p + 2, :] = maps_ref[p, 0:2, :]
            small_ref[2 * (pairs + p) : 2 * (pairs + p) + 2, :] = maps_ref[p, 2:4, :]
        for at in range(grad_ref.shape[1] // basis_count):
            cols = slice(at * basis_count, (at + 1) * basis_count)
            row = 4 * pairs + 2 * at
            small_ref[row : row + 1, :] = grad_ref[:, cols]
            small_ref[row + 1 : row + 2, :] = gain_m_ref[:, cols]
        for ride in rides:
            ride.done()


def whole_spec(*shape):
    return pl.BlockSpec(shape, lambda *_: (0,) * len(shape))


def struct(kind, *shape):
    return jax.ShapeDtypeStruct(shape, kind)


def call(kernel, name, grid, in_specs, outs, scratch=(), scalars=1, vmem=24, aliases={}, near=(), near_outs=()):
    def place_of(at, out):
        return out if math.prod(out.shape) <= 1 << 16 or at in near_outs else pltpu.HBM(out.shape, out.dtype)

    run = pl.pallas_call(
        kernel,
        grid_spec=pltpu.PrefetchScalarGridSpec(
            num_scalar_prefetch=scalars,
            grid=grid,
            in_specs=in_specs,
            out_specs=[whole_spec(*out.shape) if spec is None else spec for spec, out in outs],
            scratch_shapes=scratch,
        ),
        out_shape=[place_of(at, out) for at, (_, out) in enumerate(outs)],
        input_output_aliases=aliases,
        compiler_params=pltpu.CompilerParams(vmem_limit_bytes=vmem << 20),
        cost_estimate=pl.CostEstimate(flops=0, bytes_accessed=1 << 20, transcendentals=0),
        name=name,
    )

    def put(at, x):
        return x if x.size <= 1 << 16 or at in near else pltpu.with_memory_space_constraint(x, pltpu.HBM)

    return lambda *args: run(*(put(at, x) for at, x in enumerate(args)))


def row_spec(width):
    return pl.BlockSpec((ROWS, width), lambda s, *_: (s, 0))


def mix(context, tokens, weights, gain):
    length, width = tokens.shape
    some = row_spec(width)
    return call(
        mix_kernel, "mix", (length // ROWS,),
        [some, some, whole_spec(width, width), whole_spec(1, width)],
        [(some, struct(f32, length, width)), (some, struct(bf16, length, width))],
        scalars=0,
        near_outs=(1,),
    )(context, tokens, weights, gain)


def feed(place, normed, normed2, cot, cot2, rest, tile, order):
    length, width = normed.shape
    chips, cores, _, rows, _ = rest.shape
    block = cores * rows
    big = whole_spec(length, width)

    def weights(at):
        return pl.BlockSpec(
            (chips, cores, 1, rows, tile), lambda s, p: (0, 0, (s + 1 + p[2]) % 2, 0, at + p[0])
        )

    anywhere = pl.BlockSpec(memory_space=pl.ANY)
    half = (chips // 2, block, 2 * tile)
    turned = pl.BlockSpec((chips // 2, block, tile), lambda s, p: (0, 0, (s + 1 + p[2]) % 2))
    return call(
        lambda *refs: feed_kernel(order, *refs), "feed", (2,),
        [big, big, big, big, weights(0), weights(2)],
        [
            (None, struct(f32, length, width)),
            (None, struct(bf16, length, width)),
            (None, struct(f32, length, width)),
            (None, struct(bf16, length, width)),
            (anywhere, struct(bf16, chips, block, tile)),
            (anywhere, struct(f32, chips, block, tile)),
            (turned, struct(bf16, *half)),
            (turned, struct(f32, *half)),
        ],
        scratch=[
            pltpu.VMEM((width, 2 * length), bf16),
            pltpu.VMEM((width, 2 * length), bf16),
            pltpu.VMEM((2 * length, tile), bf16),
            pltpu.VMEM((2 * length, tile), bf16),
            pltpu.VMEM((4, length, width), f32),
            pltpu.VMEM((chips, block, tile), bf16),
            pltpu.VMEM((chips, block, tile), f32),
            pltpu.SemaphoreType.DMA((2,)),
        ],
        vmem=44,
        near=(1, 2, 4),
        near_outs=(2, 3),
    )(place, normed, normed2, cot, cot2, rest, rest)


def turn(hidden, gn, gn2, cot, weights, gain):
    length, width = hidden.shape
    some = row_spec(width)
    return call(
        turn_kernel, "turn", (length // ROWS,),
        [some] * 4 + [whole_spec(width, width), whole_spec(1, width)],
        [
            (some, struct(f32, length, width)),
            (None, struct(f32, 1, width)),
            (some, struct(bf16, length, width)),
            (pl.BlockSpec((width, ROWS), lambda s: (0, s)), struct(bf16, width, length)),
        ],
        scalars=0,
        near=(1, 2),
    )(hidden, gn, gn2, cot, weights, gain)


def finish(
    place, dq, dk, dv, weights, ridge, basis, earlier, tokens, grad_hidden, gain, gain_m_grad, maps, here, riders
):
    length, width = tokens.shape
    basis_count = ridge.shape[0]
    blocks = length // ROWS
    small = 4 * maps.shape[0] + 2 * (width // basis_count)
    all_rows = pl.BlockSpec((ROWS, width), lambda s, _: (jnp.where(s == 0, 2 * blocks, s - 1), 0))
    past = pl.BlockSpec((ROWS, width), lambda s, _: (jnp.clip(s - 1, 0, blocks - 1), 0))
    now = pl.BlockSpec((ROWS, width), lambda s, _: (jnp.maximum(s - 1 - blocks, 0), 0))
    args = (gain, gain_m_grad, maps)
    others = Riders(riders)
    outs = [
        (now, struct(f32, length, width)),
        (None, struct(f32, basis_count, width)),
        (None, struct(f32, small + (-small) % 8, basis_count)),
    ]
    scratch = [pltpu.VMEM((length, width), f32), pltpu.VMEM((1, width), f32)]
    ins = 3 + len(weights) + 2 + 3 + 3 + 1

    def kernel(place_ref, *refs):
        out = ins + len(others.arrays)
        room = out + 3 + len(others.outs)
        rides = others.going(place_ref, refs[ins:out], refs[out + 3 : room], refs[room + 2 :])
        finish_kernel(blocks, rides, *refs[:ins], *refs[out : out + 3], *refs[room : room + 2])

    results = call(
        kernel, "finish", (2 * blocks + 1,),
        [now, all_rows, all_rows]
        + [whole_spec(*x.shape) for x in (*weights, ridge, basis)]
        + [past, now, now]
        + [whole_spec(*x.shape) for x in args]
        + [pl.BlockSpec(memory_space=pltpu.SMEM)]
        + others.specs,
        outs + others.outs,
        scratch=scratch + others.scratch,
        vmem=22,
    )(place, dq, dk, dv, *weights, ridge, basis, earlier, tokens, grad_hidden, *args, here, *others.arrays)
    for i, rider in enumerate(riders):
        rider.rode(*results[3 + 2 * i : 5 + 2 * i])
    return results[:3]


class Links:
    def __init__(self, sizes):
        self.chips = sizes["chips"]
        self.bits = self.chips.bit_length()
        self.chip = lax.axis_index("chips")
        self.core = lax.axis_index("core")
        self.side = lax.axis_index("heads")
        self.places = [0, 1, "h"] + list(range(2, self.bits))

    def swap(self, value, stage):
        if stage in ("h", 0):
            return lax.ppermute(value, "heads" if stage == "h" else "core", [(0, 1), (1, 0)])
        mask = 1 << (stage - 1)
        return lax.ppermute(value, "chips", [(i, i ^ mask) for i in range(self.chips)])

    def bit(self, stage):
        if stage == "h":
            return self.side
        return self.core if stage == 0 else (self.chip >> (stage - 1)) & 1

    def gather(self, value, lead, stages, have=()):
        have = list(have)
        for stage in stages:
            other = self.swap(value, stage)
            if stage == "h":
                value = self.gather_with(value, other, stage, None)
            else:
                place = lead + sum(1 for b in have if b > stage)
                value = self.gather_with(value, other, stage, place)
                have.append(stage)
        return value

    def gather_with(self, value, other, stage, axis=0):
        mine_first = self.bit(stage) == 0
        first = jnp.where(mine_first, value, other)
        second = jnp.where(mine_first, other, value)
        if axis is None:
            return jnp.concatenate([first, second], axis=-1)
        return jnp.stack([first, second], axis=axis)

    def whole_rows(self, value, rows):
        value = value.reshape(2, rows, -1)
        mine = lax.dynamic_index_in_dim(value, self.core, 0, keepdims=False)
        other = self.swap(lax.dynamic_index_in_dim(value, 1 - self.core, 0, keepdims=False), 0)
        return self.gather_with(mine, other, 0, None)


def tie(value, *earlier):
    return lax.optimization_barrier((value,) + earlier)[0]


class Chain:
    def __init__(self, links, stages, send, keep, wire=bf16):
        self.links, self.wire = links, wire
        self.stage, self.stages = stages[0], list(stages[1:])
        self.left = [stage for stage in self.stages if stage != "h"]
        self.send, self.keep = self.spread(send), self.spread(keep)

    def spread(self, value):
        return value.reshape((2,) * len(self.left) + value.shape[1:])

    def cut(self):
        keep, came = self.keep, self.came
        self.stage = self.stages.pop(0) if self.stages else None
        if self.stage is None:
            self.value = keep + came.astype(f32)
            return
        bit = self.links.bit(self.stage)
        if self.stage == "h":
            width = keep.shape[-1] // 2
            take = lambda x, b: lax.dynamic_slice_in_dim(x, b * width, width, axis=x.ndim - 1)
        else:
            axis = self.left.index(self.stage)
            self.left.pop(axis)
            take = lambda x, b: lax.dynamic_index_in_dim(x, b, axis, keepdims=False)
        self.send = (take(keep, 1 - bit) + take(came, 1 - bit).astype(f32)).astype(self.wire)
        self.keep = take(keep, bit) + take(came, bit).astype(f32)

    def ride(self):
        self.stage = self.stages.pop(0)
        at = self.links.places.index(self.stage)
        tail = self.keep.shape[len(self.left) :]
        rows, cols = math.prod(tail[:-1]), tail[-1]
        if self.stage == "h":
            whole = (self.keep.size // (rows * cols), rows, cols)
            half = whole[:2] + (cols // 2,)
        else:
            self.left.pop(self.left.index(self.stage))
            whole = (2, self.keep.size // (2 * rows * cols), rows, cols)
            half = whole[1:]
        self.tail = tail[:-1] + half[-1:]
        return self.stage, at, [self.keep.reshape(whole), self.came.reshape(whole)], half

    def join(self, other):
        self.send = jnp.concatenate([self.send, other.send], axis=-1)
        self.keep = jnp.concatenate([self.keep, other.keep], axis=-1)

    def rode(self, send, keep):
        shape = (2,) * len(self.left) + self.tail
        self.send, self.keep = send.reshape(shape), keep.reshape(shape)


def together(values):
    return list(lax.optimization_barrier(tuple(values)))


class Riders:
    def __init__(self, chains):
        self.rides = [chain.ride() for chain in chains]
        anywhere = pl.BlockSpec(memory_space=pl.ANY)
        self.arrays = [x for _, _, arrays, _ in self.rides for x in arrays]
        self.specs = [anywhere] * len(self.arrays)
        self.outs, self.scratch = [], []
        for _, _, _, shape in self.rides:
            self.outs += [(anywhere, struct(bf16, *shape)), (anywhere, struct(f32, *shape))]
            self.scratch += [pltpu.VMEM(shape, kind) for kind in (f32, bf16, f32, bf16)]
            self.scratch += [pltpu.SemaphoreType.DMA((6,))]

    def near(self, first):
        return tuple(first + 1 + 2 * i for i in range(len(self.rides)))

    def going(self, place_ref, ins, outs, scratch):
        return [
            Ride(how, place_ref[at], ins[2 * i : 2 * i + 2], outs[2 * i : 2 * i + 2], scratch[5 * i : 5 * i + 5])
            for i, (how, at, _, _) in enumerate(self.rides)
        ]


def add_up(place, chains):
    others = Riders(chains)

    def kernel(place_ref, *refs):
        out = len(others.arrays)
        room = out + len(others.outs)
        rides = others.going(place_ref, refs[:out], refs[out:room], refs[room:])
        for ride in rides:
            ride.fetch()
        for ride in rides:
            ride.add()
        for ride in rides:
            ride.done()

    results = call(
        kernel, "add_up", (1,), others.specs, others.outs, scratch=others.scratch, vmem=24, near=others.near(1)
    )(place, *others.arrays)
    for i, chain in enumerate(chains):
        chain.rode(*results[2 * i : 2 * i + 2])


def hold(chains, *after):
    came = together([chain.came for chain in chains] + list(after))
    for chain, value in zip(chains, came):
        chain.came = value


def start(chains):
    chains = [chain for chain in chains if chain.stage is not None]
    if chains:
        for chain, send in zip(chains, together([chain.send for chain in chains])):
            chain.send = send
            chain.came = chain.links.swap(send, chain.stage)


def arrive(chains, *after):
    chains = [chain for chain in chains if chain.stage is not None]
    if chains:
        came = together([chain.came for chain in chains] + list(after))
        for chain, value in zip(chains, came):
            chain.came = value
            chain.cut()


def shards(
    tokens, earlier, coeffs, present, sample_at, w_qkv, w_out, w_up, w_down,
    gain_attn, gain_mlp, w_mean, w_var, cotangent, sizes, groups,
):
    links = Links(sizes)
    high = list(range(2, links.bits))
    count = 2 * links.chips
    tokens, earlier, coeffs, cotangent = tokens[0], earlier[0], coeffs[0], cotangent[0]
    length, width = tokens.shape
    basis_count = coeffs.shape[0]
    rows, side = w_qkv.shape[1], w_qkv.shape[2]
    ff_side = w_up.shape[1]
    local_heads, mem_part = w_mean.shape

    rest = jnp.concatenate([w_up, w_down.T], axis=1).astype(bf16)
    rest = lax.all_gather(rest, ("chips", "core", "heads"), axis=0, tiled=False)
    rest = rest.reshape(links.chips, 2, 2, rows, -1)
    tile = ff_side // 2
    small = jnp.concatenate(
        [gain_attn, gain_mlp, w_mean.reshape(-1), w_var.reshape(-1)]
    ).astype(bf16)
    small_size = small.shape[0]
    small = jnp.pad(small, (0, -small_size % LANES)).reshape(1, -1)
    small_h = links.swap(small, "h")
    first = jnp.where(links.side == 0, small, small_h)
    second = jnp.where(links.side == 0, small_h, small)
    far = high[1:][::-1]
    parts = jnp.concatenate([w_qkv, w_out.T[None]], axis=0).astype(bf16)
    parts = links.gather(parts, 1, far)
    small = links.gather(jnp.concatenate([first, second], axis=0), 0, far)
    small, parts = together([small, parts])
    turns = ([2, 1, "h"], [1, "h", 2], ["h", 2, 1], [2, 1, "h"])
    parts = [parts[c] for c in range(4)]
    have = list(far)
    haves = [list(far) for _ in range(4)]
    for step in range(3):
        small = links.gather(small, 0, [2 - step], have)
        have.append(2 - step)
        for c in range(4):
            parts[c] = links.gather(parts[c], 0, [turns[c][step]], haves[c])
            if turns[c][step] != "h":
                haves[c].append(turns[c][step])
        if step < 2:
            small, *parts = together([small] + parts)
    *qkv_full, out_full = [links.gather(parts[c], 0, [0], haves[c]).reshape(width, width) for c in range(4)]
    small = small.reshape(count, 2, -1).astype(f32)
    gain_a = small[:, 0, :rows].reshape(-1)
    gain_m = small[:, 0, rows : 2 * rows].reshape(-1)

    def head_map(start):
        part = small[:, :, start : start + local_heads * mem_part]
        part = part.reshape(count, 2, local_heads, mem_part).transpose(1, 2, 0, 3)
        return part.reshape(local_heads, 2, basis_count)

    mean_full = head_map(2 * rows)
    var_full = head_map(2 * rows + local_heads * mem_part)

    cot2 = links.swap(cotangent, 0)
    place = jnp.stack([links.bit(stage) for stage in links.places]).astype(jnp.int32)

    ridge = ridge_table(basis_count, 2 * length)
    tokens32, earlier32 = tokens.astype(f32), earlier.astype(f32)
    normed = layer_norm(tokens32, gain_a).astype(bf16)
    past = layer_norm(earlier32, gain_a).astype(bf16)
    old_basis = basis_at((sample_at[0].astype(f32) + 0.5) / GRID, basis_count).astype(bf16)
    here = present[0].astype(f32)
    samples = (here * dot(old_basis, coeffs.astype(bf16), 1, 0)).astype(bf16)
    memory = dot(ridge, jnp.concatenate([samples, past], axis=0), 1, 0).astype(bf16)
    sources = jnp.concatenate([past, normed, memory], axis=0)
    queries = dot(normed, qkv_full[0], 1, 0).astype(bf16)
    keys = dot(sources, qkv_full[1], 1, 0).astype(bf16)
    values = dot(sources, qkv_full[2], 1, 0).astype(bf16)
    old_basis, queries = together([old_basis, queries])
    context, lse, turned = attn_forward(queries, keys, values, mean_full, var_full, sources)
    gain_row = gain_m.reshape(1, -1)
    hidden, normed_mlp = mix(context, tokens, out_full, gain_row)
    normed_mlp2 = links.swap(normed_mlp, 0)
    lows = [2] + high[1:]
    order = block_order([1] + lows)
    mlp, mlp2, gn, gn2, down_send, down_keep, up_send, up_keep = feed(
        place, normed_mlp, normed_mlp2, cotangent, cot2, rest, tile, order
    )
    gn2 = links.swap(gn2, 0)
    mlp2 = links.swap(mlp2, 0)
    c_down = Chain(links, ["h", 1] + lows, down_send, down_keep)
    c_up = Chain(links, [1, 2] + high[1:] + ["h"], up_send, up_keep)
    start([c_down, c_up])
    grad_hidden, gain_m_grad, grad_ctx, branch = turn(hidden, gn, gn2, cotangent, out_full, gain_row)

    plans = (["h", 1, 2], [1, "h", 2])
    spans = [list(range(groups - 1)), [groups - 1]]
    feeds, c_qkv = [c_down, c_up], []
    into = ()
    for group in range(groups):
        late = group == groups - 1
        plan = plans[late] + high[1:]
        if late:
            into = into[:4]
        riders = c_qkv if late else feeds if group == 1 else []
        if riders:
            hold(riders, into[0])
        into = attn_backward(
            place, queries, keys, values, mean_full, var_full, lse, grad_ctx, context, turned, branch, group, groups,
            block_order([b for b in plan if b != "h"]), rows, spans[late], into, riders,
        )
        if group == spans[late][-1]:
            c_qkv = c_qkv + [Chain(links, [0] + plan, into[4], into[5])]
        sends = [c.send for c in riders]
        if not late:
            start(riders)
            if c_qkv:
                c_qkv[0].send = tie(c_qkv[0].send, *sends)
                start(c_qkv)
                sends = [c_qkv[0].send]
        grad_ctx = tie(grad_ctx, into[0], *sends)
    arrive(feeds, into[0])
    chains = feeds + c_qkv
    last = chains[-1]
    last.send = tie(last.send, *[c.send for c in feeds])
    start([last])
    start(chains[:-1])
    arrive([last])
    start([last])
    dq, dk, dv, maps = into[:4]
    dq = tie(dq, *[c.send for c in chains])
    grad_tokens, grad_coeffs, tiny = finish(
        place, dq, dk, dv, qkv_full, ridge, old_basis, earlier, tokens, grad_hidden, gain_a.reshape(1, -1),
        gain_m_grad, maps, here.reshape(1), [],
    )

    def add(value, stage):
        return value + links.swap(value, stage)

    tiny_stages = [["h", 1]] + [[stage] for stage in lows]
    hold(chains, tiny)
    add_up(place, chains)
    tiny = tie(tiny, *[c.send for c in chains])
    output = (tie(hidden, tiny) + (mlp + mlp2.astype(f32))).astype(bf16)
    tiny = add(tiny, 0)
    joined = False

    def pick(tiny):
        heads = 2 * local_heads
        item = 2 * links.chip + links.core
        pick_map = lambda first: lax.dynamic_slice(
            tiny, (first + local_heads * links.side, item * mem_part), (local_heads, mem_part)
        )
        mean_out, var_out = pick_map(0), pick_map(heads)
        gains = tiny[2 * heads : 2 * heads + 2 * (width // basis_count)].reshape(-1, 2, basis_count)
        gain_part = width // (2 * count)
        pick_gain = lambda at: lax.dynamic_slice(
            gains[:, at].reshape(-1), ((2 * item + links.side) * gain_part,), (gain_part,)
        )
        gain_a_out, gain_m_out = pick_gain(0), pick_gain(1)
        return gain_a_out, gain_m_out, mean_out, var_out

    while tiny_stages or any(chain.stage is not None for chain in chains):
        going = [c for c in chains if c.stage is not None]
        start(going)
        for stage in tiny_stages.pop(0) if tiny_stages else []:
            tiny = add(tiny, stage)
        if tiny_stages or len(going) > 1:
            *came, tiny = together([c.came for c in going] + [tiny])
            for chain, value in zip(going, came):
                chain.came = value
        on = [c for c in going if c.stages]
        ends = [c for c in going if not c.stages]
        for chain in on:
            chain.cut()
        if not joined:
            joined = True
            c_qkv[0].join(c_qkv[1])
            chains.remove(c_qkv[1])
            on = [c for c in on if c is not c_qkv[1]]
        if on and ends:
            hold(ends, *[c.send for c in on])
        elif ends and not tiny_stages:
            small_out = pick(tiny)
            hold(ends, *small_out)
        for chain in ends:
            chain.cut()
    r_down, r_up = links.whole_rows(c_down.value, rows), links.whole_rows(c_up.value, rows)
    r_proj = c_qkv[0].value
    return (
        output[None],
        grad_tokens[None],
        grad_coeffs[None],
        r_proj[:3],
        r_proj[3].T,
        r_up,
        r_down.T,
        *small_out,
    )


def solution(mesh):
    sizes = dict(mesh.shape)
    both = ("items", "heads")
    in_specs = (
        P(both, None, None),
        P(both, None, None),
        P(both, None, None),
        P(both),
        P(both, None),
        P(None, "items", "heads"),
        P("heads", "items"),
        P("items", "heads"),
        P("heads", "items"),
        P("items"),
        P("items"),
        P("heads", "items"),
        P("heads", "items"),
        P(both, None, None),
    )
    out_specs = (
        P(both, None, None),
        P(both, None, None),
        P(both, None, None),
        P(None, "items", "heads"),
        P("heads", "items"),
        P("items", "heads"),
        P("heads", "items"),
        P(both),
        P(both),
        P("heads", "items"),
        P("heads", "items"),
    )

    chips = sizes["items"] // 2
    split = Mesh(mesh.devices.reshape(chips, 2, sizes["heads"]), ("chips", "core", "heads"))

    def respec(spec):
        def axis(entry):
            names = entry if isinstance(entry, tuple) else (entry,)
            flat = tuple(n for name in names for n in (("chips", "core") if name == "items" else (name,)))
            return flat if flat != (None,) else None

        return P(*(axis(entry) for entry in spec))

    def body(*args):
        return shards(*args, sizes=dict(split.shape), groups=3)

    return jax.shard_map(
        body,
        mesh=split,
        in_specs=tuple(respec(spec) for spec in in_specs),
        out_specs=tuple(respec(spec) for spec in out_specs),
        check_vma=False,
    )
```

```python
import math

import jax
import jax.numpy as jnp
import numpy as np
from jax import lax
from jax.experimental import pallas as pl
from jax.experimental.pallas import tpu as pltpu
from jax.sharding import Mesh
from jax.sharding import PartitionSpec as P

HD = 64
GRID = 1024
EPSILON = 1e-05
VAR_SCALE = 0.01
RIDGE = 1.0
LANES = 128
ROWS = 256
NEG = -1e30
bf16 = jnp.bfloat16
f32 = jnp.float32


def dot(a, b, ca, cb):
    return lax.dot_general(a, b, (((ca,), (cb,)), ((), ())), preferred_element_type=f32)


def layer_norm(values, gain_vec):
    row_mean = jnp.mean(values, axis=-1, keepdims=True)
    centred = values - row_mean
    spread = jnp.mean(centred * centred, axis=-1, keepdims=True)
    return centred * lax.rsqrt(spread + EPSILON) * gain_vec


def basis_at(points, basis_count):
    centers = (jnp.arange(basis_count, dtype=f32) + 0.5) / basis_count
    offset = points[..., None] - centers
    return jnp.exp(-offset * offset * (0.5 * basis_count * basis_count))


def ridge_table(basis_count, samples):
    points = (np.arange(samples) + 0.5) / samples
    centers = (np.arange(basis_count) + 0.5) / basis_count
    design = np.exp(-((points[:, None] - centers) ** 2) * (0.5 * basis_count * basis_count))
    gram = design.T @ design + RIDGE * np.eye(basis_count)
    factor = np.linalg.cholesky(gram)
    table = np.linalg.solve(factor.T, np.linalg.solve(factor, design.T))
    return jnp.asarray(table.astype(np.float32)).astype(bf16)


def gelu_tanh(values):
    return jax.nn.gelu(values, approximate=True)


def near_scores(q_rows, keys, block):
    reach = keys.shape[0] // 2 + (block + 1) * ROWS
    scores = dot(q_rows, keys[:reach], 1, 1)
    row = lax.broadcasted_iota(jnp.int32, (q_rows.shape[0], ROWS), 0) % ROWS
    col = lax.broadcasted_iota(jnp.int32, (q_rows.shape[0], ROWS), 1)
    edge = jnp.where(col <= row, scores[:, reach - ROWS :], NEG)
    return jnp.concatenate([scores[:, : reach - ROWS], edge], axis=1), reach


def both_heads(x, half):
    none = jnp.zeros_like(x)
    return jnp.concatenate([jnp.where(half, x, none), jnp.where(half, none, x)], axis=0)


def by_head(ref, rows):
    return jnp.concatenate(
        [jnp.broadcast_to(ref[0, head : head + 1, :], (rows, ref.shape[2])) for head in range(2)], axis=0
    )


def density_parts(scaled, w_mean, w_var):
    basis_count = scaled.shape[1]
    index = lax.broadcasted_iota(jnp.int32, (1, basis_count), 1).astype(f32)
    centers = (index + 0.5) / basis_count
    middle = jax.nn.sigmoid(jnp.sum(scaled * w_mean, axis=1, keepdims=True))
    var_raw = jnp.sum(scaled * w_var, axis=1, keepdims=True)
    softplus = jnp.maximum(var_raw, 0.0) + jnp.log1p(jnp.exp(-jnp.abs(var_raw)))
    variance = VAR_SCALE * softplus + 1.0 / (basis_count * basis_count)
    offset = middle - centers
    inv_var = 1.0 / variance
    square = offset * offset * inv_var
    scale = lax.rsqrt(2.0 * math.pi * variance) / basis_count
    weights = jnp.exp(-0.5 * square) * scale
    return weights, middle, var_raw, inv_var, offset, square


def attn_fwd_kernel(
    q_ref, k_ref, v_ref, mk_ref, mv_ref, wm_ref, wv_ref, rows_ref, ctx_ref, lse_ref, turned_ref
):
    turned_ref[...] = rows_ref[...].T
    half = lax.broadcasted_iota(jnp.int32, (1, LANES), 1) < HD
    length = q_ref.shape[0]
    keys, values = k_ref[...], v_ref[...]
    mem_keys, mem_values = mk_ref[...], mv_ref[...]
    w_mean, w_var = by_head(wm_ref, ROWS), by_head(wv_ref, ROWS)
    for block in range(length // ROWS):
        rows = slice(block * ROWS, (block + 1) * ROWS)
        q_both = both_heads(q_ref[rows, :] * jnp.asarray(0.125, bf16), half)
        scores, reach = near_scores(q_both, keys, block)
        top = jnp.max(scores, axis=1, keepdims=True)
        raw = jnp.exp(scores - top)
        total = jnp.sum(raw, axis=1, keepdims=True)
        near = dot((raw * (1.0 / total)).astype(bf16), values[:reach], 1, 0)
        weights = density_parts(dot(q_both, mem_keys, 1, 1), w_mean, w_var)[0]
        out = near + dot(weights.astype(bf16), mem_values, 1, 0)
        logs = top + jnp.log(total)
        ctx_ref[rows, :] = jnp.where(half, out[:ROWS], out[ROWS:]).astype(bf16)
        lse_ref[rows, :] = jnp.where(half, logs[:ROWS], logs[ROWS:])


def attn_bwd_kernel(
    order, rows_own, place_ref,
    q_ref, k_ref, v_ref, mk_ref, mv_ref, wm_ref, wv_ref, lse_ref, do_ref, ctx_ref, far_turned_ref, far_branch_ref,
    dq_ref, dk_ref, dv_ref, maps_ref, send_ref, keep_ref, acck_ref, accv_ref, turned_ref, branch_ref, sems, rides,
):
    fetches = (
        pltpu.make_async_copy(far_turned_ref, turned_ref, sems.at[0]),
        pltpu.make_async_copy(far_branch_ref, branch_ref, sems.at[1]),
    )

    @pl.when(pl.program_id(0) == 0)
    def _():
        for fetch in fetches:
            fetch.start()
        for ride in rides:
            ride.fetch()

    @pl.when(pl.program_id(0) == 1)
    def _():
        for ride in rides:
            ride.add()

    half = lax.broadcasted_iota(jnp.int32, (1, LANES), 1) < HD
    length = q_ref.shape[0]
    near_rows = k_ref.shape[0]
    keys, values = k_ref[...], v_ref[...]
    mem_keys, mem_values = mk_ref[...], mv_ref[...]
    both = lambda x: both_heads(x, half)
    w_mean, w_var = by_head(wm_ref, length), by_head(wv_ref, length)
    early = near_rows - ROWS
    q_full, do_full = q_ref[...], do_ref[...]
    q_turn, do_turn = q_full.T, do_full.T
    q_both = both(q_full * jnp.asarray(0.125, bf16))
    do_both = both(do_full)

    def late(x):
        return jnp.concatenate([x[ROWS:length], x[length + ROWS :]], axis=0)

    row = lax.broadcasted_iota(jnp.int32, (2 * length, ROWS), 0) % length
    col = lax.broadcasted_iota(jnp.int32, (2 * length, ROWS), 1)
    scores = dot(q_both, keys[:early], 1, 1)
    edge = jnp.where(col <= row, scores[:, early - ROWS :], NEG)
    scores = jnp.concatenate([scores[:, : early - ROWS], edge], axis=1)
    row = lax.broadcasted_iota(jnp.int32, (length, ROWS), 0) % ROWS
    col = lax.broadcasted_iota(jnp.int32, (length, ROWS), 1)
    tail = jnp.where(col <= row, dot(late(q_both), keys[early:], 1, 1), NEG)
    lse = jnp.concatenate([lse_ref[:, 0:1], lse_ref[:, HD : HD + 1]], axis=0)
    probs, probs_tail = jnp.exp(scores - lse), jnp.exp(tail - late(lse))
    grad_probs = dot(do_both, values[:early], 1, 1)
    grad_tail = dot(late(do_both), values[early:], 1, 1)
    inner = jnp.sum(probs * grad_probs, axis=1, keepdims=True)
    more = jnp.sum(probs_tail * grad_tail, axis=1, keepdims=True)
    inner_late = late(inner) + more
    inner = jnp.concatenate(
        [inner[:ROWS], inner_late[:ROWS], inner[length : length + ROWS], inner_late[ROWS:]], axis=0
    )
    grad_raw = (0.125 * probs * (grad_probs - inner)).astype(bf16)
    raw_tail = (0.125 * probs_tail * (grad_tail - inner_late)).astype(bf16)
    probs_low, low_tail = probs.astype(bf16), probs_tail.astype(bf16)
    scaled = dot(q_both, mem_keys, 1, 1)
    weights, middle, var_raw, inv_var, offset, square = density_parts(scaled, w_mean, w_var)
    grad_w = dot(do_both, mem_values, 1, 1) * weights
    d_mid = -jnp.sum(grad_w * offset, axis=1, keepdims=True) * inv_var
    d_var = jnp.sum(grad_w * (square - 1.0), axis=1, keepdims=True) * (0.5 * inv_var)
    d_mid = d_mid * middle * (1.0 - middle)
    d_var = d_var * VAR_SCALE * jax.nn.sigmoid(var_raw)
    gm, gv = scaled * d_mid, scaled * d_var
    grad_mem = (0.125 * (d_mid * w_mean + d_var * w_var)).astype(bf16)
    weights_low = weights.astype(bf16)
    out = dot(grad_raw, keys[:early], 1, 0) + dot(grad_mem, mem_keys, 1, 0)
    out_tail = dot(raw_tail, keys[early:], 1, 0)
    for head in range(2):
        part = slice(head * HD, (head + 1) * HD)
        mine = slice(head * length, (head + 1) * length)
        ends = slice(head * ROWS, (head + 1) * ROWS)
        acck_ref[part, :early] = dot(q_turn[part], grad_raw[mine], 1, 0)
        accv_ref[part, :early] = dot(do_turn[part], probs_low[mine], 1, 0)
        acck_ref[part, early:near_rows] = dot(q_turn[part, ROWS:], raw_tail[ends], 1, 0)
        accv_ref[part, early:near_rows] = dot(do_turn[part, ROWS:], low_tail[ends], 1, 0)
        acck_ref[part, near_rows:] = dot(q_turn[part], grad_mem[mine], 1, 0)
        accv_ref[part, near_rows:] = dot(do_turn[part], weights_low[mine], 1, 0)
        maps_ref[0, head : head + 1, :] = jnp.sum(gm[mine], axis=0, keepdims=True)
        maps_ref[0, 2 + head : 3 + head, :] = jnp.sum(gv[mine], axis=0, keepdims=True)
    dq_ref[:ROWS, :] = jnp.where(half, out[:ROWS], out[length : length + ROWS]).astype(bf16)
    out = late(out) + out_tail
    dq_ref[ROWS:, :] = jnp.where(half, out[:ROWS], out[ROWS:]).astype(bf16)
    dk_ref[...] = acck_ref[...].T.astype(bf16)
    dv_ref[...] = accv_ref[...].T.astype(bf16)

    @pl.when(pl.program_id(0) == 0)
    def _():
        for fetch in fetches:
            fetch.wait()

    turned = turned_ref[...]
    grads = (
        dot(turned[:, length : 2 * length], dq_ref[...], 1, 0),
        dot(turned, dk_ref[...], 1, 0),
        dot(turned, dv_ref[...], 1, 0),
        dot(branch_ref[...], ctx_ref[...], 1, 0),
    )
    for at, grad in enumerate(grads):
        send, keep = cut_core(grad, place_ref[0], rows_own, order)
        send_ref[:, at], keep_ref[:, at] = send.astype(bf16), keep

    @pl.when(pl.program_id(0) == pl.num_programs(0) - 1)
    def _():
        for ride in rides:
            ride.done()


class Ride:
    def __init__(self, cut, bit, ins, outs, scratch):
        keep, came = ins
        width = keep.shape[-1] // 2

        def half(ref, b):
            return ref.at[:, :, pl.ds(pl.multiple_of(b * width, LANES), width)] if cut == "h" else ref.at[b]

        self.far, self.near, sems = scratch[:2], scratch[2:4], scratch[4]
        copy = pltpu.make_async_copy
        self.fetches = [
            copy(half(keep, 1 - bit), scratch[0], sems.at[0]),
            copy(half(came, 1 - bit), scratch[1], sems.at[1]),
            copy(half(keep, bit), scratch[2], sems.at[2]),
            copy(half(came, bit), scratch[3], sems.at[3]),
        ]
        self.writes = [copy(scratch[1], outs[0], sems.at[4]), copy(scratch[2], outs[1], sems.at[5])]

    def fetch(self):
        for one in self.fetches:
            one.start()

    def add(self):
        for one in self.fetches:
            one.wait()
        keep, came = self.far
        came[...] = (keep[...] + came[...].astype(f32)).astype(bf16)
        keep, came = self.near
        keep[...] = keep[...] + came[...].astype(f32)
        for one in self.writes:
            one.start()

    def done(self):
        for one in self.writes:
            one.wait()


def attn_specs(length, basis_count, place):
    near_rows = 2 * length
    near = pl.BlockSpec((near_rows, LANES), lambda p, *_: (0, place(p)))
    far = pl.BlockSpec((basis_count, LANES), lambda p, *_: (near_rows // basis_count, place(p)))
    maps = pl.BlockSpec((1, 2, basis_count), lambda p, *_: (place(p), 0, 0))
    return [pl.BlockSpec((length, LANES), lambda p, *_: (0, place(p))), near, near, far, far, maps, maps]


def attn_forward(queries, keys, values, w_mean, w_var, rows):
    length, width = queries.shape
    basis_count = w_mean.shape[-1]
    pairs = width // LANES
    size = rows.shape[0]
    ours = pl.BlockSpec((length, LANES), lambda p: (0, p))
    return call(
        attn_fwd_kernel, "attn_forward", (pairs,),
        attn_specs(length, basis_count, lambda p: p) + [pl.BlockSpec((size, LANES), lambda p: (0, p))],
        [
            (ours, struct(bf16, length, width)),
            (ours, struct(f32, length, width)),
            (pl.BlockSpec((LANES, size), lambda p: (p, 0)), struct(bf16, width, size)),
        ],
        scalars=0,
        near=tuple(range(8)),
    )(queries, keys, values, keys, values, w_mean, w_var, rows)


def attn_backward(
    place, queries, keys, values, w_mean, w_var, lse, grad_ctx, context, turned, branch, group, groups, order, rows,
    span, into, riders,
):
    length, width = queries.shape
    basis_count = w_mean.shape[-1]
    pairs = width // LANES
    count = pairs // groups
    where = lambda p: p * groups + group
    all_rows = keys.shape[0]
    ours = lambda size: pl.BlockSpec((size, LANES), lambda p, _: (0, where(p)))
    cut = (len(order), 4, rows)
    mine = pl.BlockSpec(cut + (LANES,), lambda p, _: (0, 0, 0, p * len(span) + group - span[0]))
    specs = attn_specs(length, basis_count, where) + [ours(length)] * 3
    specs += [pl.BlockSpec(memory_space=pl.ANY)] * 2
    held = [pl.BlockSpec(memory_space=pl.ANY)] * len(into)

    others = Riders(riders)
    outs = [
        (ours(length), struct(bf16, length, width)),
        (ours(all_rows), struct(bf16, all_rows, width)),
        (ours(all_rows), struct(bf16, all_rows, width)),
        (pl.BlockSpec((1, 4, basis_count), lambda p, _: (where(p), 0, 0)), struct(f32, pairs, 4, basis_count)),
        (mine, struct(bf16, *cut, count * LANES * len(span))),
        (mine, struct(f32, *cut, count * LANES * len(span))),
    ]
    scratch = [
        pltpu.VMEM((LANES, all_rows), f32),
        pltpu.VMEM((LANES, all_rows), f32),
        pltpu.VMEM(turned.shape, bf16),
        pltpu.VMEM(branch.shape, bf16),
        pltpu.SemaphoreType.DMA((2,)),
    ]
    own = (1 + len(specs), len(outs), len(scratch))

    def kernel(*refs):
        first = own[0] + len(into)
        out = first + len(others.arrays)
        room = out + own[1] + len(others.outs)
        rides = others.going(refs[0], refs[first:out], refs[out + own[1] : room], refs[room + own[2] :])
        attn_bwd_kernel(order, rows, *refs[: own[0]], *refs[out : out + own[1]], *refs[room : room + own[2]], rides)

    results = call(
        kernel, "attn_backward", (count,),
        specs + held + others.specs,
        outs + others.outs,
        scratch=scratch + others.scratch,
        vmem=32 if riders else 22,
        aliases={own[0] + i: i for i in range(len(into))},
        near=tuple(range(own[0], own[0] + len(into))) + others.near(own[0] + len(into)),
    )(
        place, queries, keys, values, keys, values, w_mean, w_var, lse, grad_ctx, context, turned, branch, *into,
        *others.arrays,
    )
    for i, rider in enumerate(riders):
        rider.rode(*results[own[1] + 2 * i : own[1] + 2 * i + 2])
    return results[: own[1]]


def norm_stats(values):
    centred = values - jnp.mean(values, axis=-1, keepdims=True)
    spread = jnp.mean(centred * centred, axis=-1, keepdims=True)
    inverse = lax.rsqrt(spread + EPSILON)
    return centred * inverse, inverse


def norm_back(grad, hat, inverse, gain):
    scaled = grad * gain
    inner = jnp.mean(scaled * hat, axis=-1, keepdims=True)
    return inverse * (scaled - jnp.mean(scaled, axis=-1, keepdims=True) - hat * inner)


def side_block(ref):
    chips, cores, _, rows, cols = ref.shape
    return ref[...].reshape(chips * cores * rows, cols)


def block_order(bits):
    chips = []
    for place in range(1 << len(bits)):
        chip = 0
        for at, bit in enumerate(reversed(bits)):
            chip |= ((place >> at) & 1) << (bit - 1)
        chips.append(chip)
    return chips


def cut_core(value, core, rows, order):
    split = value.reshape(value.shape[0] // (2 * rows), 2, rows, value.shape[1])
    low = jnp.stack([split[chip, 0] for chip in order])
    high = jnp.stack([split[chip, 1] for chip in order])
    return jnp.where(core == 0, high, low), jnp.where(core == 0, low, high)


def mix_kernel(ctx_ref, tokens_ref, w_ref, gain_ref, hidden_ref, normed_ref):
    hidden = tokens_ref[...].astype(f32) + dot(ctx_ref[...], w_ref[...], 1, 1)
    hidden_ref[...] = hidden
    normed_ref[...] = (norm_stats(hidden)[0] * gain_ref[...]).astype(bf16)


def feed_kernel(
    order, place_ref, normed_ref, normed2_ref, cot_ref, cot2_ref, up_ref, down_ref,
    mlp_ref, mlp2_ref, gn_ref, gn2_ref, down_send_ref, down_keep_ref, up_send_ref, up_keep_ref,
    nt_ref, ct_ref, act_ref, pre_ref, acc_ref, near_send_ref, near_keep_ref, sems,
):
    step = pl.program_id(0)
    length, width = normed_ref.shape
    block = up_ref.shape[1] * up_ref.shape[3]
    w_up, w_down = side_block(up_ref), side_block(down_ref)
    slope = math.sqrt(2.0 / math.pi)

    @pl.when(step == 0)
    def _():
        nt_ref[:, :length] = normed_ref[...].T
        nt_ref[:, length:] = normed2_ref[...].T
        ct_ref[:, :length] = cot_ref[...].T
        ct_ref[:, length:] = cot2_ref[...].T

    for half in range(2):
        rows = slice(half * length, (half + 1) * length)
        normed = (normed_ref, normed2_ref)[half][...]
        cot = (cot_ref, cot2_ref)[half][...]
        pre = dot(normed, w_up, 1, 0)
        square = pre * pre
        bend = jnp.tanh(slope * pre * (1.0 + 0.044715 * square))
        lift = 0.5 + 0.5 * bend
        act = (pre * lift).astype(bf16)
        rise = lift + 0.5 * pre * (1.0 - bend * bend) * (slope + (3.0 * 0.044715 * slope) * square)
        grad_pre = (dot(cot, w_down, 1, 0) * rise).astype(bf16)
        act_ref[rows, :] = act
        pre_ref[rows, :] = grad_pre
        mlp = dot(act, w_down, 1, 1)
        grad_normed = dot(grad_pre, w_up, 1, 1)

        @pl.when(step == 0)
        def _():
            acc_ref[2 * half] = mlp
            acc_ref[2 * half + 1] = grad_normed

        @pl.when(step == 1)
        def _():
            if half == 0:
                mlp_ref[...] = acc_ref[0] + mlp
                gn_ref[...] = acc_ref[1] + grad_normed
            else:
                mlp2_ref[...] = (acc_ref[2] + mlp).astype(bf16)
                gn2_ref[...] = (acc_ref[3] + grad_normed).astype(bf16)

    sent = pltpu.make_async_copy(near_send_ref, down_send_ref, sems.at[0])
    kept = pltpu.make_async_copy(near_keep_ref, down_keep_ref, sems.at[1])
    g_down = dot(ct_ref[...], act_ref[...], 1, 0).reshape(width // block, block, -1)
    g_down = jnp.stack([g_down[chip] for chip in order])

    @pl.when(step == 0)
    def _():
        near_send_ref[...] = g_down.astype(bf16)
        sent.start()

    @pl.when(step == 1)
    def _():
        near_keep_ref[...] = g_down
        kept.start()

    g_up = dot(nt_ref[...], pre_ref[...], 1, 0).reshape(width // block, block, -1)
    low = jnp.stack([g_up[chip] for chip in order[: len(order) // 2]])
    high = jnp.stack([g_up[chip] for chip in order[len(order) // 2 :]])
    first = place_ref[1] == 0
    up_send_ref[...] = jnp.where(first, high, low).astype(bf16)
    up_keep_ref[...] = jnp.where(first, low, high)

    @pl.when(step == 1)
    def _():
        sent.wait()
        kept.wait()


def turn_kernel(
    hidden_ref, gn_ref, gn2_ref, cot_ref, w_ref, gain_ref, gh_ref, gain_grad_ref, gc_ref, branch_ref
):
    step = pl.program_id(0)
    hidden = hidden_ref[...]
    hat, inverse = norm_stats(hidden)
    grad = gn_ref[...] + gn2_ref[...].astype(f32)
    grad_hidden = cot_ref[...].astype(f32) + norm_back(grad, hat, inverse, gain_ref[...])
    gh_ref[...] = grad_hidden
    branch = grad_hidden.astype(bf16)
    branch_ref[...] = branch.T
    gc_ref[...] = dot(branch, w_ref[...], 1, 0).astype(bf16)

    @pl.when(step == 0)
    def _():
        gain_grad_ref[...] = jnp.zeros_like(gain_grad_ref)

    gain_grad_ref[...] += jnp.sum(grad * hat, axis=0, keepdims=True)


def finish_kernel(
    blocks, rides, dq_ref, dk_ref, dv_ref, wq_ref, wk_ref, wv_ref, ridge_ref, basis_ref, earlier_ref, tokens_ref, gh_ref,
    gain_ref, gain_m_ref, maps_ref, here_ref, gt_ref, gc_ref, small_ref, fit_ref, grad_ref,
):
    step = pl.program_id(0)
    length = ridge_ref.shape[1] // 2

    @pl.when(step == 0)
    def _():
        for ride in rides:
            ride.fetch()

    @pl.when(step == blocks + 1)
    def _():
        for ride in rides:
            ride.add()

    part = dot(dk_ref[...], wk_ref[...], 1, 1) + dot(dv_ref[...], wv_ref[...], 1, 1)

    @pl.when(step == 0)
    def _():
        memory = part.astype(bf16)
        samples = dot(ridge_ref[:, :length], memory, 0, 0).astype(bf16)
        gc_ref[...] = here_ref[0] * dot(basis_ref[...], samples, 0, 0)
        fit_ref[...] = dot(ridge_ref[:, length:], memory, 0, 0)
        grad_ref[...] = jnp.zeros_like(grad_ref)

    @pl.when(jnp.logical_and(step > 0, step <= blocks))
    def _():
        past = part + fit_ref[pl.ds(pl.multiple_of((step - 1) * ROWS, ROWS), ROWS), :]
        hat = norm_stats(earlier_ref[...].astype(f32))[0]
        grad_ref[...] += jnp.sum(past * hat, axis=0, keepdims=True)

    @pl.when(step > blocks)
    def _():
        grad = part + dot(dq_ref[...], wq_ref[...], 1, 1)
        hat, inverse = norm_stats(tokens_ref[...].astype(f32))
        grad_ref[...] += jnp.sum(grad * hat, axis=0, keepdims=True)
        gt_ref[...] = gh_ref[...] + norm_back(grad, hat, inverse, gain_ref[...])

    @pl.when(step == 2 * blocks)
    def _():
        small_ref[...] = jnp.zeros_like(small_ref)
        pairs, _, basis_count = maps_ref.shape
        for p in range(pairs):
            small_ref[2 * p : 2 * p + 2, :] = maps_ref[p, 0:2, :]
            small_ref[2 * (pairs + p) : 2 * (pairs + p) + 2, :] = maps_ref[p, 2:4, :]
        for at in range(grad_ref.shape[1] // basis_count):
            cols = slice(at * basis_count, (at + 1) * basis_count)
            row = 4 * pairs + 2 * at
            small_ref[row : row + 1, :] = grad_ref[:, cols]
            small_ref[row + 1 : row + 2, :] = gain_m_ref[:, cols]
        for ride in rides:
            ride.done()


def whole_spec(*shape):
    return pl.BlockSpec(shape, lambda *_: (0,) * len(shape))


def struct(kind, *shape):
    return jax.ShapeDtypeStruct(shape, kind)


def call(kernel, name, grid, in_specs, outs, scratch=(), scalars=1, vmem=24, aliases={}, near=(), near_outs=()):
    def place_of(at, out):
        return out if math.prod(out.shape) <= 1 << 16 or at in near_outs else pltpu.HBM(out.shape, out.dtype)

    run = pl.pallas_call(
        kernel,
        grid_spec=pltpu.PrefetchScalarGridSpec(
            num_scalar_prefetch=scalars,
            grid=grid,
            in_specs=in_specs,
            out_specs=[whole_spec(*out.shape) if spec is None else spec for spec, out in outs],
            scratch_shapes=scratch,
        ),
        out_shape=[place_of(at, out) for at, (_, out) in enumerate(outs)],
        input_output_aliases=aliases,
        compiler_params=pltpu.CompilerParams(vmem_limit_bytes=vmem << 20),
        cost_estimate=pl.CostEstimate(flops=0, bytes_accessed=1 << 20, transcendentals=0),
        name=name,
    )

    def put(at, x):
        return x if x.size <= 1 << 16 or at in near else pltpu.with_memory_space_constraint(x, pltpu.HBM)

    return lambda *args: run(*(put(at, x) for at, x in enumerate(args)))


def row_spec(width):
    return pl.BlockSpec((ROWS, width), lambda s, *_: (s, 0))


def mix(context, tokens, weights, gain):
    length, width = tokens.shape
    some = row_spec(width)
    return call(
        mix_kernel, "mix", (length // ROWS,),
        [some, some, whole_spec(width, width), whole_spec(1, width)],
        [(some, struct(f32, length, width)), (some, struct(bf16, length, width))],
        scalars=0,
        near_outs=(1,),
    )(context, tokens, weights, gain)


def feed(place, normed, normed2, cot, cot2, rest, tile, order):
    length, width = normed.shape
    chips, cores, _, rows, _ = rest.shape
    block = cores * rows
    big = whole_spec(length, width)

    def weights(at):
        return pl.BlockSpec(
            (chips, cores, 1, rows, tile), lambda s, p: (0, 0, (s + 1 + p[2]) % 2, 0, at + p[0])
        )

    anywhere = pl.BlockSpec(memory_space=pl.ANY)
    half = (chips // 2, block, 2 * tile)
    turned = pl.BlockSpec((chips // 2, block, tile), lambda s, p: (0, 0, (s + 1 + p[2]) % 2))
    return call(
        lambda *refs: feed_kernel(order, *refs), "feed", (2,),
        [big, big, big, big, weights(0), weights(2)],
        [
            (None, struct(f32, length, width)),
            (None, struct(bf16, length, width)),
            (None, struct(f32, length, width)),
            (None, struct(bf16, length, width)),
            (anywhere, struct(bf16, chips, block, tile)),
            (anywhere, struct(f32, chips, block, tile)),
            (turned, struct(bf16, *half)),
            (turned, struct(f32, *half)),
        ],
        scratch=[
            pltpu.VMEM((width, 2 * length), bf16),
            pltpu.VMEM((width, 2 * length), bf16),
            pltpu.VMEM((2 * length, tile), bf16),
            pltpu.VMEM((2 * length, tile), bf16),
            pltpu.VMEM((4, length, width), f32),
            pltpu.VMEM((chips, block, tile), bf16),
            pltpu.VMEM((chips, block, tile), f32),
            pltpu.SemaphoreType.DMA((2,)),
        ],
        vmem=44,
        near=(1, 2, 4),
        near_outs=(2, 3),
    )(place, normed, normed2, cot, cot2, rest, rest)


def turn(hidden, gn, gn2, cot, weights, gain):
    length, width = hidden.shape
    some = row_spec(width)
    return call(
        turn_kernel, "turn", (length // ROWS,),
        [some] * 4 + [whole_spec(width, width), whole_spec(1, width)],
        [
            (some, struct(f32, length, width)),
            (None, struct(f32, 1, width)),
            (some, struct(bf16, length, width)),
            (pl.BlockSpec((width, ROWS), lambda s: (0, s)), struct(bf16, width, length)),
        ],
        scalars=0,
        near=(1, 2),
    )(hidden, gn, gn2, cot, weights, gain)


def finish(
    place, dq, dk, dv, weights, ridge, basis, earlier, tokens, grad_hidden, gain, gain_m_grad, maps, here, riders
):
    length, width = tokens.shape
    basis_count = ridge.shape[0]
    blocks = length // ROWS
    small = 4 * maps.shape[0] + 2 * (width // basis_count)
    all_rows = pl.BlockSpec((ROWS, width), lambda s, _: (jnp.where(s == 0, 2 * blocks, s - 1), 0))
    past = pl.BlockSpec((ROWS, width), lambda s, _: (jnp.clip(s - 1, 0, blocks - 1), 0))
    now = pl.BlockSpec((ROWS, width), lambda s, _: (jnp.maximum(s - 1 - blocks, 0), 0))
    args = (gain, gain_m_grad, maps)
    others = Riders(riders)
    outs = [
        (now, struct(f32, length, width)),
        (None, struct(f32, basis_count, width)),
        (None, struct(f32, small + (-small) % 8, basis_count)),
    ]
    scratch = [pltpu.VMEM((length, width), f32), pltpu.VMEM((1, width), f32)]
    ins = 3 + len(weights) + 2 + 3 + 3 + 1

    def kernel(place_ref, *refs):
        out = ins + len(others.arrays)
        room = out + 3 + len(others.outs)
        rides = others.going(place_ref, refs[ins:out], refs[out + 3 : room], refs[room + 2 :])
        finish_kernel(blocks, rides, *refs[:ins], *refs[out : out + 3], *refs[room : room + 2])

    results = call(
        kernel, "finish", (2 * blocks + 1,),
        [now, all_rows, all_rows]
        + [whole_spec(*x.shape) for x in (*weights, ridge, basis)]
        + [past, now, now]
        + [whole_spec(*x.shape) for x in args]
        + [pl.BlockSpec(memory_space=pltpu.SMEM)]
        + others.specs,
        outs + others.outs,
        scratch=scratch + others.scratch,
        vmem=22,
    )(place, dq, dk, dv, *weights, ridge, basis, earlier, tokens, grad_hidden, *args, here, *others.arrays)
    for i, rider in enumerate(riders):
        rider.rode(*results[3 + 2 * i : 5 + 2 * i])
    return results[:3]


class Links:
    def __init__(self, sizes):
        self.chips = sizes["chips"]
        self.bits = self.chips.bit_length()
        self.chip = lax.axis_index("chips")
        self.core = lax.axis_index("core")
        self.side = lax.axis_index("heads")
        self.places = [0, 1, "h"] + list(range(2, self.bits))

    def swap(self, value, stage):
        if stage in ("h", 0):
            return lax.ppermute(value, "heads" if stage == "h" else "core", [(0, 1), (1, 0)])
        mask = 1 << (stage - 1)
        return lax.ppermute(value, "chips", [(i, i ^ mask) for i in range(self.chips)])

    def bit(self, stage):
        if stage == "h":
            return self.side
        return self.core if stage == 0 else (self.chip >> (stage - 1)) & 1

    def gather(self, value, lead, stages, have=()):
        have = list(have)
        for stage in stages:
            other = self.swap(value, stage)
            if stage == "h":
                value = self.gather_with(value, other, stage, None)
            else:
                place = lead + sum(1 for b in have if b > stage)
                value = self.gather_with(value, other, stage, place)
                have.append(stage)
        return value

    def gather_with(self, value, other, stage, axis=0):
        mine_first = self.bit(stage) == 0
        first = jnp.where(mine_first, value, other)
        second = jnp.where(mine_first, other, value)
        if axis is None:
            return jnp.concatenate([first, second], axis=-1)
        return jnp.stack([first, second], axis=axis)

    def whole_rows(self, value, rows):
        value = value.reshape(2, rows, -1)
        mine = lax.dynamic_index_in_dim(value, self.core, 0, keepdims=False)
        other = self.swap(lax.dynamic_index_in_dim(value, 1 - self.core, 0, keepdims=False), 0)
        return self.gather_with(mine, other, 0, None)


def tie(value, *earlier):
    return lax.optimization_barrier((value,) + earlier)[0]


class Chain:
    def __init__(self, links, stages, send, keep, wire=bf16):
        self.links, self.wire = links, wire
        self.stage, self.stages = stages[0], list(stages[1:])
        self.left = [stage for stage in self.stages if stage != "h"]
        self.send, self.keep = self.spread(send), self.spread(keep)

    def spread(self, value):
        return value.reshape((2,) * len(self.left) + value.shape[1:])

    def cut(self):
        keep, came = self.keep, self.came
        self.stage = self.stages.pop(0) if self.stages else None
        if self.stage is None:
            self.value = keep + came.astype(f32)
            return
        bit = self.links.bit(self.stage)
        if self.stage == "h":
            width = keep.shape[-1] // 2
            take = lambda x, b: lax.dynamic_slice_in_dim(x, b * width, width, axis=x.ndim - 1)
        else:
            axis = self.left.index(self.stage)
            self.left.pop(axis)
            take = lambda x, b: lax.dynamic_index_in_dim(x, b, axis, keepdims=False)
        self.send = (take(keep, 1 - bit) + take(came, 1 - bit).astype(f32)).astype(self.wire)
        self.keep = take(keep, bit) + take(came, bit).astype(f32)

    def ride(self):
        self.stage = self.stages.pop(0)
        at = self.links.places.index(self.stage)
        tail = self.keep.shape[len(self.left) :]
        rows, cols = math.prod(tail[:-1]), tail[-1]
        if self.stage == "h":
            whole = (self.keep.size // (rows * cols), rows, cols)
            half = whole[:2] + (cols // 2,)
        else:
            self.left.pop(self.left.index(self.stage))
            whole = (2, self.keep.size // (2 * rows * cols), rows, cols)
            half = whole[1:]
        self.tail = tail[:-1] + half[-1:]
        return self.stage, at, [self.keep.reshape(whole), self.came.reshape(whole)], half

    def join(self, other):
        self.send = jnp.concatenate([self.send, other.send], axis=-1)
        self.keep = jnp.concatenate([self.keep, other.keep], axis=-1)

    def rode(self, send, keep):
        shape = (2,) * len(self.left) + self.tail
        self.send, self.keep = send.reshape(shape), keep.reshape(shape)


def together(values):
    return list(lax.optimization_barrier(tuple(values)))


class Riders:
    def __init__(self, chains):
        self.rides = [chain.ride() for chain in chains]
        anywhere = pl.BlockSpec(memory_space=pl.ANY)
        self.arrays = [x for _, _, arrays, _ in self.rides for x in arrays]
        self.specs = [anywhere] * len(self.arrays)
        self.outs, self.scratch = [], []
        for _, _, _, shape in self.rides:
            self.outs += [(anywhere, struct(bf16, *shape)), (anywhere, struct(f32, *shape))]
            self.scratch += [pltpu.VMEM(shape, kind) for kind in (f32, bf16, f32, bf16)]
            self.scratch += [pltpu.SemaphoreType.DMA((6,))]

    def near(self, first):
        return tuple(first + 1 + 2 * i for i in range(len(self.rides)))

    def going(self, place_ref, ins, outs, scratch):
        return [
            Ride(how, place_ref[at], ins[2 * i : 2 * i + 2], outs[2 * i : 2 * i + 2], scratch[5 * i : 5 * i + 5])
            for i, (how, at, _, _) in enumerate(self.rides)
        ]


def add_up(place, chains):
    others = Riders(chains)

    def kernel(place_ref, *refs):
        out = len(others.arrays)
        room = out + len(others.outs)
        rides = others.going(place_ref, refs[:out], refs[out:room], refs[room:])
        for ride in rides:
            ride.fetch()
        for ride in rides:
            ride.add()
        for ride in rides:
            ride.done()

    results = call(
        kernel, "add_up", (1,), others.specs, others.outs, scratch=others.scratch, vmem=24, near=others.near(1)
    )(place, *others.arrays)
    for i, chain in enumerate(chains):
        chain.rode(*results[2 * i : 2 * i + 2])


def hold(chains, *after):
    came = together([chain.came for chain in chains] + list(after))
    for chain, value in zip(chains, came):
        chain.came = value


def start(chains):
    chains = [chain for chain in chains if chain.stage is not None]
    if chains:
        for chain, send in zip(chains, together([chain.send for chain in chains])):
            chain.send = send
            chain.came = chain.links.swap(send, chain.stage)


def arrive(chains, *after):
    chains = [chain for chain in chains if chain.stage is not None]
    if chains:
        came = together([chain.came for chain in chains] + list(after))
        for chain, value in zip(chains, came):
            chain.came = value
            chain.cut()


def shards(
    tokens, earlier, coeffs, present, sample_at, w_qkv, w_out, w_up, w_down,
    gain_attn, gain_mlp, w_mean, w_var, cotangent, sizes, groups,
):
    links = Links(sizes)
    high = list(range(2, links.bits))
    count = 2 * links.chips
    tokens, earlier, coeffs, cotangent = tokens[0], earlier[0], coeffs[0], cotangent[0]
    length, width = tokens.shape
    basis_count = coeffs.shape[0]
    rows, side = w_qkv.shape[1], w_qkv.shape[2]
    ff_side = w_up.shape[1]
    local_heads, mem_part = w_mean.shape

    rest = jnp.concatenate([w_up, w_down.T], axis=1).astype(bf16)
    rest = lax.all_gather(rest, ("chips", "core", "heads"), axis=0, tiled=False)
    rest = rest.reshape(links.chips, 2, 2, rows, -1)
    tile = ff_side // 2
    small = jnp.concatenate(
        [gain_attn, gain_mlp, w_mean.reshape(-1), w_var.reshape(-1)]
    ).astype(bf16)
    small_size = small.shape[0]
    small = jnp.pad(small, (0, -small_size % LANES)).reshape(1, -1)
    small_h = links.swap(small, "h")
    first = jnp.where(links.side == 0, small, small_h)
    second = jnp.where(links.side == 0, small_h, small)
    far = high[1:][::-1]
    parts = jnp.concatenate([w_qkv, w_out.T[None]], axis=0).astype(bf16)
    parts = links.gather(parts, 1, far)
    small = links.gather(jnp.concatenate([first, second], axis=0), 0, far)
    small, parts = together([small, parts])
    turns = ([2, 1, "h"], [1, "h", 2], ["h", 2, 1], [2, 1, "h"])
    parts = [parts[c] for c in range(4)]
    have = list(far)
    haves = [list(far) for _ in range(4)]
    for step in range(3):
        small = links.gather(small, 0, [2 - step], have)
        have.append(2 - step)
        for c in range(4):
            parts[c] = links.gather(parts[c], 0, [turns[c][step]], haves[c])
            if turns[c][step] != "h":
                haves[c].append(turns[c][step])
        if step < 2:
            small, *parts = together([small] + parts)
    *qkv_full, out_full = [links.gather(parts[c], 0, [0], haves[c]).reshape(width, width) for c in range(4)]
    small = small.reshape(count, 2, -1).astype(f32)
    gain_a = small[:, 0, :rows].reshape(-1)
    gain_m = small[:, 0, rows : 2 * rows].reshape(-1)

    def head_map(start):
        part = small[:, :, start : start + local_heads * mem_part]
        part = part.reshape(count, 2, local_heads, mem_part).transpose(1, 2, 0, 3)
        return part.reshape(local_heads, 2, basis_count)

    mean_full = head_map(2 * rows)
    var_full = head_map(2 * rows + local_heads * mem_part)

    cot2 = links.swap(cotangent, 0)
    place = jnp.stack([links.bit(stage) for stage in links.places]).astype(jnp.int32)

    ridge = ridge_table(basis_count, 2 * length)
    tokens32, earlier32 = tokens.astype(f32), earlier.astype(f32)
    normed = layer_norm(tokens32, gain_a).astype(bf16)
    past = layer_norm(earlier32, gain_a).astype(bf16)
    old_basis = basis_at((sample_at[0].astype(f32) + 0.5) / GRID, basis_count).astype(bf16)
    here = present[0].astype(f32)
    samples = (here * dot(old_basis, coeffs.astype(bf16), 1, 0)).astype(bf16)
    memory = dot(ridge, jnp.concatenate([samples, past], axis=0), 1, 0).astype(bf16)
    sources = jnp.concatenate([past, normed, memory], axis=0)
    queries = dot(normed, qkv_full[0], 1, 0).astype(bf16)
    keys = dot(sources, qkv_full[1], 1, 0).astype(bf16)
    values = dot(sources, qkv_full[2], 1, 0).astype(bf16)
    old_basis, queries = together([old_basis, queries])
    context, lse, turned = attn_forward(queries, keys, values, mean_full, var_full, sources)
    gain_row = gain_m.reshape(1, -1)
    hidden, normed_mlp = mix(context, tokens, out_full, gain_row)
    normed_mlp2 = links.swap(normed_mlp, 0)
    lows = [2] + high[1:]
    order = block_order([1] + lows)
    mlp, mlp2, gn, gn2, down_send, down_keep, up_send, up_keep = feed(
        place, normed_mlp, normed_mlp2, cotangent, cot2, rest, tile, order
    )
    gn2 = links.swap(gn2, 0)
    mlp2 = links.swap(mlp2, 0)
    c_down = Chain(links, ["h", 1] + lows, down_send, down_keep)
    c_up = Chain(links, [1, 2] + high[1:] + ["h"], up_send, up_keep)
    start([c_down, c_up])
    grad_hidden, gain_m_grad, grad_ctx, branch = turn(hidden, gn, gn2, cotangent, out_full, gain_row)

    plans = (["h", 1, 2], [1, "h", 2])
    spans = [list(range(groups - 1)), [groups - 1]]
    feeds, c_qkv = [c_down, c_up], []
    into = ()
    for group in range(groups):
        late = group == groups - 1
        plan = plans[late] + high[1:]
        if late:
            into = into[:4]
        riders = c_qkv if late else feeds if group == 1 else []
        if group == 1:
            output = (tie(hidden, into[0]) + (mlp + mlp2.astype(f32))).astype(bf16)
            hold(riders, into[0], output)
        elif riders:
            hold(riders, into[0])
        into = attn_backward(
            place, queries, keys, values, mean_full, var_full, lse, grad_ctx, context, turned, branch, group, groups,
            block_order([b for b in plan if b != "h"]), rows, spans[late], into, riders,
        )
        if group == spans[late][-1]:
            c_qkv = c_qkv + [Chain(links, [0] + plan, into[4], into[5])]
        sends = [c.send for c in riders]
        if not late:
            start(riders)
            if c_qkv:
                c_qkv[0].send = tie(c_qkv[0].send, *sends)
                start(c_qkv)
                sends = [c_qkv[0].send]
        grad_ctx = tie(grad_ctx, into[0], *sends)
    arrive(feeds, into[0])
    chains = feeds + c_qkv
    last = chains[-1]
    last.send = tie(last.send, *[c.send for c in feeds])
    start([last])
    start(chains[:-1])
    arrive([last])
    start([last])
    dq, dk, dv, maps = into[:4]
    dq = tie(dq, *[c.send for c in chains])
    grad_tokens, grad_coeffs, tiny = finish(
        place, dq, dk, dv, qkv_full, ridge, old_basis, earlier, tokens, grad_hidden, gain_a.reshape(1, -1),
        gain_m_grad, maps, here.reshape(1), [],
    )

    def add(value, stage):
        return value + links.swap(value, stage)

    tiny_stages = [[lows[0]], [1]] + [[stage] for stage in lows[1:]]
    tiny = add(tiny, 0)
    hold(chains, tiny)
    other = links.swap(tiny, "h")
    add_up(place, chains)
    other, *sends = together([other] + [c.send for c in chains])
    for chain, value in zip(chains, sends):
        chain.send = value
    tiny = tiny + other
    joined = False

    def pick(tiny):
        heads = 2 * local_heads
        item = 2 * links.chip + links.core
        pick_map = lambda first: lax.dynamic_slice(
            tiny, (first + local_heads * links.side, item * mem_part), (local_heads, mem_part)
        )
        mean_out, var_out = pick_map(0), pick_map(heads)
        gains = tiny[2 * heads : 2 * heads + 2 * (width // basis_count)].reshape(-1, 2, basis_count)
        gain_part = width // (2 * count)
        pick_gain = lambda at: lax.dynamic_slice(
            gains[:, at].reshape(-1), ((2 * item + links.side) * gain_part,), (gain_part,)
        )
        gain_a_out, gain_m_out = pick_gain(0), pick_gain(1)
        return gain_a_out, gain_m_out, mean_out, var_out

    while tiny_stages or any(chain.stage is not None for chain in chains):
        going = [c for c in chains if c.stage is not None]
        start(going)
        for stage in tiny_stages.pop(0) if tiny_stages else []:
            tiny = add(tiny, stage)
        if tiny_stages or len(going) > 1:
            *came, tiny = together([c.came for c in going] + [tiny])
            for chain, value in zip(going, came):
                chain.came = value
        on = [c for c in going if c.stages]
        ends = [c for c in going if not c.stages]
        for chain in on:
            chain.cut()
        if not joined:
            joined = True
            c_qkv[0].join(c_qkv[1])
            chains.remove(c_qkv[1])
            on = [c for c in on if c is not c_qkv[1]]
        if on and ends:
            hold(ends, *[c.send for c in on])
        elif ends and not tiny_stages:
            small_out = pick(tiny)
            hold(ends, *small_out)
        for chain in ends:
            chain.cut()
    r_down, r_up = links.whole_rows(c_down.value, rows), links.whole_rows(c_up.value, rows)
    r_proj = c_qkv[0].value
    return (
        output[None],
        grad_tokens[None],
        grad_coeffs[None],
        r_proj[:3],
        r_proj[3].T,
        r_up,
        r_down.T,
        *small_out,
    )


def solution(mesh):
    sizes = dict(mesh.shape)
    both = ("items", "heads")
    in_specs = (
        P(both, None, None),
        P(both, None, None),
        P(both, None, None),
        P(both),
        P(both, None),
        P(None, "items", "heads"),
        P("heads", "items"),
        P("items", "heads"),
        P("heads", "items"),
        P("items"),
        P("items"),
        P("heads", "items"),
        P("heads", "items"),
        P(both, None, None),
    )
    out_specs = (
        P(both, None, None),
        P(both, None, None),
        P(both, None, None),
        P(None, "items", "heads"),
        P("heads", "items"),
        P("items", "heads"),
        P("heads", "items"),
        P(both),
        P(both),
        P("heads", "items"),
        P("heads", "items"),
    )

    chips = sizes["items"] // 2
    split = Mesh(mesh.devices.reshape(chips, 2, sizes["heads"]), ("chips", "core", "heads"))

    def respec(spec):
        def axis(entry):
            names = entry if isinstance(entry, tuple) else (entry,)
            flat = tuple(n for name in names for n in (("chips", "core") if name == "items" else (name,)))
            return flat if flat != (None,) else None

        return P(*(axis(entry) for entry in spec))

    def body(*args):
        return shards(*args, sizes=dict(split.shape), groups=3)

    return jax.shard_map(
        body,
        mesh=split,
        in_specs=tuple(respec(spec) for spec in in_specs),
        out_specs=tuple(respec(spec) for spec in out_specs),
        check_vma=False,
    )
```

```python
import math

import jax
import jax.numpy as jnp
import numpy as np
from jax import lax
from jax.experimental import pallas as pl
from jax.experimental.pallas import tpu as pltpu
from jax.sharding import Mesh
from jax.sharding import PartitionSpec as P

HD = 64
GRID = 1024
EPSILON = 1e-05
VAR_SCALE = 0.01
RIDGE = 1.0
LANES = 128
ROWS = 256
NEG = -1e30
bf16 = jnp.bfloat16
f32 = jnp.float32


def dot(a, b, ca, cb):
    return lax.dot_general(a, b, (((ca,), (cb,)), ((), ())), preferred_element_type=f32)


def layer_norm(values, gain_vec):
    row_mean = jnp.mean(values, axis=-1, keepdims=True)
    centred = values - row_mean
    spread = jnp.mean(centred * centred, axis=-1, keepdims=True)
    return centred * lax.rsqrt(spread + EPSILON) * gain_vec


def basis_at(points, basis_count):
    centers = (jnp.arange(basis_count, dtype=f32) + 0.5) / basis_count
    offset = points[..., None] - centers
    return jnp.exp(-offset * offset * (0.5 * basis_count * basis_count))


def ridge_table(basis_count, samples):
    points = (np.arange(samples) + 0.5) / samples
    centers = (np.arange(basis_count) + 0.5) / basis_count
    design = np.exp(-((points[:, None] - centers) ** 2) * (0.5 * basis_count * basis_count))
    gram = design.T @ design + RIDGE * np.eye(basis_count)
    factor = np.linalg.cholesky(gram)
    table = np.linalg.solve(factor.T, np.linalg.solve(factor, design.T))
    return jnp.asarray(table.astype(np.float32)).astype(bf16)


def gelu_tanh(values):
    return jax.nn.gelu(values, approximate=True)


def near_scores(q_rows, keys, block):
    reach = keys.shape[0] // 2 + (block + 1) * ROWS
    scores = dot(q_rows, keys[:reach], 1, 1)
    row = lax.broadcasted_iota(jnp.int32, (q_rows.shape[0], ROWS), 0) % ROWS
    col = lax.broadcasted_iota(jnp.int32, (q_rows.shape[0], ROWS), 1)
    edge = jnp.where(col <= row, scores[:, reach - ROWS :], NEG)
    return jnp.concatenate([scores[:, : reach - ROWS], edge], axis=1), reach


def both_heads(x, half):
    none = jnp.zeros_like(x)
    return jnp.concatenate([jnp.where(half, x, none), jnp.where(half, none, x)], axis=0)


def by_head(ref, rows):
    return jnp.concatenate(
        [jnp.broadcast_to(ref[0, head : head + 1, :], (rows, ref.shape[2])) for head in range(2)], axis=0
    )


def density_parts(scaled, w_mean, w_var):
    basis_count = scaled.shape[1]
    index = lax.broadcasted_iota(jnp.int32, (1, basis_count), 1).astype(f32)
    centers = (index + 0.5) / basis_count
    middle = jax.nn.sigmoid(jnp.sum(scaled * w_mean, axis=1, keepdims=True))
    var_raw = jnp.sum(scaled * w_var, axis=1, keepdims=True)
    softplus = jnp.maximum(var_raw, 0.0) + jnp.log1p(jnp.exp(-jnp.abs(var_raw)))
    variance = VAR_SCALE * softplus + 1.0 / (basis_count * basis_count)
    offset = middle - centers
    inv_var = 1.0 / variance
    square = offset * offset * inv_var
    scale = lax.rsqrt(2.0 * math.pi * variance) / basis_count
    weights = jnp.exp(-0.5 * square) * scale
    return weights, middle, var_raw, inv_var, offset, square


def attn_fwd_kernel(
    q_ref, k_ref, v_ref, mk_ref, mv_ref, wm_ref, wv_ref, rows_ref, ctx_ref, lse_ref, turned_ref
):
    turned_ref[...] = rows_ref[...].T
    half = lax.broadcasted_iota(jnp.int32, (1, LANES), 1) < HD
    length = q_ref.shape[0]
    keys, values = k_ref[...], v_ref[...]
    mem_keys, mem_values = mk_ref[...], mv_ref[...]
    w_mean, w_var = by_head(wm_ref, ROWS), by_head(wv_ref, ROWS)
    for block in range(length // ROWS):
        rows = slice(block * ROWS, (block + 1) * ROWS)
        q_both = both_heads(q_ref[rows, :] * jnp.asarray(0.125, bf16), half)
        scores, reach = near_scores(q_both, keys, block)
        top = jnp.max(scores, axis=1, keepdims=True)
        raw = jnp.exp(scores - top)
        total = jnp.sum(raw, axis=1, keepdims=True)
        near = dot((raw * (1.0 / total)).astype(bf16), values[:reach], 1, 0)
        weights = density_parts(dot(q_both, mem_keys, 1, 1), w_mean, w_var)[0]
        out = near + dot(weights.astype(bf16), mem_values, 1, 0)
        logs = top + jnp.log(total)
        ctx_ref[rows, :] = jnp.where(half, out[:ROWS], out[ROWS:]).astype(bf16)
        lse_ref[rows, :] = jnp.where(half, logs[:ROWS], logs[ROWS:])


def attn_bwd_kernel(
    order, rows_own, place_ref,
    q_ref, k_ref, v_ref, mk_ref, mv_ref, wm_ref, wv_ref, lse_ref, do_ref, ctx_ref, far_turned_ref, far_branch_ref,
    dq_ref, dk_ref, dv_ref, maps_ref, send_ref, keep_ref, acck_ref, accv_ref, turned_ref, branch_ref, sems, rides,
):
    fetches = (
        pltpu.make_async_copy(far_turned_ref, turned_ref, sems.at[0]),
        pltpu.make_async_copy(far_branch_ref, branch_ref, sems.at[1]),
    )

    @pl.when(pl.program_id(0) == 0)
    def _():
        for fetch in fetches:
            fetch.start()
        for ride in rides:
            ride.fetch()

    @pl.when(pl.program_id(0) == 1)
    def _():
        for ride in rides:
            ride.add()

    half = lax.broadcasted_iota(jnp.int32, (1, LANES), 1) < HD
    length = q_ref.shape[0]
    near_rows = k_ref.shape[0]
    keys, values = k_ref[...], v_ref[...]
    mem_keys, mem_values = mk_ref[...], mv_ref[...]
    both = lambda x: both_heads(x, half)
    w_mean, w_var = by_head(wm_ref, length), by_head(wv_ref, length)
    early = near_rows - ROWS
    q_full, do_full = q_ref[...], do_ref[...]
    q_turn, do_turn = q_full.T, do_full.T
    q_both = both(q_full * jnp.asarray(0.125, bf16))
    do_both = both(do_full)

    def late(x):
        return jnp.concatenate([x[ROWS:length], x[length + ROWS :]], axis=0)

    row = lax.broadcasted_iota(jnp.int32, (2 * length, ROWS), 0) % length
    col = lax.broadcasted_iota(jnp.int32, (2 * length, ROWS), 1)
    scores = dot(q_both, keys[:early], 1, 1)
    edge = jnp.where(col <= row, scores[:, early - ROWS :], NEG)
    scores = jnp.concatenate([scores[:, : early - ROWS], edge], axis=1)
    row = lax.broadcasted_iota(jnp.int32, (length, ROWS), 0) % ROWS
    col = lax.broadcasted_iota(jnp.int32, (length, ROWS), 1)
    tail = jnp.where(col <= row, dot(late(q_both), keys[early:], 1, 1), NEG)
    lse = jnp.concatenate([lse_ref[:, 0:1], lse_ref[:, HD : HD + 1]], axis=0)
    probs, probs_tail = jnp.exp(scores - lse), jnp.exp(tail - late(lse))
    grad_probs = dot(do_both, values[:early], 1, 1)
    grad_tail = dot(late(do_both), values[early:], 1, 1)
    inner = jnp.sum(probs * grad_probs, axis=1, keepdims=True)
    more = jnp.sum(probs_tail * grad_tail, axis=1, keepdims=True)
    inner_late = late(inner) + more
    inner = jnp.concatenate(
        [inner[:ROWS], inner_late[:ROWS], inner[length : length + ROWS], inner_late[ROWS:]], axis=0
    )
    grad_raw = (0.125 * probs * (grad_probs - inner)).astype(bf16)
    raw_tail = (0.125 * probs_tail * (grad_tail - inner_late)).astype(bf16)
    probs_low, low_tail = probs.astype(bf16), probs_tail.astype(bf16)
    scaled = dot(q_both, mem_keys, 1, 1)
    weights, middle, var_raw, inv_var, offset, square = density_parts(scaled, w_mean, w_var)
    grad_w = dot(do_both, mem_values, 1, 1) * weights
    d_mid = -jnp.sum(grad_w * offset, axis=1, keepdims=True) * inv_var
    d_var = jnp.sum(grad_w * (square - 1.0), axis=1, keepdims=True) * (0.5 * inv_var)
    d_mid = d_mid * middle * (1.0 - middle)
    d_var = d_var * VAR_SCALE * jax.nn.sigmoid(var_raw)
    gm, gv = scaled * d_mid, scaled * d_var
    grad_mem = (0.125 * (d_mid * w_mean + d_var * w_var)).astype(bf16)
    weights_low = weights.astype(bf16)
    out = dot(grad_raw, keys[:early], 1, 0) + dot(grad_mem, mem_keys, 1, 0)
    out_tail = dot(raw_tail, keys[early:], 1, 0)
    for head in range(2):
        part = slice(head * HD, (head + 1) * HD)
        mine = slice(head * length, (head + 1) * length)
        ends = slice(head * ROWS, (head + 1) * ROWS)
        acck_ref[part, :early] = dot(q_turn[part], grad_raw[mine], 1, 0)
        accv_ref[part, :early] = dot(do_turn[part], probs_low[mine], 1, 0)
        acck_ref[part, early:near_rows] = dot(q_turn[part, ROWS:], raw_tail[ends], 1, 0)
        accv_ref[part, early:near_rows] = dot(do_turn[part, ROWS:], low_tail[ends], 1, 0)
        acck_ref[part, near_rows:] = dot(q_turn[part], grad_mem[mine], 1, 0)
        accv_ref[part, near_rows:] = dot(do_turn[part], weights_low[mine], 1, 0)
        maps_ref[0, head : head + 1, :] = jnp.sum(gm[mine], axis=0, keepdims=True)
        maps_ref[0, 2 + head : 3 + head, :] = jnp.sum(gv[mine], axis=0, keepdims=True)
    dq_ref[:ROWS, :] = jnp.where(half, out[:ROWS], out[length : length + ROWS]).astype(bf16)
    out = late(out) + out_tail
    dq_ref[ROWS:, :] = jnp.where(half, out[:ROWS], out[ROWS:]).astype(bf16)
    dk_ref[...] = acck_ref[...].T.astype(bf16)
    dv_ref[...] = accv_ref[...].T.astype(bf16)

    @pl.when(pl.program_id(0) == 0)
    def _():
        for fetch in fetches:
            fetch.wait()

    turned = turned_ref[...]
    grads = (
        dot(turned[:, length : 2 * length], dq_ref[...], 1, 0),
        dot(turned, dk_ref[...], 1, 0),
        dot(turned, dv_ref[...], 1, 0),
        dot(branch_ref[...], ctx_ref[...], 1, 0),
    )
    for at, grad in enumerate(grads):
        send, keep = cut_core(grad, place_ref[0], rows_own, order)
        send_ref[:, at], keep_ref[:, at] = send.astype(bf16), keep

    @pl.when(pl.program_id(0) == pl.num_programs(0) - 1)
    def _():
        for ride in rides:
            ride.done()


class Ride:
    def __init__(self, cut, bit, ins, outs, scratch):
        keep, came = ins
        width = keep.shape[-1] // 2

        def half(ref, b):
            return ref.at[:, :, pl.ds(pl.multiple_of(b * width, LANES), width)] if cut == "h" else ref.at[b]

        self.far, self.near, sems = scratch[:2], scratch[2:4], scratch[4]
        copy = pltpu.make_async_copy
        self.fetches = [
            copy(half(keep, 1 - bit), scratch[0], sems.at[0]),
            copy(half(came, 1 - bit), scratch[1], sems.at[1]),
            copy(half(keep, bit), scratch[2], sems.at[2]),
            copy(half(came, bit), scratch[3], sems.at[3]),
        ]
        self.writes = [copy(scratch[1], outs[0], sems.at[4]), copy(scratch[2], outs[1], sems.at[5])]

    def fetch(self):
        for one in self.fetches:
            one.start()

    def add(self):
        for one in self.fetches:
            one.wait()
        keep, came = self.far
        came[...] = (keep[...] + came[...].astype(f32)).astype(bf16)
        keep, came = self.near
        keep[...] = keep[...] + came[...].astype(f32)
        for one in self.writes:
            one.start()

    def done(self):
        for one in self.writes:
            one.wait()


def attn_specs(length, basis_count, place):
    near_rows = 2 * length
    near = pl.BlockSpec((near_rows, LANES), lambda p, *_: (0, place(p)))
    far = pl.BlockSpec((basis_count, LANES), lambda p, *_: (near_rows // basis_count, place(p)))
    maps = pl.BlockSpec((1, 2, basis_count), lambda p, *_: (place(p), 0, 0))
    return [pl.BlockSpec((length, LANES), lambda p, *_: (0, place(p))), near, near, far, far, maps, maps]


def attn_forward(queries, keys, values, w_mean, w_var, rows):
    length, width = queries.shape
    basis_count = w_mean.shape[-1]
    pairs = width // LANES
    size = rows.shape[0]
    ours = pl.BlockSpec((length, LANES), lambda p: (0, p))
    return call(
        attn_fwd_kernel, "attn_forward", (pairs,),
        attn_specs(length, basis_count, lambda p: p) + [pl.BlockSpec((size, LANES), lambda p: (0, p))],
        [
            (ours, struct(bf16, length, width)),
            (ours, struct(f32, length, width)),
            (pl.BlockSpec((LANES, size), lambda p: (p, 0)), struct(bf16, width, size)),
        ],
        scalars=0,
        near=tuple(range(8)),
    )(queries, keys, values, keys, values, w_mean, w_var, rows)


def attn_backward(
    place, queries, keys, values, w_mean, w_var, lse, grad_ctx, context, turned, branch, group, groups, order, rows,
    span, into, riders,
):
    length, width = queries.shape
    basis_count = w_mean.shape[-1]
    pairs = width // LANES
    count = pairs // groups
    where = lambda p: p * groups + group
    all_rows = keys.shape[0]
    ours = lambda size: pl.BlockSpec((size, LANES), lambda p, _: (0, where(p)))
    cut = (len(order), 4, rows)
    mine = pl.BlockSpec(cut + (LANES,), lambda p, _: (0, 0, 0, p * len(span) + group - span[0]))
    specs = attn_specs(length, basis_count, where) + [ours(length)] * 3
    specs += [pl.BlockSpec(memory_space=pl.ANY)] * 2
    held = [pl.BlockSpec(memory_space=pl.ANY)] * len(into)

    others = Riders(riders)
    outs = [
        (ours(length), struct(bf16, length, width)),
        (ours(all_rows), struct(bf16, all_rows, width)),
        (ours(all_rows), struct(bf16, all_rows, width)),
        (pl.BlockSpec((1, 4, basis_count), lambda p, _: (where(p), 0, 0)), struct(f32, pairs, 4, basis_count)),
        (mine, struct(bf16, *cut, count * LANES * len(span))),
        (mine, struct(f32, *cut, count * LANES * len(span))),
    ]
    scratch = [
        pltpu.VMEM((LANES, all_rows), f32),
        pltpu.VMEM((LANES, all_rows), f32),
        pltpu.VMEM(turned.shape, bf16),
        pltpu.VMEM(branch.shape, bf16),
        pltpu.SemaphoreType.DMA((2,)),
    ]
    own = (1 + len(specs), len(outs), len(scratch))

    def kernel(*refs):
        first = own[0] + len(into)
        out = first + len(others.arrays)
        room = out + own[1] + len(others.outs)
        rides = others.going(refs[0], refs[first:out], refs[out + own[1] : room], refs[room + own[2] :])
        attn_bwd_kernel(order, rows, *refs[: own[0]], *refs[out : out + own[1]], *refs[room : room + own[2]], rides)

    results = call(
        kernel, "attn_backward", (count,),
        specs + held + others.specs,
        outs + others.outs,
        scratch=scratch + others.scratch,
        vmem=32 if riders else 22,
        aliases={own[0] + i: i for i in range(len(into))},
        near=tuple(range(own[0], own[0] + len(into))) + others.near(own[0] + len(into)),
    )(
        place, queries, keys, values, keys, values, w_mean, w_var, lse, grad_ctx, context, turned, branch, *into,
        *others.arrays,
    )
    for i, rider in enumerate(riders):
        rider.rode(*results[own[1] + 2 * i : own[1] + 2 * i + 2])
    return results[: own[1]]


def norm_stats(values):
    centred = values - jnp.mean(values, axis=-1, keepdims=True)
    spread = jnp.mean(centred * centred, axis=-1, keepdims=True)
    inverse = lax.rsqrt(spread + EPSILON)
    return centred * inverse, inverse


def norm_back(grad, hat, inverse, gain):
    scaled = grad * gain
    inner = jnp.mean(scaled * hat, axis=-1, keepdims=True)
    return inverse * (scaled - jnp.mean(scaled, axis=-1, keepdims=True) - hat * inner)


def side_block(ref):
    chips, cores, _, rows, cols = ref.shape
    return ref[...].reshape(chips * cores * rows, cols)


def block_order(bits):
    chips = []
    for place in range(1 << len(bits)):
        chip = 0
        for at, bit in enumerate(reversed(bits)):
            chip |= ((place >> at) & 1) << (bit - 1)
        chips.append(chip)
    return chips


def cut_core(value, core, rows, order):
    split = value.reshape(value.shape[0] // (2 * rows), 2, rows, value.shape[1])
    low = jnp.stack([split[chip, 0] for chip in order])
    high = jnp.stack([split[chip, 1] for chip in order])
    return jnp.where(core == 0, high, low), jnp.where(core == 0, low, high)


def mix_kernel(ctx_ref, tokens_ref, w_ref, gain_ref, hidden_ref, normed_ref):
    hidden = tokens_ref[...].astype(f32) + dot(ctx_ref[...], w_ref[...], 1, 1)
    hidden_ref[...] = hidden
    normed_ref[...] = (norm_stats(hidden)[0] * gain_ref[...]).astype(bf16)


def feed_kernel(
    order, place_ref, normed_ref, normed2_ref, cot_ref, cot2_ref, up_ref, down_ref,
    mlp_ref, mlp2_ref, gn_ref, gn2_ref, down_send_ref, down_keep_ref, up_send_ref, up_keep_ref,
    nt_ref, ct_ref, act_ref, pre_ref, acc_ref, near_send_ref, near_keep_ref, sems,
):
    step = pl.program_id(0)
    length, width = normed_ref.shape
    block = up_ref.shape[1] * up_ref.shape[3]
    w_up, w_down = side_block(up_ref), side_block(down_ref)
    slope = math.sqrt(2.0 / math.pi)

    @pl.when(step == 0)
    def _():
        nt_ref[:, :length] = normed_ref[...].T
        nt_ref[:, length:] = normed2_ref[...].T
        ct_ref[:, :length] = cot_ref[...].T
        ct_ref[:, length:] = cot2_ref[...].T

    for half in range(2):
        rows = slice(half * length, (half + 1) * length)
        normed = (normed_ref, normed2_ref)[half][...]
        cot = (cot_ref, cot2_ref)[half][...]
        pre = dot(normed, w_up, 1, 0)
        square = pre * pre
        bend = jnp.tanh(slope * pre * (1.0 + 0.044715 * square))
        lift = 0.5 + 0.5 * bend
        act = (pre * lift).astype(bf16)
        rise = lift + 0.5 * pre * (1.0 - bend * bend) * (slope + (3.0 * 0.044715 * slope) * square)
        grad_pre = (dot(cot, w_down, 1, 0) * rise).astype(bf16)
        act_ref[rows, :] = act
        pre_ref[rows, :] = grad_pre
        mlp = dot(act, w_down, 1, 1)
        grad_normed = dot(grad_pre, w_up, 1, 1)

        @pl.when(step == 0)
        def _():
            acc_ref[2 * half] = mlp
            acc_ref[2 * half + 1] = grad_normed

        @pl.when(step == 1)
        def _():
            if half == 0:
                mlp_ref[...] = acc_ref[0] + mlp
                gn_ref[...] = acc_ref[1] + grad_normed
            else:
                mlp2_ref[...] = (acc_ref[2] + mlp).astype(bf16)
                gn2_ref[...] = (acc_ref[3] + grad_normed).astype(bf16)

    sent = pltpu.make_async_copy(near_send_ref, down_send_ref, sems.at[0])
    kept = pltpu.make_async_copy(near_keep_ref, down_keep_ref, sems.at[1])
    g_down = dot(ct_ref[...], act_ref[...], 1, 0).reshape(width // block, block, -1)
    g_down = jnp.stack([g_down[chip] for chip in order])

    @pl.when(step == 0)
    def _():
        near_send_ref[...] = g_down.astype(bf16)
        sent.start()

    @pl.when(step == 1)
    def _():
        near_keep_ref[...] = g_down
        kept.start()

    g_up = dot(nt_ref[...], pre_ref[...], 1, 0).reshape(width // block, block, -1)
    low = jnp.stack([g_up[chip] for chip in order[: len(order) // 2]])
    high = jnp.stack([g_up[chip] for chip in order[len(order) // 2 :]])
    first = place_ref[1] == 0
    up_send_ref[...] = jnp.where(first, high, low).astype(bf16)
    up_keep_ref[...] = jnp.where(first, low, high)

    @pl.when(step == 1)
    def _():
        sent.wait()
        kept.wait()


def turn_kernel(
    hidden_ref, gn_ref, gn2_ref, cot_ref, w_ref, gain_ref, gh_ref, gain_grad_ref, gc_ref, branch_ref
):
    step = pl.program_id(0)
    hidden = hidden_ref[...]
    hat, inverse = norm_stats(hidden)
    grad = gn_ref[...] + gn2_ref[...].astype(f32)
    grad_hidden = cot_ref[...].astype(f32) + norm_back(grad, hat, inverse, gain_ref[...])
    gh_ref[...] = grad_hidden
    branch = grad_hidden.astype(bf16)
    branch_ref[...] = branch.T
    gc_ref[...] = dot(branch, w_ref[...], 1, 0).astype(bf16)

    @pl.when(step == 0)
    def _():
        gain_grad_ref[...] = jnp.zeros_like(gain_grad_ref)

    gain_grad_ref[...] += jnp.sum(grad * hat, axis=0, keepdims=True)


def finish_kernel(
    blocks, rides, dq_ref, dk_ref, dv_ref, wq_ref, wk_ref, wv_ref, ridge_ref, basis_ref, earlier_ref, tokens_ref, gh_ref,
    gain_ref, gain_m_ref, maps_ref, here_ref, gt_ref, gc_ref, small_ref, fit_ref, grad_ref,
):
    step = pl.program_id(0)
    length = ridge_ref.shape[1] // 2

    @pl.when(step == 0)
    def _():
        for ride in rides:
            ride.fetch()

    @pl.when(step == blocks + 1)
    def _():
        for ride in rides:
            ride.add()

    part = dot(dk_ref[...], wk_ref[...], 1, 1) + dot(dv_ref[...], wv_ref[...], 1, 1)

    @pl.when(step == 0)
    def _():
        memory = part.astype(bf16)
        samples = dot(ridge_ref[:, :length], memory, 0, 0).astype(bf16)
        gc_ref[...] = here_ref[0] * dot(basis_ref[...], samples, 0, 0)
        fit_ref[...] = dot(ridge_ref[:, length:], memory, 0, 0)
        grad_ref[...] = jnp.zeros_like(grad_ref)

    @pl.when(jnp.logical_and(step > 0, step <= blocks))
    def _():
        past = part + fit_ref[pl.ds(pl.multiple_of((step - 1) * ROWS, ROWS), ROWS), :]
        hat = norm_stats(earlier_ref[...].astype(f32))[0]
        grad_ref[...] += jnp.sum(past * hat, axis=0, keepdims=True)

    @pl.when(step > blocks)
    def _():
        grad = part + dot(dq_ref[...], wq_ref[...], 1, 1)
        hat, inverse = norm_stats(tokens_ref[...].astype(f32))
        grad_ref[...] += jnp.sum(grad * hat, axis=0, keepdims=True)
        gt_ref[...] = gh_ref[...] + norm_back(grad, hat, inverse, gain_ref[...])

    @pl.when(step == 2 * blocks)
    def _():
        small_ref[...] = jnp.zeros_like(small_ref)
        pairs, _, basis_count = maps_ref.shape
        for p in range(pairs):
            small_ref[2 * p : 2 * p + 2, :] = maps_ref[p, 0:2, :]
            small_ref[2 * (pairs + p) : 2 * (pairs + p) + 2, :] = maps_ref[p, 2:4, :]
        for at in range(grad_ref.shape[1] // basis_count):
            cols = slice(at * basis_count, (at + 1) * basis_count)
            row = 4 * pairs + 2 * at
            small_ref[row : row + 1, :] = grad_ref[:, cols]
            small_ref[row + 1 : row + 2, :] = gain_m_ref[:, cols]
        for ride in rides:
            ride.done()


def whole_spec(*shape):
    return pl.BlockSpec(shape, lambda *_: (0,) * len(shape))


def struct(kind, *shape):
    return jax.ShapeDtypeStruct(shape, kind)


def call(kernel, name, grid, in_specs, outs, scratch=(), scalars=1, vmem=24, aliases={}, near=(), near_outs=()):
    def place_of(at, out):
        return out if math.prod(out.shape) <= 1 << 16 or at in near_outs else pltpu.HBM(out.shape, out.dtype)

    run = pl.pallas_call(
        kernel,
        grid_spec=pltpu.PrefetchScalarGridSpec(
            num_scalar_prefetch=scalars,
            grid=grid,
            in_specs=in_specs,
            out_specs=[whole_spec(*out.shape) if spec is None else spec for spec, out in outs],
            scratch_shapes=scratch,
        ),
        out_shape=[place_of(at, out) for at, (_, out) in enumerate(outs)],
        input_output_aliases=aliases,
        compiler_params=pltpu.CompilerParams(vmem_limit_bytes=vmem << 20),
        cost_estimate=pl.CostEstimate(flops=0, bytes_accessed=1 << 20, transcendentals=0),
        name=name,
    )

    def put(at, x):
        return x if x.size <= 1 << 16 or at in near else pltpu.with_memory_space_constraint(x, pltpu.HBM)

    return lambda *args: run(*(put(at, x) for at, x in enumerate(args)))


def row_spec(width):
    return pl.BlockSpec((ROWS, width), lambda s, *_: (s, 0))


def mix(context, tokens, weights, gain):
    length, width = tokens.shape
    some = row_spec(width)
    return call(
        mix_kernel, "mix", (length // ROWS,),
        [some, some, whole_spec(width, width), whole_spec(1, width)],
        [(some, struct(f32, length, width)), (some, struct(bf16, length, width))],
        scalars=0,
        near_outs=(1,),
    )(context, tokens, weights, gain)


def feed(place, normed, normed2, cot, cot2, rest, tile, order):
    length, width = normed.shape
    chips, cores, _, rows, _ = rest.shape
    block = cores * rows
    big = whole_spec(length, width)

    def weights(at):
        return pl.BlockSpec(
            (chips, cores, 1, rows, tile), lambda s, p: (0, 0, (s + 1 + p[2]) % 2, 0, at + p[0])
        )

    anywhere = pl.BlockSpec(memory_space=pl.ANY)
    half = (chips // 2, block, 2 * tile)
    turned = pl.BlockSpec((chips // 2, block, tile), lambda s, p: (0, 0, (s + 1 + p[2]) % 2))
    return call(
        lambda *refs: feed_kernel(order, *refs), "feed", (2,),
        [big, big, big, big, weights(0), weights(2)],
        [
            (None, struct(f32, length, width)),
            (None, struct(bf16, length, width)),
            (None, struct(f32, length, width)),
            (None, struct(bf16, length, width)),
            (anywhere, struct(bf16, chips, block, tile)),
            (anywhere, struct(f32, chips, block, tile)),
            (turned, struct(bf16, *half)),
            (turned, struct(f32, *half)),
        ],
        scratch=[
            pltpu.VMEM((width, 2 * length), bf16),
            pltpu.VMEM((width, 2 * length), bf16),
            pltpu.VMEM((2 * length, tile), bf16),
            pltpu.VMEM((2 * length, tile), bf16),
            pltpu.VMEM((4, length, width), f32),
            pltpu.VMEM((chips, block, tile), bf16),
            pltpu.VMEM((chips, block, tile), f32),
            pltpu.SemaphoreType.DMA((2,)),
        ],
        vmem=44,
        near=(1, 2, 4),
        near_outs=(2, 3),
    )(place, normed, normed2, cot, cot2, rest, rest)


def turn(hidden, gn, gn2, cot, weights, gain):
    length, width = hidden.shape
    some = row_spec(width)
    return call(
        turn_kernel, "turn", (length // ROWS,),
        [some] * 4 + [whole_spec(width, width), whole_spec(1, width)],
        [
            (some, struct(f32, length, width)),
            (None, struct(f32, 1, width)),
            (some, struct(bf16, length, width)),
            (pl.BlockSpec((width, ROWS), lambda s: (0, s)), struct(bf16, width, length)),
        ],
        scalars=0,
        near=(1, 2),
    )(hidden, gn, gn2, cot, weights, gain)


def finish(
    place, dq, dk, dv, weights, ridge, basis, earlier, tokens, grad_hidden, gain, gain_m_grad, maps, here, riders
):
    length, width = tokens.shape
    basis_count = ridge.shape[0]
    blocks = length // ROWS
    small = 4 * maps.shape[0] + 2 * (width // basis_count)
    all_rows = pl.BlockSpec((ROWS, width), lambda s, _: (jnp.where(s == 0, 2 * blocks, s - 1), 0))
    past = pl.BlockSpec((ROWS, width), lambda s, _: (jnp.clip(s - 1, 0, blocks - 1), 0))
    now = pl.BlockSpec((ROWS, width), lambda s, _: (jnp.maximum(s - 1 - blocks, 0), 0))
    args = (gain, gain_m_grad, maps)
    others = Riders(riders)
    outs = [
        (now, struct(f32, length, width)),
        (None, struct(f32, basis_count, width)),
        (None, struct(f32, small + (-small) % 8, basis_count)),
    ]
    scratch = [pltpu.VMEM((length, width), f32), pltpu.VMEM((1, width), f32)]
    ins = 3 + len(weights) + 2 + 3 + 3 + 1

    def kernel(place_ref, *refs):
        out = ins + len(others.arrays)
        room = out + 3 + len(others.outs)
        rides = others.going(place_ref, refs[ins:out], refs[out + 3 : room], refs[room + 2 :])
        finish_kernel(blocks, rides, *refs[:ins], *refs[out : out + 3], *refs[room : room + 2])

    results = call(
        kernel, "finish", (2 * blocks + 1,),
        [now, all_rows, all_rows]
        + [whole_spec(*x.shape) for x in (*weights, ridge, basis)]
        + [past, now, now]
        + [whole_spec(*x.shape) for x in args]
        + [pl.BlockSpec(memory_space=pltpu.SMEM)]
        + others.specs,
        outs + others.outs,
        scratch=scratch + others.scratch,
        vmem=22,
    )(place, dq, dk, dv, *weights, ridge, basis, earlier, tokens, grad_hidden, *args, here, *others.arrays)
    for i, rider in enumerate(riders):
        rider.rode(*results[3 + 2 * i : 5 + 2 * i])
    return results[:3]


class Links:
    def __init__(self, sizes):
        self.chips = sizes["chips"]
        self.bits = self.chips.bit_length()
        self.chip = lax.axis_index("chips")
        self.core = lax.axis_index("core")
        self.side = lax.axis_index("heads")
        self.places = [0, 1, "h"] + list(range(2, self.bits))

    def swap(self, value, stage):
        if stage in ("h", 0):
            return lax.ppermute(value, "heads" if stage == "h" else "core", [(0, 1), (1, 0)])
        mask = 1 << (stage - 1)
        return lax.ppermute(value, "chips", [(i, i ^ mask) for i in range(self.chips)])

    def bit(self, stage):
        if stage == "h":
            return self.side
        return self.core if stage == 0 else (self.chip >> (stage - 1)) & 1

    def gather(self, value, lead, stages, have=()):
        have = list(have)
        for stage in stages:
            other = self.swap(value, stage)
            if stage == "h":
                value = self.gather_with(value, other, stage, None)
            else:
                place = lead + sum(1 for b in have if b > stage)
                value = self.gather_with(value, other, stage, place)
                have.append(stage)
        return value

    def gather_with(self, value, other, stage, axis=0):
        mine_first = self.bit(stage) == 0
        first = jnp.where(mine_first, value, other)
        second = jnp.where(mine_first, other, value)
        if axis is None:
            return jnp.concatenate([first, second], axis=-1)
        return jnp.stack([first, second], axis=axis)

    def whole_rows(self, value, rows):
        value = value.reshape(2, rows, -1)
        mine = lax.dynamic_index_in_dim(value, self.core, 0, keepdims=False)
        other = self.swap(lax.dynamic_index_in_dim(value, 1 - self.core, 0, keepdims=False), 0)
        return self.gather_with(mine, other, 0, None)


def tie(value, *earlier):
    return lax.optimization_barrier((value,) + earlier)[0]


class Chain:
    def __init__(self, links, stages, send, keep, wire=bf16):
        self.links, self.wire = links, wire
        self.stage, self.stages = stages[0], list(stages[1:])
        self.left = [stage for stage in self.stages if stage != "h"]
        self.send, self.keep = self.spread(send), self.spread(keep)

    def spread(self, value):
        return value.reshape((2,) * len(self.left) + value.shape[1:])

    def cut(self):
        keep, came = self.keep, self.came
        self.stage = self.stages.pop(0) if self.stages else None
        if self.stage is None:
            self.value = keep + came.astype(f32)
            return
        bit = self.links.bit(self.stage)
        if self.stage == "h":
            width = keep.shape[-1] // 2
            take = lambda x, b: lax.dynamic_slice_in_dim(x, b * width, width, axis=x.ndim - 1)
        else:
            axis = self.left.index(self.stage)
            self.left.pop(axis)
            take = lambda x, b: lax.dynamic_index_in_dim(x, b, axis, keepdims=False)
        self.send = (take(keep, 1 - bit) + take(came, 1 - bit).astype(f32)).astype(self.wire)
        self.keep = take(keep, bit) + take(came, bit).astype(f32)

    def ride(self):
        self.stage = self.stages.pop(0)
        at = self.links.places.index(self.stage)
        tail = self.keep.shape[len(self.left) :]
        rows, cols = math.prod(tail[:-1]), tail[-1]
        if self.stage == "h":
            whole = (self.keep.size // (rows * cols), rows, cols)
            half = whole[:2] + (cols // 2,)
        else:
            self.left.pop(self.left.index(self.stage))
            whole = (2, self.keep.size // (2 * rows * cols), rows, cols)
            half = whole[1:]
        self.tail = tail[:-1] + half[-1:]
        return self.stage, at, [self.keep.reshape(whole), self.came.reshape(whole)], half

    def join(self, other):
        self.send = jnp.concatenate([self.send, other.send], axis=-1)
        self.keep = jnp.concatenate([self.keep, other.keep], axis=-1)

    def rode(self, send, keep):
        shape = (2,) * len(self.left) + self.tail
        self.send, self.keep = send.reshape(shape), keep.reshape(shape)


def together(values):
    return list(lax.optimization_barrier(tuple(values)))


class Riders:
    def __init__(self, chains):
        self.rides = [chain.ride() for chain in chains]
        anywhere = pl.BlockSpec(memory_space=pl.ANY)
        self.arrays = [x for _, _, arrays, _ in self.rides for x in arrays]
        self.specs = [anywhere] * len(self.arrays)
        self.outs, self.scratch = [], []
        for _, _, _, shape in self.rides:
            self.outs += [(anywhere, struct(bf16, *shape)), (anywhere, struct(f32, *shape))]
            self.scratch += [pltpu.VMEM(shape, kind) for kind in (f32, bf16, f32, bf16)]
            self.scratch += [pltpu.SemaphoreType.DMA((6,))]

    def near(self, first):
        return tuple(first + 1 + 2 * i for i in range(len(self.rides)))

    def going(self, place_ref, ins, outs, scratch):
        return [
            Ride(how, place_ref[at], ins[2 * i : 2 * i + 2], outs[2 * i : 2 * i + 2], scratch[5 * i : 5 * i + 5])
            for i, (how, at, _, _) in enumerate(self.rides)
        ]


def add_up(place, chains):
    others = Riders(chains)

    def kernel(place_ref, *refs):
        out = len(others.arrays)
        room = out + len(others.outs)
        rides = others.going(place_ref, refs[:out], refs[out:room], refs[room:])
        for ride in rides:
            ride.fetch()
        for ride in rides:
            ride.add()
        for ride in rides:
            ride.done()

    results = call(
        kernel, "add_up", (1,), others.specs, others.outs, scratch=others.scratch, vmem=24, near=others.near(1)
    )(place, *others.arrays)
    for i, chain in enumerate(chains):
        chain.rode(*results[2 * i : 2 * i + 2])


def hold(chains, *after):
    came = together([chain.came for chain in chains] + list(after))
    for chain, value in zip(chains, came):
        chain.came = value


def start(chains):
    chains = [chain for chain in chains if chain.stage is not None]
    if chains:
        for chain, send in zip(chains, together([chain.send for chain in chains])):
            chain.send = send
            chain.came = chain.links.swap(send, chain.stage)


def arrive(chains, *after):
    chains = [chain for chain in chains if chain.stage is not None]
    if chains:
        came = together([chain.came for chain in chains] + list(after))
        for chain, value in zip(chains, came):
            chain.came = value
            chain.cut()


def shards(
    tokens, earlier, coeffs, present, sample_at, w_qkv, w_out, w_up, w_down,
    gain_attn, gain_mlp, w_mean, w_var, cotangent, sizes, groups,
):
    links = Links(sizes)
    high = list(range(2, links.bits))
    count = 2 * links.chips
    tokens, earlier, coeffs, cotangent = tokens[0], earlier[0], coeffs[0], cotangent[0]
    length, width = tokens.shape
    basis_count = coeffs.shape[0]
    rows, side = w_qkv.shape[1], w_qkv.shape[2]
    ff_side = w_up.shape[1]
    local_heads, mem_part = w_mean.shape

    rest = jnp.concatenate([w_up, w_down.T], axis=1).astype(bf16)
    rest = lax.all_gather(rest, ("chips", "core", "heads"), axis=0, tiled=False)
    rest = rest.reshape(links.chips, 2, 2, rows, -1)
    tile = ff_side // 2
    small = jnp.concatenate(
        [gain_attn, gain_mlp, w_mean.reshape(-1), w_var.reshape(-1)]
    ).astype(bf16)
    small_size = small.shape[0]
    small = jnp.pad(small, (0, -small_size % LANES)).reshape(1, -1)
    small_h = links.swap(small, "h")
    first = jnp.where(links.side == 0, small, small_h)
    second = jnp.where(links.side == 0, small_h, small)
    far = high[1:][::-1]
    parts = jnp.concatenate([w_qkv, w_out.T[None]], axis=0).astype(bf16)
    parts = links.gather(parts, 1, far)
    small = links.gather(jnp.concatenate([first, second], axis=0), 0, far)
    small, parts = together([small, parts])
    turns = ([2, 1, "h"], [1, "h", 2], ["h", 2, 1], [2, 1, "h"])
    parts = [parts[c] for c in range(4)]
    have = list(far)
    haves = [list(far) for _ in range(4)]
    for step in range(3):
        small = links.gather(small, 0, [2 - step], have)
        have.append(2 - step)
        for c in range(4):
            parts[c] = links.gather(parts[c], 0, [turns[c][step]], haves[c])
            if turns[c][step] != "h":
                haves[c].append(turns[c][step])
        if step < 2:
            small, *parts = together([small] + parts)
    *qkv_full, out_full = [links.gather(parts[c], 0, [0], haves[c]).reshape(width, width) for c in range(4)]
    small = small.reshape(count, 2, -1).astype(f32)
    gain_a = small[:, 0, :rows].reshape(-1)
    gain_m = small[:, 0, rows : 2 * rows].reshape(-1)

    def head_map(start):
        part = small[:, :, start : start + local_heads * mem_part]
        part = part.reshape(count, 2, local_heads, mem_part).transpose(1, 2, 0, 3)
        return part.reshape(local_heads, 2, basis_count)

    mean_full = head_map(2 * rows)
    var_full = head_map(2 * rows + local_heads * mem_part)

    cot2 = links.swap(cotangent, 0)
    place = jnp.stack([links.bit(stage) for stage in links.places]).astype(jnp.int32)

    ridge = ridge_table(basis_count, 2 * length)
    tokens32, earlier32 = tokens.astype(f32), earlier.astype(f32)
    normed = layer_norm(tokens32, gain_a).astype(bf16)
    past = layer_norm(earlier32, gain_a).astype(bf16)
    old_basis = basis_at((sample_at[0].astype(f32) + 0.5) / GRID, basis_count).astype(bf16)
    here = present[0].astype(f32)
    samples = (here * dot(old_basis, coeffs.astype(bf16), 1, 0)).astype(bf16)
    memory = dot(ridge, jnp.concatenate([samples, past], axis=0), 1, 0).astype(bf16)
    sources = jnp.concatenate([past, normed, memory], axis=0)
    queries = dot(normed, qkv_full[0], 1, 0).astype(bf16)
    keys = dot(sources, qkv_full[1], 1, 0).astype(bf16)
    values = dot(sources, qkv_full[2], 1, 0).astype(bf16)
    old_basis, queries = together([old_basis, queries])
    context, lse, turned = attn_forward(queries, keys, values, mean_full, var_full, sources)
    gain_row = gain_m.reshape(1, -1)
    hidden, normed_mlp = mix(context, tokens, out_full, gain_row)
    normed_mlp2 = links.swap(normed_mlp, 0)
    lows = [2] + high[1:]
    order = block_order([1] + lows)
    mlp, mlp2, gn, gn2, down_send, down_keep, up_send, up_keep = feed(
        place, normed_mlp, normed_mlp2, cotangent, cot2, rest, tile, order
    )
    gn2 = links.swap(gn2, 0)
    mlp2 = links.swap(mlp2, 0)
    c_down = Chain(links, ["h", 1] + lows, down_send, down_keep)
    c_up = Chain(links, [1, 2] + high[1:] + ["h"], up_send, up_keep)
    start([c_down, c_up])
    grad_hidden, gain_m_grad, grad_ctx, branch = turn(hidden, gn, gn2, cotangent, out_full, gain_row)

    plans = (["h", 1, 2], [1, "h", 2])
    spans = [list(range(groups - 1)), [groups - 1]]
    feeds, c_qkv = [c_down, c_up], []
    into = ()
    for group in range(groups):
        late = group == groups - 1
        plan = plans[late] + high[1:]
        if late:
            into = into[:4]
        riders = c_qkv if late else feeds if group == 1 else []
        if group == 1:
            output = (tie(hidden, into[0]) + (mlp + mlp2.astype(f32))).astype(bf16)
            hold(riders, into[0], output)
        elif riders:
            hold(riders, into[0])
        into = attn_backward(
            place, queries, keys, values, mean_full, var_full, lse, grad_ctx, context, turned, branch, group, groups,
            block_order([b for b in plan if b != "h"]), rows, spans[late], into, riders,
        )
        if group == spans[late][-1]:
            c_qkv = c_qkv + [Chain(links, [0] + plan, into[4], into[5])]
        sends = [c.send for c in riders]
        if not late:
            start(riders)
            if c_qkv:
                c_qkv[0].send = tie(c_qkv[0].send, *sends)
                start(c_qkv)
                sends = [c_qkv[0].send]
        grad_ctx = tie(grad_ctx, into[0], *sends)
    arrive(feeds, into[0])
    chains = feeds + c_qkv
    last = chains[-1]
    last.send = tie(last.send, *[c.send for c in feeds])
    start([last])
    start(chains[:-1])
    arrive([last])
    start([last])
    dq, dk, dv, maps = into[:4]
    dq = tie(dq, *[c.send for c in chains])
    grad_tokens, grad_coeffs, tiny = finish(
        place, dq, dk, dv, qkv_full, ridge, old_basis, earlier, tokens, grad_hidden, gain_a.reshape(1, -1),
        gain_m_grad, maps, here.reshape(1), [],
    )

    def add(value, stage):
        return value + links.swap(value, stage)

    tiny_stages = [[lows[0]], [1]] + [[stage] for stage in lows[1:]]
    tiny = add(tiny, 0)
    hold(chains, tiny)
    other = links.swap(tiny, "h")
    add_up(place, c_qkv)
    other, *sends = together([other] + [c.send for c in c_qkv])
    for chain, value in zip(c_qkv, sends):
        chain.send = value
    tiny = tiny + other
    start(c_qkv)
    hold(feeds, *[c.send for c in c_qkv])
    for chain in feeds:
        chain.cut()
    start(feeds)
    begun = True
    joined = False

    def pick(tiny):
        heads = 2 * local_heads
        item = 2 * links.chip + links.core
        pick_map = lambda first: lax.dynamic_slice(
            tiny, (first + local_heads * links.side, item * mem_part), (local_heads, mem_part)
        )
        mean_out, var_out = pick_map(0), pick_map(heads)
        gains = tiny[2 * heads : 2 * heads + 2 * (width // basis_count)].reshape(-1, 2, basis_count)
        gain_part = width // (2 * count)
        pick_gain = lambda at: lax.dynamic_slice(
            gains[:, at].reshape(-1), ((2 * item + links.side) * gain_part,), (gain_part,)
        )
        gain_a_out, gain_m_out = pick_gain(0), pick_gain(1)
        return gain_a_out, gain_m_out, mean_out, var_out

    while tiny_stages or any(chain.stage is not None for chain in chains):
        going = [c for c in chains if c.stage is not None]
        if not begun:
            start(going)
        begun = False
        for stage in tiny_stages.pop(0) if tiny_stages else []:
            tiny = add(tiny, stage)
        if tiny_stages or len(going) > 1:
            *came, tiny = together([c.came for c in going] + [tiny])
            for chain, value in zip(going, came):
                chain.came = value
        on = [c for c in going if c.stages]
        ends = [c for c in going if not c.stages]
        for chain in on:
            chain.cut()
        if not joined:
            joined = True
            c_qkv[0].join(c_qkv[1])
            chains.remove(c_qkv[1])
            on = [c for c in on if c is not c_qkv[1]]
        if on and ends:
            hold(ends, *[c.send for c in on])
        elif ends and not tiny_stages:
            small_out = pick(tiny)
            hold(ends, *small_out)
        for chain in ends:
            chain.cut()
    r_down, r_up = links.whole_rows(c_down.value, rows), links.whole_rows(c_up.value, rows)
    r_proj = c_qkv[0].value
    return (
        output[None],
        grad_tokens[None],
        grad_coeffs[None],
        r_proj[:3],
        r_proj[3].T,
        r_up,
        r_down.T,
        *small_out,
    )


def solution(mesh):
    sizes = dict(mesh.shape)
    both = ("items", "heads")
    in_specs = (
        P(both, None, None),
        P(both, None, None),
        P(both, None, None),
        P(both),
        P(both, None),
        P(None, "items", "heads"),
        P("heads", "items"),
        P("items", "heads"),
        P("heads", "items"),
        P("items"),
        P("items"),
        P("heads", "items"),
        P("heads", "items"),
        P(both, None, None),
    )
    out_specs = (
        P(both, None, None),
        P(both, None, None),
        P(both, None, None),
        P(None, "items", "heads"),
        P("heads", "items"),
        P("items", "heads"),
        P("heads", "items"),
        P(both),
        P(both),
        P("heads", "items"),
        P("heads", "items"),
    )

    chips = sizes["items"] // 2
    split = Mesh(mesh.devices.reshape(chips, 2, sizes["heads"]), ("chips", "core", "heads"))

    def respec(spec):
        def axis(entry):
            names = entry if isinstance(entry, tuple) else (entry,)
            flat = tuple(n for name in names for n in (("chips", "core") if name == "items" else (name,)))
            return flat if flat != (None,) else None

        return P(*(axis(entry) for entry in spec))

    def body(*args):
        return shards(*args, sizes=dict(split.shape), groups=3)

    return jax.shard_map(
        body,
        mesh=split,
        in_specs=tuple(respec(spec) for spec in in_specs),
        out_specs=tuple(respec(spec) for spec in out_specs),
        check_vma=False,
    )
```
